32 devices in a mesh: dp: 8 (over z, y), context: 2 (over core), tensor: 2 (over x).
Axes of the slice: x: 2, y: 2, z: 4, core: 2. Of those that a mesh axis runs over, the one named last changes fastest.
Arguments:
- latents: bfloat16 [16, 1024, 1408], P('dp', ('context', 'tensor')), may hold values from -6 to 6
- skip_states: bfloat16 [16, 1024, 1408], P('dp', ('context', 'tensor')), may hold values from -6 to 6
- text_states: bfloat16 [16, 333, 1024], P('dp'), may hold values from -6 to 6
- time_vector: float32 [16, 1408], P('dp'), may hold values from -6 to 6
- grid_pos: int32 [16, 1024, 2], P('dp', 'context'), may hold values from 0 to 31
- out_grad: float32 [16, 1024, 1408], P('dp', ('context', 'tensor')), may hold values from -6 to 6
- norm0_gain: float32 [2, 1408], replicated, may hold values from 0.25 to 1.75
- norm0_beta: float32 [2, 1408], replicated, may hold values from -3 to 3
- skip_weight: bfloat16 [2, 1408, 1408], P(None, ('dp', 'context'), 'tensor'), may hold values from -0.109375 to 0.109375
- skip_bias: float32 [1408], replicated, may hold values from -3 to 3
- mod_weight: bfloat16 [1408, 1408], P(('dp', 'context')), may hold values from -0.15625 to 0.15625
- mod_bias: float32 [1408], replicated, may hold values from -3 to 3
- norm1_gain: float32 [1408], replicated, may hold values from 0.25 to 1.75
- norm1_beta: float32 [1408], replicated, may hold values from -3 to 3
- qkv_weight: bfloat16 [1408, 3, 1408], P(('dp', 'context'), None, 'tensor'), may hold values from -0.15625 to 0.15625
- qkv_bias: float32 [3, 1408], P(None, 'tensor'), may hold values from -3 to 3
- qnorm_gain: float32 [88], replicated, may hold values from 0.25 to 1.75
- qnorm_beta: float32 [88], replicated, may hold values from -3 to 3
- knorm_gain: float32 [88], replicated, may hold values from 0.25 to 1.75
- knorm_beta: float32 [88], replicated, may hold values from -3 to 3
- proj_weight: bfloat16 [1408, 1408], P('tensor', ('dp', 'context')), may hold values from -2.5 to 2.5
- proj_bias: float32 [1408], replicated, may hold values from -3 to 3
- norm3_gain: float32 [1408], replicated, may hold values from 0.25 to 1.75
- norm3_beta: float32 [1408], replicated, may hold values from -3 to 3
- cross_q_weight: bfloat16 [1408, 1408], P(('dp', 'context'), 'tensor'), may hold values from -0.15625 to 0.15625
- cross_q_bias: float32 [1408], P('tensor'), may hold values from -3 to 3
- cross_kv_weight: bfloat16 [1024, 2, 1408], P(('dp', 'context'), None, 'tensor'), may hold values from -0.1875 to 0.1875
- cross_kv_bias: float32 [2, 1408], P(None, 'tensor'), may hold values from -3 to 3
- cqnorm_gain: float32 [88], replicated, may hold values from 0.25 to 1.75
- cqnorm_beta: float32 [88], replicated, may hold values from -3 to 3
- cknorm_gain: float32 [88], replicated, may hold values from 0.25 to 1.75
- cross_proj_weight: bfloat16 [1408, 1408], P('tensor', ('dp', 'context')), may hold values from -1.5 to 1.5
- cross_proj_bias: float32 [1408], replicated, may hold values from -3 to 3
- norm2_gain: float32 [1408], replicated, may hold values from 0.25 to 1.75
- norm2_beta: float32 [1408], replicated, may hold values from -3 to 3
- fc1_weight: bfloat16 [1408, 6144], P(('dp', 'context'), 'tensor'), may hold values from -0.15625 to 0.15625
- fc1_bias: float32 [6144], P('tensor'), may hold values from -3 to 3
- fc2_weight: bfloat16 [6144, 1408], P('tensor', ('dp', 'context')), may hold values from -0.078125 to 0.078125
- fc2_bias: float32 [1408], replicated, may hold values from -3 to 3
Outputs:
- output: bfloat16 [16, 1024, 1408], P('dp', ('context', 'tensor'))
- grad_latents: float32 [16, 1024, 1408], P('dp', ('context', 'tensor'))
- grad_skip: float32 [16, 1024, 1408], P('dp', ('context', 'tensor'))
- grad_text: float32 [16, 333, 1024], P('dp')
- grad_norm0_gain: float32 [2, 1408], replicated
- grad_norm0_beta: float32 [2, 1408], replicated
- grad_skip_weight: float32 [2, 1408, 1408], P(None, ('dp', 'context'), 'tensor')
- grad_skip_bias: float32 [1408], replicated
- grad_mod_weight: float32 [1408, 1408], P(('dp', 'context'))
- grad_mod_bias: float32 [1408], replicated
- grad_norm1_gain: float32 [1408], replicated
- grad_norm1_beta: float32 [1408], replicated
- grad_qkv_weight: float32 [1408, 3, 1408], P(('dp', 'context'), None, 'tensor')
- grad_qkv_bias: float32 [3, 1408], P(None, 'tensor')
- grad_qnorm_gain: float32 [88], replicated
- grad_qnorm_beta: float32 [88], replicated
- grad_knorm_gain: float32 [88], replicated
- grad_knorm_beta: float32 [88], replicated
- grad_proj_weight: float32 [1408, 1408], P('tensor', ('dp', 'context'))
- grad_proj_bias: float32 [1408], replicated
- grad_norm3_gain: float32 [1408], replicated
- grad_norm3_beta: float32 [1408], replicated
- grad_cross_q_weight: float32 [1408, 1408], P(('dp', 'context'), 'tensor')
- grad_cross_q_bias: float32 [1408], P('tensor')
- grad_cross_kv_weight: float32 [1024, 2, 1408], P(('dp', 'context'), None, 'tensor')
- grad_cross_kv_bias: float32 [2, 1408], P(None, 'tensor')
- grad_cqnorm_gain: float32 [88], replicated
- grad_cqnorm_beta: float32 [88], replicated
- grad_cknorm_gain: float32 [88], replicated
- grad_cross_proj_weight: float32 [1408, 1408], P('tensor', ('dp', 'context'))
- grad_cross_proj_bias: float32 [1408], replicated
- grad_norm2_gain: float32 [1408], replicated
- grad_norm2_beta: float32 [1408], replicated
- grad_fc1_weight: float32 [1408, 6144], P(('dp', 'context'), 'tensor')
- grad_fc1_bias: float32 [6144], P('tensor')
- grad_fc2_weight: float32 [6144, 1408], P('tensor', ('dp', 'context'))
- grad_fc2_bias: float32 [1408], replicated
The draws below stay inside these ranges and needn't reach their ends.
Inputs may be any that keep to these rules, and one draw needn't show every extreme that they name: `grid_pos`: row and column of each token on the image's patch grid.
All inputs are finite; a program needn't handle non-finite values.
Results may differ from the reference program's by a relative error of at most 0.028.
Values may be sent and summed in bfloat16 or wider, within the bound.
No kernel may reach another device: no remote copies, remote signals or barrier semaphores. Data moves between devices by JAX's collectives and lax.ppermute only.
A program may use at most 320 MiB of HBM per device.

```python
import jax
import jax.numpy as jnp
from jax import lax

D = 1408
H = 16
HD = 88
FF = 6144
DT = 1024
L = 333
SEQ = 1024
GRID = 32
IMAGES = 16


def set_ends(drawn, rng, smallest, high):
    longest = drawn.shape.index(max(drawn.shape))
    spots = []
    for shift in (0, 1):
        where = [jax.random.randint(jax.random.fold_in(rng, axis), (), 0, length) for axis, length in enumerate(drawn.shape)]
        where[longest] = (where[longest] + shift) % drawn.shape[longest]
        spots.append(tuple(where))
    return drawn.at[spots[0]].set(smallest).at[spots[1]].set(high)


def steps_of(rng, dims, cuts, smallest, high):
    def one(position, parts):
        steps = jax.random.uniform(jax.random.fold_in(jax.random.fold_in(rng, 6), position), (parts,), jnp.float32, smallest / len(cuts), high / len(cuts))
        return jnp.repeat(jnp.exp(steps), dims[position] // parts).reshape((-1,) + (1,) * (len(dims) - position - 1))

    gain = one(*cuts[0])
    for cut in cuts[1:]:
        gain = gain * one(*cut)
    return gain


def bell_draw(rng, extent, width, limit, split=(), kind=jnp.bfloat16):
    values = width * jax.random.normal(rng, extent, jnp.float32)
    if split:
        values = values * steps_of(rng, extent, split, -0.22, 0.18)
    return jnp.clip(values, -limit, limit).astype(kind)


def setup_inputs(seed: int = 0) -> dict:
    key_list = jax.random.split(jax.random.key(seed), 40)
    return {
        "latents": bell_draw(key_list[0], (IMAGES, SEQ, D), 1.0, 6.0, ((0, 8), (1, 4))),
        "skip_states": bell_draw(key_list[1], (IMAGES, SEQ, D), 1.0, 6.0, ((0, 8), (1, 4))),
        "text_states": bell_draw(key_list[2], (IMAGES, L, DT), 1.0, 6.0, ((0, 8),)),
        "time_vector": bell_draw(key_list[3], (IMAGES, D), 1.0, 6.0, ((0, 8),), jnp.float32),
        "grid_pos": set_ends(jax.random.randint(key_list[4], (IMAGES, SEQ, 2), 0, GRID), jax.random.fold_in(key_list[4], 1), 0, GRID - 1).astype(jnp.int32),
        "out_grad": bell_draw(key_list[5], (IMAGES, SEQ, D), 1.0, 6.0, ((0, 8), (1, 4)), jnp.float32),
        "norm0_gain": jnp.clip(1.0 + 0.15 * jax.random.normal(key_list[6], (2, D), jnp.float32), 0.25, 1.75),
        "norm0_beta": bell_draw(key_list[7], (2, D), 0.5, 3.0, (), jnp.float32),
        "skip_weight": bell_draw(key_list[8], (2, D, D), (2 * D) ** -0.5, 0.109375, ((1, 16), (2, 2))),
        "skip_bias": bell_draw(key_list[9], (D,), 0.5, 3.0, (), jnp.float32),
        "mod_weight": bell_draw(key_list[10], (D, D), D ** -0.5, 0.15625, ((0, 16),)),
        "mod_bias": bell_draw(key_list[11], (D,), 0.5, 3.0, (), jnp.float32),
        "norm1_gain": jnp.clip(1.0 + 0.15 * jax.random.normal(key_list[12], (D,), jnp.float32), 0.25, 1.75),
        "norm1_beta": bell_draw(key_list[13], (D,), 0.5, 3.0, (), jnp.float32),
        "qkv_weight": bell_draw(key_list[14], (D, 3, D), D ** -0.5, 0.15625, ((0, 16), (2, 2))),
        "qkv_bias": bell_draw(key_list[15], (3, D), 0.5, 3.0, ((1, 2),), jnp.float32),
        "qnorm_gain": jnp.clip(1.0 + 0.15 * jax.random.normal(key_list[16], (HD,), jnp.float32), 0.25, 1.75),
        "qnorm_beta": bell_draw(key_list[17], (HD,), 0.5, 3.0, (), jnp.float32),
        "knorm_gain": jnp.clip(1.0 + 0.15 * jax.random.normal(key_list[18], (HD,), jnp.float32), 0.25, 1.75),
        "knorm_beta": bell_draw(key_list[19], (HD,), 0.5, 3.0, (), jnp.float32),
        "proj_weight": bell_draw(key_list[20], (D, D), (max(1, 4 * D // SEQ)) ** -0.5, 2.5, ((0, 2), (1, 16))),
        "proj_bias": bell_draw(key_list[21], (D,), 0.5, 3.0, (), jnp.float32),
        "norm3_gain": jnp.clip(1.0 + 0.15 * jax.random.normal(key_list[22], (D,), jnp.float32), 0.25, 1.75),
        "norm3_beta": bell_draw(key_list[23], (D,), 0.5, 3.0, (), jnp.float32),
        "cross_q_weight": bell_draw(key_list[24], (D, D), D ** -0.5, 0.15625, ((0, 16), (1, 2))),
        "cross_q_bias": bell_draw(key_list[25], (D,), 0.5, 3.0, ((0, 2),), jnp.float32),
        "cross_kv_weight": bell_draw(key_list[26], (DT, 2, D), DT ** -0.5, 0.1875, ((0, 16), (2, 2))),
        "cross_kv_bias": bell_draw(key_list[27], (2, D), 0.5, 3.0, ((1, 2),), jnp.float32),
        "cqnorm_gain": jnp.clip(1.0 + 0.15 * jax.random.normal(key_list[28], (HD,), jnp.float32), 0.25, 1.75),
        "cqnorm_beta": bell_draw(key_list[29], (HD,), 0.5, 3.0, (), jnp.float32),
        "cknorm_gain": jnp.clip(1.0 + 0.15 * jax.random.normal(key_list[30], (HD,), jnp.float32), 0.25, 1.75),
        "cross_proj_weight": bell_draw(key_list[31], (D, D), (max(1, 4 * D // L)) ** -0.5, 1.5, ((0, 2), (1, 16))),
        "cross_proj_bias": bell_draw(key_list[32], (D,), 0.5, 3.0, (), jnp.float32),
        "norm2_gain": jnp.clip(1.0 + 0.15 * jax.random.normal(key_list[33], (D,), jnp.float32), 0.25, 1.75),
        "norm2_beta": bell_draw(key_list[34], (D,), 0.5, 3.0, (), jnp.float32),
        "fc1_weight": bell_draw(key_list[35], (D, FF), D ** -0.5, 0.15625, ((0, 16), (1, 2))),
        "fc1_bias": bell_draw(key_list[36], (FF,), 0.5, 3.0, ((0, 2),), jnp.float32),
        "fc2_weight": bell_draw(key_list[37], (FF, D), FF ** -0.5, 0.078125, ((0, 2), (1, 16))),
        "fc2_bias": bell_draw(key_list[38], (D,), 0.5, 3.0, (), jnp.float32),
    }


@jax.custom_vjp
def low(v):
    return lax.optimization_barrier(v.astype(jnp.bfloat16)).astype(jnp.float32)

@jax.custom_vjp
def low_back(v):
    return v

def low_keep(v):
    return (low(v), None)

def low_pass(kept, grad):
    return (grad,)

def back_keep(v):
    return (v, None)

def back_low(kept, grad):
    return (low(grad),)
low.defvjp(low_keep, low_pass)
low_back.defvjp(back_keep, back_low)
EPS = 1e-06

def layer_norm(values, norm_gain, norm_beta):
    centered = values - lax.optimization_barrier(jnp.mean(values, axis=-1, keepdims=True))
    variance = lax.optimization_barrier(jnp.mean(centered * centered, axis=-1, keepdims=True))
    return centered * lax.rsqrt(variance + EPS) * norm_gain + norm_beta

def matmul(left_mat, right_mat):
    return jnp.dot(left_mat, right_mat, precision=lax.Precision.HIGHEST, preferred_element_type=jnp.float32)

def rope_angles(positions):
    quarter = HD // 4
    frequency = 10000.0 ** (-2.0 * jnp.arange(quarter, dtype=jnp.float32) / (HD // 2))
    places = positions.astype(jnp.float32)
    return jnp.concatenate([places[..., 0:1] * frequency, places[..., 1:2] * frequency], axis=-1)

def rotate(values, angles):
    full_shape = values.shape
    paired = values.reshape(full_shape[:-1] + (HD // 2, 2))
    cos_part = jnp.cos(angles)[..., None, :]
    sin_part = jnp.sin(angles)[..., None, :]
    former = paired[..., 0]
    latter = paired[..., 1]
    turned = jnp.stack([former * cos_part - latter * sin_part, former * sin_part + latter * cos_part], axis=-1)
    return turned.reshape(full_shape)

def attend_block(query_block, keys, values_in):
    scores = jnp.einsum('qhd,khd->hqk', query_block, keys, precision=lax.Precision.HIGHEST, preferred_element_type=jnp.float32)
    scores = low_back(scores * HD ** (-0.5))
    weights_low = low(jax.nn.softmax(scores, axis=-1))
    return jnp.einsum('hqk,khd->qhd', weights_low, values_in, precision=lax.Precision.HIGHEST, preferred_element_type=jnp.float32)

def attention(queries, keys, values_in):
    row_count = queries.shape[0]
    block_rows = min(512, row_count)
    num_blocks = row_count // block_rows
    blocked = queries.reshape((num_blocks, block_rows) + queries.shape[1:])
    outputs = lax.map(jax.checkpoint(lambda query_block: attend_block(query_block, keys, values_in)), blocked)
    return outputs.reshape(queries.shape)

def block_forward(params, latent, skip_in, text_in, time_in, angles):
    norm0_gain, norm0_beta, skip_weight, skip_bias, mod_weight, mod_bias, norm1_gain, norm1_beta, qkv_weight, qkv_bias, qnorm_gain, qnorm_beta, knorm_gain, knorm_beta, proj_weight, proj_bias, norm3_gain, norm3_beta, cross_q_weight, cross_q_bias, cross_kv_weight, cross_kv_bias, cqnorm_gain, cqnorm_beta, cknorm_gain, cross_proj_weight, cross_proj_bias, norm2_gain, norm2_beta, fc1_weight, fc1_bias, fc2_weight, fc2_bias = params
    joined = jnp.concatenate([latent, skip_in], axis=-1)
    act_zero = low(layer_norm(joined, norm0_gain.reshape(-1), norm0_beta.reshape(-1)))
    hidden1 = low_back(matmul(act_zero, skip_weight.reshape(2 * D, D)) + skip_bias)
    shift = matmul(low(jax.nn.silu(time_in))[None, :], mod_weight)[0] + mod_bias
    act_one = low(layer_norm(hidden1, norm1_gain, norm1_beta) + shift)
    merged = low_back(matmul(act_one, qkv_weight.reshape(D, 3 * D)) + qkv_bias.reshape(-1)).reshape(SEQ, 3, H, HD)
    queries = low(rotate(layer_norm(merged[:, 0], qnorm_gain, qnorm_beta), angles))
    keys = low(rotate(layer_norm(merged[:, 1], knorm_gain, knorm_beta), angles))
    values_in = low(merged[:, 2])
    self_out = low(low_back(attention(queries, keys, values_in))).reshape(SEQ, D)
    hidden2 = hidden1 + low_back(matmul(self_out, proj_weight) + proj_bias)
    act_three = low(layer_norm(hidden2, norm3_gain, norm3_beta))
    cross_raw = low_back(matmul(act_three, cross_q_weight) + cross_q_bias).reshape(SEQ, H, HD)
    cross_queries = low(rotate(layer_norm(cross_raw, cqnorm_gain, cqnorm_beta), angles))
    text_kv = low_back(matmul(text_in, cross_kv_weight.reshape(DT, 2 * D)) + cross_kv_bias.reshape(-1)).reshape(L, 2, H, HD)
    cross_keys = low(layer_norm(text_kv[:, 0], cknorm_gain, jnp.float32(0.0)))
    cross_values = low(text_kv[:, 1])
    cross_out = low(low_back(attention(cross_queries, cross_keys, cross_values))).reshape(SEQ, D)
    hidden3 = hidden2 + low_back(matmul(cross_out, cross_proj_weight) + cross_proj_bias)
    act_two = low(layer_norm(hidden3, norm2_gain, norm2_beta))
    pre_act = low_back(matmul(act_two, fc1_weight) + fc1_bias)
    post_act = low(jax.nn.gelu(pre_act, approximate=True))
    return hidden3 + low_back(matmul(post_act, fc2_weight) + fc2_bias)

def reference(latents, skip_states, text_states, time_vector, grid_pos, out_grad, norm0_gain, norm0_beta, skip_weight, skip_bias, mod_weight, mod_bias, norm1_gain, norm1_beta, qkv_weight, qkv_bias, qnorm_gain, qnorm_beta, knorm_gain, knorm_beta, proj_weight, proj_bias, norm3_gain, norm3_beta, cross_q_weight, cross_q_bias, cross_kv_weight, cross_kv_bias, cqnorm_gain, cqnorm_beta, cknorm_gain, cross_proj_weight, cross_proj_bias, norm2_gain, norm2_beta, fc1_weight, fc1_bias, fc2_weight, fc2_bias):
    params = tuple((param.astype(jnp.float32) for param in (norm0_gain, norm0_beta, skip_weight, skip_bias, mod_weight, mod_bias, norm1_gain, norm1_beta, qkv_weight, qkv_bias, qnorm_gain, qnorm_beta, knorm_gain, knorm_beta, proj_weight, proj_bias, norm3_gain, norm3_beta, cross_q_weight, cross_q_bias, cross_kv_weight, cross_kv_bias, cqnorm_gain, cqnorm_beta, cknorm_gain, cross_proj_weight, cross_proj_bias, norm2_gain, norm2_beta, fc1_weight, fc1_bias, fc2_weight, fc2_bias)))

    def one_image(totals, inputs):
        latent, skip_in, text_in, time_in, positions, cotangent = inputs
        angles = rope_angles(positions)

        def forward(param_list, latent_in, skip_part, text_part):
            return block_forward(param_list, latent_in, skip_part, text_part, time_in, angles)
        result, pullback = jax.vjp(forward, params, latent.astype(jnp.float32), skip_in.astype(jnp.float32), text_in.astype(jnp.float32))
        grad_params, grad_latent, grad_skip_in, grad_text_in = pullback(cotangent.astype(jnp.float32))
        totals = jax.tree.map(lambda running, addend: running + addend, totals, grad_params)
        return (totals, (result.astype(jnp.bfloat16), grad_latent, grad_skip_in, grad_text_in))
    zeros = jax.tree.map(jnp.zeros_like, params)
    totals, (output, grad_latents, grad_skip, grad_text) = lax.scan(one_image, zeros, (latents, skip_states, text_states, time_vector, grid_pos, out_grad))
    return (output, grad_latents, grad_skip, grad_text, totals[0], totals[1], totals[2], totals[3], totals[4], totals[5], totals[6], totals[7], totals[8], totals[9], totals[10], totals[11], totals[12], totals[13], totals[14], totals[15], totals[16], totals[17], totals[18], totals[19], totals[20], totals[21], totals[22], totals[23], totals[24], totals[25], totals[26], totals[27], totals[28], totals[29], totals[30], totals[31], totals[32])
```

```python
import functools

import jax
import jax.numpy as jnp
from jax import lax
from jax.experimental import pallas as pl
from jax.experimental.pallas import tpu as pltpu
from jax.sharding import Mesh
from jax.sharding import PartitionSpec as P

D = 1408
HD = 88
FF = 6144
DT = 1024


EPS = 1e-06
ROWS_CONTRACT = (((0,), (0,)), ((), ()))
COLS_CONTRACT = (((1,), (1,)), ((), ()))


def spread(values):
    return lax.all_gather(values, "tensor", axis=1, tiled=True)


def collect(values):
    return lax.psum_scatter(values, "tensor", scatter_dimension=1, tiled=True)


def weight_grad(activations, gradients):
    return lax.dot_general(
        activations, gradients, ROWS_CONTRACT, preferred_element_type=jnp.float32
    )


def input_grad(gradients, weight_mat):
    return lax.dot_general(gradients, weight_mat, COLS_CONTRACT, preferred_element_type=jnp.float32)


def norm_forward(values, norm_gain, norm_beta):
    centered = values - jnp.mean(values, axis=-1, keepdims=True)
    inv_std = lax.rsqrt(jnp.mean(centered * centered, axis=-1, keepdims=True) + EPS)
    normed = centered * inv_std
    return (normed * norm_gain + norm_beta, normed, inv_std)


def norm_backward(upstream, normed, inv_std, norm_gain):
    scaled = upstream * norm_gain
    inner_term = (
        scaled
        - jnp.mean(scaled, axis=-1, keepdims=True)
        - normed * jnp.mean(scaled * normed, axis=-1, keepdims=True)
    )
    lead_axes = tuple(range(upstream.ndim - 1))
    return (
        inv_std * inner_term,
        jnp.sum(upstream * normed, axis=lead_axes),
        jnp.sum(upstream, axis=lead_axes),
    )


def rope_angles(positions):
    quarter = HD // 4
    frequency = 10000.0 ** (-2.0 * jnp.arange(quarter, dtype=jnp.float32) / (HD // 2))
    places = positions.astype(jnp.float32)
    return jnp.concatenate([places[..., 0:1] * frequency, places[..., 1:2] * frequency], axis=-1)


def rotate(values, angles, direction):
    full_shape = values.shape
    paired = values.reshape(full_shape[:-1] + (HD // 2, 2))
    cos_part = jnp.cos(angles)[..., None, :]
    sin_part = jnp.sin(angles)[..., None, :] * direction
    former = paired[..., 0]
    latter = paired[..., 1]
    turned = jnp.stack(
        [former * cos_part - latter * sin_part, former * sin_part + latter * cos_part], axis=-1
    )
    return turned.reshape(full_shape)


def attend_forward(query_img, key_img, value_img):
    scores = jnp.einsum(
        "qhd,khd->hqk", query_img, key_img, preferred_element_type=jnp.float32
    ) * HD ** (-0.5)
    row_peak = jnp.max(scores, axis=-1, keepdims=True)
    exponent = jnp.exp(scores - row_peak)
    row_total = jnp.sum(exponent, axis=-1, keepdims=True)
    weights_low = (exponent / row_total).astype(jnp.bfloat16)
    result = jnp.einsum("hqk,khd->qhd", weights_low, value_img, preferred_element_type=jnp.float32)
    return (result, row_peak[..., 0] + jnp.log(row_total[..., 0]))


def attend_backward(query_img, key_img, value_img, logsum, grad_img):
    scores = jnp.einsum(
        "qhd,khd->hqk", query_img, key_img, preferred_element_type=jnp.float32
    ) * HD ** (-0.5)
    probs_full = jnp.exp(scores - logsum[..., None])
    grad_probs = jnp.einsum("qhd,khd->hqk", grad_img, value_img, preferred_element_type=jnp.float32)
    delta_row = jnp.sum(probs_full * grad_probs, axis=-1, keepdims=True)
    grad_scores = (probs_full * (grad_probs - delta_row)).astype(jnp.bfloat16)
    grad_query = jnp.einsum(
        "hqk,khd->qhd", grad_scores, key_img, preferred_element_type=jnp.float32
    ) * HD ** (-0.5)
    grad_key = jnp.einsum(
        "hqk,qhd->khd", grad_scores, query_img, preferred_element_type=jnp.float32
    ) * HD ** (-0.5)
    grad_value = jnp.einsum(
        "hqk,qhd->khd",
        probs_full.astype(jnp.bfloat16),
        grad_img,
        preferred_element_type=jnp.float32,
    )
    return (grad_query, grad_key, grad_value)


def bias_total(gradients):
    return jnp.sum(gradients.astype(jnp.float32).reshape(-1, gradients.shape[-1]), axis=0)


def on_device(
    latents,
    skip_states,
    text_states,
    time_vector,
    grid_pos,
    out_grad,
    norm0_gain,
    norm0_beta,
    skip_weight,
    skip_bias,
    mod_weight,
    mod_bias,
    norm1_gain,
    norm1_beta,
    qkv_weight,
    qkv_bias,
    qnorm_gain,
    qnorm_beta,
    knorm_gain,
    knorm_beta,
    proj_weight,
    proj_bias,
    norm3_gain,
    norm3_beta,
    cross_q_weight,
    cross_q_bias,
    cross_kv_weight,
    cross_kv_bias,
    cqnorm_gain,
    cqnorm_beta,
    cknorm_gain,
    cross_proj_weight,
    cross_proj_bias,
    norm2_gain,
    norm2_beta,
    fc1_weight,
    fc1_bias,
    fc2_weight,
    fc2_bias,
):
    context_count = lax.axis_size("context")
    tensor_rank = lax.axis_index("tensor")
    gathered = (
        lax.all_gather(skip_weight, ("dp", "context"), axis=1, tiled=True),
        lax.all_gather(mod_weight, ("dp", "context"), axis=0, tiled=True),
        lax.all_gather(qkv_weight, ("dp", "context"), axis=0, tiled=True),
        lax.all_gather(proj_weight, ("dp", "context"), axis=1, tiled=True),
        lax.all_gather(cross_q_weight, ("dp", "context"), axis=0, tiled=True),
        lax.all_gather(cross_kv_weight, ("dp", "context"), axis=0, tiled=True),
        lax.all_gather(cross_proj_weight, ("dp", "context"), axis=1, tiled=True),
        lax.all_gather(fc1_weight, ("dp", "context"), axis=0, tiled=True),
        lax.all_gather(fc2_weight, ("dp", "context"), axis=1, tiled=True),
    )
    (
        skip_full,
        mod_full,
        qkv_full,
        proj_full,
        crossq_full,
        crosskv_full,
        crossproj_full,
        fc1_full,
        fc2_full,
    ) = gathered
    local_width = qkv_full.shape[2]
    heads_local = local_width // HD
    images = latents.shape[0]
    group_rows = grid_pos.shape[1]
    text_rows = text_states.shape[1]
    flat_rows = images * group_rows
    angles = rope_angles(grid_pos)
    joined = jnp.concatenate(
        [latents.astype(jnp.float32), skip_states.astype(jnp.float32)], axis=-1
    )
    skip_normed, skip_unit, skip_inv = norm_forward(
        joined, norm0_gain.reshape(-1), norm0_beta.reshape(-1)
    )
    skip_act = spread(skip_normed.astype(jnp.bfloat16)).reshape(flat_rows, 2 * D)
    skip_cols = jnp.dot(
        skip_act, skip_full.reshape(2 * D, local_width), preferred_element_type=jnp.float32
    )
    hidden1 = (
        lax.all_to_all(
            skip_cols.reshape(images, group_rows, local_width),
            "tensor",
            split_axis=1,
            concat_axis=2,
            tiled=True,
        )
        + skip_bias
    )
    silu_low = jax.nn.silu(time_vector).astype(jnp.bfloat16)
    shift = jnp.dot(silu_low, mod_full, preferred_element_type=jnp.float32) + mod_bias
    norm1_out, unit_one, inv_one = norm_forward(hidden1, norm1_gain, norm1_beta)
    attn_act = spread((norm1_out + shift[:, None, :]).astype(jnp.bfloat16)).reshape(flat_rows, D)
    merged = jnp.dot(
        attn_act, qkv_full.reshape(D, 3 * local_width), preferred_element_type=jnp.float32
    ) + qkv_bias.reshape(-1)
    merged = merged.reshape(images, group_rows, 3, heads_local, HD)
    query_norm, query_unit, query_inv = norm_forward(merged[:, :, 0], qnorm_gain, qnorm_beta)
    key_norm, key_unit, key_inv = norm_forward(merged[:, :, 1], knorm_gain, knorm_beta)
    queries = rotate(query_norm, angles, 1.0).astype(jnp.bfloat16)
    keys_low = rotate(key_norm, angles, 1.0).astype(jnp.bfloat16)
    values_low = merged[:, :, 2].astype(jnp.bfloat16)
    keys_all, values_all = (
        lax.all_gather(
            keys_low.reshape(images, group_rows, local_width), "context", axis=1, tiled=True
        ),
        lax.all_gather(
            values_low.reshape(images, group_rows, local_width), "context", axis=1, tiled=True
        ),
    )
    keys_all = keys_all.reshape(images, -1, heads_local, HD)
    values_all = values_all.reshape(images, -1, heads_local, HD)
    attn_out, attn_lse = lax.map(
        lambda packed: attend_forward(*packed), (queries, keys_all, values_all)
    )
    attn_low = attn_out.reshape(flat_rows, local_width).astype(jnp.bfloat16)
    hidden2 = (
        hidden1
        + collect(
            jnp.dot(attn_low, proj_full, preferred_element_type=jnp.float32).reshape(
                images, group_rows, D
            )
        )
        + proj_bias
    )
    norm3_out, unit_three, inv_three = norm_forward(hidden2, norm3_gain, norm3_beta)
    cross_act = spread(norm3_out.astype(jnp.bfloat16)).reshape(flat_rows, D)
    cross_raw = (
        jnp.dot(cross_act, crossq_full, preferred_element_type=jnp.float32) + cross_q_bias
    ).reshape(images, group_rows, heads_local, HD)
    cquery_norm, cquery_unit, cquery_inv = norm_forward(cross_raw, cqnorm_gain, cqnorm_beta)
    cross_queries = rotate(cquery_norm, angles, 1.0).astype(jnp.bfloat16)
    text_low = text_states.reshape(images * text_rows, DT)
    text_kv = jnp.dot(
        text_low, crosskv_full.reshape(DT, 2 * local_width), preferred_element_type=jnp.float32
    ) + cross_kv_bias.reshape(-1)
    text_kv = text_kv.reshape(images, text_rows, 2, heads_local, HD)
    ckey_norm, ckey_unit, ckey_inv = norm_forward(text_kv[:, :, 0], cknorm_gain, 0.0)
    cross_keys = ckey_norm.astype(jnp.bfloat16)
    cross_values = text_kv[:, :, 1].astype(jnp.bfloat16)
    cross_out, cross_lse = lax.map(
        lambda packed: attend_forward(*packed), (cross_queries, cross_keys, cross_values)
    )
    cross_low = cross_out.reshape(flat_rows, local_width).astype(jnp.bfloat16)
    hidden3 = (
        hidden2
        + collect(
            jnp.dot(cross_low, crossproj_full, preferred_element_type=jnp.float32).reshape(
                images, group_rows, D
            )
        )
        + cross_proj_bias
    )
    norm2_out, unit_two, inv_two = norm_forward(hidden3, norm2_gain, norm2_beta)
    mlp_act = spread(norm2_out.astype(jnp.bfloat16)).reshape(flat_rows, D)
    pre_act = jnp.dot(mlp_act, fc1_full, preferred_element_type=jnp.float32) + fc1_bias
    post_low = jax.nn.gelu(pre_act, approximate=True).astype(jnp.bfloat16)
    output = (
        hidden3
        + collect(
            jnp.dot(post_low, fc2_full, preferred_element_type=jnp.float32).reshape(
                images, group_rows, D
            )
        )
        + fc2_bias
    )
    out_low = out_grad.astype(jnp.bfloat16)
    fc2_bias_grad = bias_total(out_low)
    out_all = spread(out_low).reshape(flat_rows, D)
    fc2_grad = weight_grad(post_low, out_all)
    post_grad = input_grad(out_all, fc2_full)
    gelu_pull = jax.vjp(lambda inputs: jax.nn.gelu(inputs, approximate=True), pre_act)[1]
    pre_low = gelu_pull(post_grad)[0].astype(jnp.bfloat16)
    fc1_grad = weight_grad(mlp_act, pre_low)
    fc1_bias_grad = bias_total(pre_low)
    mlp_up = collect(input_grad(pre_low, fc1_full).reshape(images, group_rows, D))
    norm2_in, norm2_gain_grad, norm2_beta_grad = norm_backward(
        mlp_up, unit_two, inv_two, norm2_gain
    )
    grad_three = out_grad + norm2_in
    cross_grad_low = grad_three.astype(jnp.bfloat16)
    cross_proj_bias_grad = bias_total(cross_grad_low)
    cross_grad_all = spread(cross_grad_low).reshape(flat_rows, D)
    cross_proj_grad = weight_grad(cross_low, cross_grad_all)
    cross_o_grad = (
        input_grad(cross_grad_all, crossproj_full)
        .astype(jnp.bfloat16)
        .reshape(images, group_rows, heads_local, HD)
    )
    cq_grad, ck_grad, cv_grad = lax.map(
        lambda packed: attend_backward(*packed),
        (cross_queries, cross_keys, cross_values, cross_lse, cross_o_grad),
    )
    ck_grad, cv_grad = (
        lax.psum(ck_grad.astype(jnp.bfloat16), "context").astype(jnp.float32),
        lax.psum(cv_grad.astype(jnp.bfloat16), "context").astype(jnp.float32),
    )
    share = 1.0 / context_count
    ck_in, cknorm_gain_grad, cknorm_unused = norm_backward(
        ck_grad, ckey_unit, ckey_inv, cknorm_gain
    )
    text_grad_low = (
        jnp.stack([ck_in, cv_grad], axis=2)
        .reshape(images * text_rows, 2 * local_width)
        .astype(jnp.bfloat16)
    )
    cross_kv_grad = weight_grad(text_low, text_grad_low).reshape(DT, 2, local_width) * share
    cross_kv_bias_grad = bias_total(text_grad_low).reshape(2, local_width) * share
    text_part = input_grad(text_grad_low, crosskv_full.reshape(DT, 2 * local_width)).reshape(
        images, text_rows, DT
    )
    cq_raw, cqnorm_gain_grad, cqnorm_beta_grad = norm_backward(
        rotate(cq_grad, angles, -1.0), cquery_unit, cquery_inv, cqnorm_gain
    )
    cq_low = cq_raw.reshape(flat_rows, local_width).astype(jnp.bfloat16)
    cross_q_grad = weight_grad(cross_act, cq_low)
    cross_q_bias_grad = bias_total(cq_low)
    norm3_up = collect(input_grad(cq_low, crossq_full).reshape(images, group_rows, D))
    norm3_in, norm3_gain_grad, norm3_beta_grad = norm_backward(
        norm3_up, unit_three, inv_three, norm3_gain
    )
    grad_two = grad_three + norm3_in
    attn_grad_low = grad_two.astype(jnp.bfloat16)
    proj_bias_grad = bias_total(attn_grad_low)
    attn_grad_all = spread(attn_grad_low).reshape(flat_rows, D)
    proj_grad = weight_grad(attn_low, attn_grad_all)
    attn_o_grad = (
        input_grad(attn_grad_all, proj_full)
        .astype(jnp.bfloat16)
        .reshape(images, group_rows, heads_local, HD)
    )
    q_grad, k_all_grad, v_all_grad = lax.map(
        lambda packed: attend_backward(*packed),
        (queries, keys_all, values_all, attn_lse, attn_o_grad),
    )
    k_grad, v_grad = (
        lax.psum_scatter(
            k_all_grad.reshape(images, -1, local_width).astype(jnp.bfloat16),
            "context",
            scatter_dimension=1,
            tiled=True,
        ).astype(jnp.float32),
        lax.psum_scatter(
            v_all_grad.reshape(images, -1, local_width).astype(jnp.bfloat16),
            "context",
            scatter_dimension=1,
            tiled=True,
        ).astype(jnp.float32),
    )
    q_raw, qnorm_gain_grad, qnorm_beta_grad = norm_backward(
        rotate(q_grad, angles, -1.0), query_unit, query_inv, qnorm_gain
    )
    k_raw, knorm_gain_grad, knorm_beta_grad = norm_backward(
        rotate(k_grad.reshape(images, group_rows, heads_local, HD), angles, -1.0),
        key_unit,
        key_inv,
        knorm_gain,
    )
    merged_low = jnp.stack(
        [q_raw, k_raw, v_grad.reshape(images, group_rows, heads_local, HD)], axis=2
    )
    merged_low = merged_low.reshape(flat_rows, 3 * local_width).astype(jnp.bfloat16)
    qkv_grad = weight_grad(attn_act, merged_low).reshape(D, 3, local_width)
    qkv_bias_grad = bias_total(merged_low).reshape(3, local_width)
    norm1_up = collect(
        input_grad(merged_low, qkv_full.reshape(D, 3 * local_width)).reshape(images, group_rows, D)
    )
    shift_part = jnp.sum(norm1_up, axis=1)
    mod_bias_grad = jnp.sum(shift_part, axis=0)
    text_grad, shift_grad = (
        lax.psum(text_part.astype(jnp.bfloat16), "tensor").astype(jnp.float32),
        lax.psum(shift_part.astype(jnp.bfloat16), "tensor").astype(jnp.float32),
    )
    mod_grad = lax.dot_general(
        silu_low.astype(jnp.float32),
        shift_grad,
        ROWS_CONTRACT,
        precision=lax.Precision.HIGHEST,
        preferred_element_type=jnp.float32,
    )
    norm1_in, norm1_gain_grad, norm1_beta_grad = norm_backward(
        norm1_up, unit_one, inv_one, norm1_gain
    )
    grad_one = grad_two + norm1_in
    skip_grad_low = grad_one.astype(jnp.bfloat16)
    skip_bias_grad = bias_total(skip_grad_low)
    skip_cols_grad = lax.all_to_all(
        skip_grad_low, "tensor", split_axis=2, concat_axis=1, tiled=True
    ).reshape(flat_rows, local_width)
    skip_grad = weight_grad(skip_act, skip_cols_grad).reshape(2, D, local_width)
    cat_up = collect(
        input_grad(skip_cols_grad, skip_full.reshape(2 * D, local_width)).reshape(
            images, group_rows, 2 * D
        )
    )
    cat_in, norm0_gain_grad, norm0_beta_grad = norm_backward(
        cat_up, skip_unit, skip_inv, norm0_gain.reshape(-1)
    )
    grad_latents = cat_in[..., :D]
    grad_skip = cat_in[..., D:]

    def widen(piece, total_width):
        blank = jnp.zeros(piece.shape[:-1] + (total_width,), jnp.float32)
        return lax.dynamic_update_slice_in_dim(
            blank, piece, tensor_rank * piece.shape[-1], piece.ndim - 1
        )

    summed = lax.psum(
        (
            norm0_gain_grad,
            norm0_beta_grad,
            skip_bias_grad,
            mod_bias_grad,
            norm1_gain_grad,
            norm1_beta_grad,
            widen(qkv_bias_grad, D),
            qnorm_gain_grad,
            qnorm_beta_grad,
            knorm_gain_grad,
            knorm_beta_grad,
            proj_bias_grad,
            norm3_gain_grad,
            norm3_beta_grad,
            widen(cross_q_bias_grad, D),
            widen(cross_kv_bias_grad, D),
            cqnorm_gain_grad,
            cqnorm_beta_grad,
            cknorm_gain_grad * share,
            cross_proj_bias_grad,
            norm2_gain_grad,
            norm2_beta_grad,
            widen(fc1_bias_grad, FF),
            fc2_bias_grad,
        ),
        ("dp", "context", "tensor"),
    )

    def narrow(whole, piece_width):
        return lax.dynamic_slice_in_dim(
            whole, tensor_rank * piece_width, piece_width, whole.ndim - 1
        )

    weight_sums = (
        lax.psum_scatter(
            skip_grad.astype(jnp.bfloat16), ("dp", "context"), scatter_dimension=1, tiled=True
        ).astype(jnp.float32),
        lax.psum_scatter(
            mod_grad.astype(jnp.bfloat16), ("dp", "context"), scatter_dimension=0, tiled=True
        ).astype(jnp.float32),
        lax.psum_scatter(
            qkv_grad.astype(jnp.bfloat16), ("dp", "context"), scatter_dimension=0, tiled=True
        ).astype(jnp.float32),
        lax.psum_scatter(
            proj_grad.astype(jnp.bfloat16), ("dp", "context"), scatter_dimension=1, tiled=True
        ).astype(jnp.float32),
        lax.psum_scatter(
            cross_q_grad.astype(jnp.bfloat16), ("dp", "context"), scatter_dimension=0, tiled=True
        ).astype(jnp.float32),
        lax.psum_scatter(
            cross_kv_grad.astype(jnp.bfloat16), ("dp", "context"), scatter_dimension=0, tiled=True
        ).astype(jnp.float32),
        lax.psum_scatter(
            cross_proj_grad.astype(jnp.bfloat16), ("dp", "context"), scatter_dimension=1, tiled=True
        ).astype(jnp.float32),
        lax.psum_scatter(
            fc1_grad.astype(jnp.bfloat16), ("dp", "context"), scatter_dimension=0, tiled=True
        ).astype(jnp.float32),
        lax.psum_scatter(
            fc2_grad.astype(jnp.bfloat16), ("dp", "context"), scatter_dimension=1, tiled=True
        ).astype(jnp.float32),
    )
    return (
        output.astype(jnp.bfloat16),
        grad_latents,
        grad_skip,
        text_grad,
        summed[0].reshape(2, D),
        summed[1].reshape(2, D),
        weight_sums[0],
        summed[2],
        weight_sums[1],
        summed[3],
        summed[4],
        summed[5],
        weight_sums[2],
        narrow(summed[6], local_width),
        summed[7],
        summed[8],
        summed[9],
        summed[10],
        weight_sums[3],
        summed[11],
        summed[12],
        summed[13],
        weight_sums[4],
        narrow(summed[14], local_width),
        weight_sums[5],
        narrow(summed[15], local_width),
        summed[16],
        summed[17],
        summed[18],
        weight_sums[6],
        summed[19],
        summed[20],
        summed[21],
        weight_sums[7],
        narrow(summed[22], fc1_bias.shape[0]),
        weight_sums[8],
        summed[23],
    )


F32 = jnp.float32
BF = jnp.bfloat16
VMEM_BYTES = 60 << 20
NN = (((1,), (0,)), ((), ()))
NT = (((1,), (1,)), ((), ()))
TN = (((0,), (0,)), ((), ()))
GRID_AXES = ("z", "y", "context", "tensor")
SWAP = [(0, 1), (1, 0)]
GELU_C = (2.0 / jnp.pi) ** 0.5


def dotf(a, b, dims):
    return lax.dot_general(a, b, dims, preferred_element_type=F32)


def kernel_params():
    return pltpu.CompilerParams(vmem_limit_bytes=VMEM_BYTES)


def over_x(v):
    return lax.ppermute(v, "tensor", SWAP)


def over_core(v):
    return lax.ppermute(v, "context", SWAP)


def over_y(v):
    return lax.ppermute(v, "y", SWAP)


def over_z(v, k):
    return lax.ppermute(v, "z", [(i, i ^ k) for i in range(4)])


class Link:
    def __init__(self, depth=2):
        self.depth = depth
        self.done = []

    def send(self, move, value):
        if len(self.done) >= self.depth:
            value, _ = lax.optimization_barrier((value, self.done[-self.depth]))
        out = move(value)
        self.done.append(out)
        return out


def assemble_body(ids, a, b, c, d, o):
    for k, ref in enumerate((a, b, c, d)):
        o[:, 0, (ids[1] ^ (k >> 1)) * 2 + (ids[2] ^ (k & 1))] = ref[0]


def assemble(ids, pieces):
    _, n, r, w = pieces[0].shape
    spec = pl.BlockSpec((1, n, r, w), lambda s, i: (s, 0, 0, 0))
    out = pl.pallas_call(
        assemble_body,
        out_shape=jax.ShapeDtypeStruct((n, 4, 4, r, w), pieces[0].dtype),
        grid_spec=pltpu.PrefetchScalarGridSpec(
            num_scalar_prefetch=1,
            grid=(4,),
            in_specs=[spec] * 4,
            out_specs=pl.BlockSpec((n, 1, 4, r, w), lambda s, i: (0, s ^ i[0], 0, 0, 0)),
        ),
        compiler_params=kernel_params(),
        name="assemble",
    )(ids, *pieces)
    return out.reshape(n, 16 * r, w)


def mm_nn_body(act, w, b, o):
    o[0] = (dotf(act[...], w[0], NN) + b[0]).astype(o.dtype)


def mm_nn(act, w, first, n, bias, dtype):
    t, k = act.shape
    width = w.shape[2]
    return pl.pallas_call(
        mm_nn_body,
        grid=(n,),
        in_specs=[
            pl.BlockSpec((t, k), lambda s: (0, 0)),
            pl.BlockSpec((1, k, width), lambda s: (first + s, 0, 0)),
            pl.BlockSpec((1, 1, width), lambda s: (s, 0, 0)),
        ],
        out_specs=pl.BlockSpec((1, t, width), lambda s: (s, 0, 0)),
        out_shape=jax.ShapeDtypeStruct((n, t, width), dtype),
        compiler_params=kernel_params(),
        name="mm_nn",
    )(act, w, bias)


def mm_nt_body(n, *refs):
    g_own, g_oth = refs[:n], refs[n : 2 * n]
    w_own, w_oth, o = refs[2 * n :]
    for s in range(n):

        @pl.when(pl.program_id(0) == s)
        def _(s=s):
            part = dotf(g_own[s][...], w_own[0], NT) + dotf(g_oth[s][...], w_oth[0], NT)
            if s:
                part = part + o[...]
            o[...] = part


def mm_nt(gs_own, gs_oth, w_own, w_oth, first):
    n = len(gs_own)
    t, width = gs_own[0].shape
    k = w_own.shape[1]
    g_spec = pl.BlockSpec((t, width), lambda s: (0, 0))
    w_spec = pl.BlockSpec((1, k, width), lambda s: (first + s, 0, 0))
    return pl.pallas_call(
        functools.partial(mm_nt_body, n),
        grid=(n,),
        in_specs=[g_spec] * (2 * n) + [w_spec] * 2,
        out_specs=pl.BlockSpec((t, k), lambda s: (0, 0)),
        out_shape=jax.ShapeDtypeStruct((t, k), F32),
        compiler_params=kernel_params(),
        name="mm_nt",
    )(*gs_own, *gs_oth, w_own, w_oth)


def ff_up_body(act, w, b, post, slope):
    v = dotf(act[...], w[0], NN) + b[...]
    inner = jnp.tanh(GELU_C * (v + 0.044715 * v * v * v))
    half = 0.5 * (1.0 + inner)
    post[...] = (v * half).astype(BF)
    slope[...] = (
        half + 0.5 * v * (1.0 - inner * inner) * (GELU_C * (1.0 + 0.134145 * v * v))
    ).astype(BF)


def ff_tile(width):
    return 768 if width % 768 == 0 else width


def ff_up(act, w, bias):
    t, k = act.shape
    width = w.shape[2]
    tile = ff_tile(width)
    col = pl.BlockSpec((t, tile), lambda j: (0, j))
    return pl.pallas_call(
        ff_up_body,
        grid=(width // tile,),
        in_specs=[
            pl.BlockSpec((t, k), lambda j: (0, 0)),
            pl.BlockSpec((1, k, tile), lambda j: (0, 0, j)),
            pl.BlockSpec((1, tile), lambda j: (0, j)),
        ],
        out_specs=[col, col],
        out_shape=[jax.ShapeDtypeStruct((t, width), BF)] * 2,
        compiler_params=kernel_params(),
        name="ff_up",
    )(act, w, bias)


def ff_up_grad_body(gm, w, slope, g, total):
    low = (dotf(gm[...], w[0], NN) * slope[...].astype(F32)).astype(BF)
    g[...] = low
    total[...] = jnp.sum(low.astype(F32), axis=0, keepdims=True)


def ff_up_grad(gm, w, slope):
    t, k = gm.shape
    width = w.shape[2]
    tile = ff_tile(width)
    col = pl.BlockSpec((t, tile), lambda j: (0, j))
    return pl.pallas_call(
        ff_up_grad_body,
        grid=(width // tile,),
        in_specs=[
            pl.BlockSpec((t, k), lambda j: (0, 0)),
            pl.BlockSpec((1, k, tile), lambda j: (0, 0, j)),
            col,
        ],
        out_specs=[col, pl.BlockSpec((1, tile), lambda j: (0, j))],
        out_shape=[
            jax.ShapeDtypeStruct((t, width), BF),
            jax.ShapeDtypeStruct((1, width), F32),
        ],
        compiler_params=kernel_params(),
        name="ff_up_grad",
    )(gm, w, slope)


def ff_down_body(h, w, o, acc):
    part = dotf(h[...], w[0], NT)
    step = pl.program_id(0)

    @pl.when(step == 0)
    def _():
        acc[...] = part

    @pl.when(step > 0)
    def _():
        acc[...] += part

    @pl.when(step == pl.num_programs(0) - 1)
    def _():
        o[...] = acc[...].astype(o.dtype)


def ff_down(h, w, dtype):
    t, width = h.shape
    k = w.shape[1]
    tile = ff_tile(width)
    return pl.pallas_call(
        ff_down_body,
        grid=(width // tile,),
        in_specs=[
            pl.BlockSpec((t, tile), lambda j: (0, j)),
            pl.BlockSpec((1, k, tile), lambda j: (0, 0, j)),
        ],
        out_specs=pl.BlockSpec((t, k), lambda j: (0, 0)),
        out_shape=jax.ShapeDtypeStruct((t, k), dtype),
        scratch_shapes=[pltpu.VMEM((t, k), F32)],
        compiler_params=kernel_params(),
        name="ff_down",
    )(h, w)


def wgrad_body(jobs, n_in, *refs):
    ins, outs = refs[:n_in], refs[n_in:]
    for pairs, places in jobs:
        acc = None
        for a, g in pairs:
            part = dotf(ins[a][...], ins[g][...], NN)
            acc = part if acc is None else acc + part
        rows = acc.shape[0] // len(places)
        for k, (out, slab) in enumerate(places):
            outs[out][slab] = acc[k * rows : (k + 1) * rows].astype(BF)


def wgrad(arrays, jobs, out_shapes):
    return pl.pallas_call(
        functools.partial(wgrad_body, jobs, len(arrays)),
        out_shape=[jax.ShapeDtypeStruct(s, BF) for s in out_shapes],
        compiler_params=kernel_params(),
        name="wgrad",
    )(*arrays)


def ff_wgrad_body(n, *refs):
    outs = refs[2 * n :]
    acc = None
    for a, g in zip(refs[:n], refs[n : 2 * n]):
        part = dotf(a[...], g[...], NN)
        acc = part if acc is None else acc + part
    rows = acc.shape[0] // 2
    outs[0][...] = acc[:rows].astype(BF)
    outs[1][...] = acc[rows:].astype(BF)


def ff_wgrad(ats, gs):
    n = len(ats)
    m, t = ats[0].shape
    width = gs[0].shape[1]
    tile = ff_tile(width)
    return pl.pallas_call(
        functools.partial(ff_wgrad_body, n),
        grid=(width // tile,),
        in_specs=[pl.BlockSpec((m, t), lambda j: (0, 0))] * n
        + [pl.BlockSpec((t, tile), lambda j: (0, j))] * n,
        out_specs=[pl.BlockSpec((m // 2, tile), lambda j: (0, j))] * 2,
        out_shape=[jax.ShapeDtypeStruct((m // 2, width), BF)] * 2,
        compiler_params=kernel_params(),
        name="ff_wgrad",
    )(*ats, *gs)


def head_sums(v, spread_in, spread_out):
    high = v.astype(BF)
    low = (v - high.astype(F32)).astype(BF)
    sums = dotf(high, spread_in, NN) + dotf(low, spread_in, NN)
    high = sums.astype(BF)
    low = (sums - high.astype(F32)).astype(BF)
    return dotf(high, spread_out, NN) + dotf(low, spread_out, NN)


def head_unit(v, spread_in, spread_out):
    centered = v - head_sums(v, spread_in, spread_out) * (1.0 / HD)
    var = head_sums(centered * centered, spread_in, spread_out) * (1.0 / HD)
    inv = lax.rsqrt(var + EPS)
    return centered * inv, inv


def swap_pairs(v):
    t, w = v.shape
    pad = -w % 128
    wide = jnp.concatenate([v, jnp.zeros((t, pad), F32)], axis=1) if pad else v
    even = lax.broadcasted_iota(jnp.int32, wide.shape, 1) % 2 == 0
    turned = jnp.where(
        even, pltpu.roll(wide, wide.shape[1] - 1, 1), pltpu.roll(wide, 1, 1)
    )
    return turned[:, :w]


def head_spreads(width):
    lanes = jnp.arange(width) // HD
    into = (lanes[:, None] == jnp.arange(128)[None, :]).astype(BF)
    return into, into.T


def norm_rope_body(kinds, *refs):
    n = len(kinds)
    ins = refs[:n]
    gain, beta, cos, sin, s_in, s_out = refs[n : n + 6]
    outs = refs[n + 6 :]
    for k, kind in enumerate(kinds):
        v = ins[k][0]
        if kind != "cast":
            unit, _ = head_unit(v, s_in[...], s_out[...])
            v = unit * gain[k : k + 1, :] + beta[k : k + 1, :]
            if kind == "rope":
                v = v * cos[...] + swap_pairs(v) * sin[...]
        outs[k][...] = v.astype(BF)


def slab_spec(rows, width, slab):
    return pl.BlockSpec((1, rows, width), lambda i: (slab, i, 0))


def norm_rope(raws, kinds, gains, betas, cos, sin, rows):
    n = len(raws)
    _, t, w = raws[0][0].shape
    row = pl.BlockSpec((rows, w), lambda i: (i, 0))
    whole = pl.BlockSpec((n, w), lambda i: (0, 0))
    s_in, s_out = head_spreads(w)
    return pl.pallas_call(
        functools.partial(norm_rope_body, kinds),
        grid=(t // rows,),
        in_specs=[slab_spec(rows, w, s) for _, s in raws]
        + [whole, whole, row, row]
        + [pl.BlockSpec(s_in.shape, lambda i: (0, 0)), pl.BlockSpec(s_out.shape, lambda i: (0, 0))],
        out_specs=[row] * n,
        out_shape=[jax.ShapeDtypeStruct((t, w), BF)] * n,
        compiler_params=kernel_params(),
        name="norm_rope",
    )(*[a for a, _ in raws], gains, betas, cos, sin, s_in, s_out)


def norm_rope_grad_body(kinds, plan, n_up, *refs):
    n = len(kinds)
    ins = refs[:n]
    ups = refs[n : n + n_up]
    gain, cos, sin, s_in, s_out = refs[n + n_up : n + n_up + 5]
    outs = refs[n + n_up + 5 : 2 * n + n_up + 5]
    sums = refs[2 * n + n_up + 5]

    @pl.when(pl.program_id(0) == 0)
    def _():
        sums[...] = jnp.zeros_like(sums)

    for k, kind in enumerate(kinds):
        up = ups[plan[k][0]][...].astype(F32)
        for extra in plan[k][1:]:
            up = up + ups[extra][...].astype(F32)
        if kind != "cast":
            if kind == "rope":
                up = up * cos[...] - swap_pairs(up) * sin[...]
            unit, inv = head_unit(ins[k][0], s_in[...], s_out[...])
            scaled = up * gain[k : k + 1, :]
            m1 = head_sums(scaled, s_in[...], s_out[...]) * (1.0 / HD)
            m2 = head_sums(scaled * unit, s_in[...], s_out[...]) * (1.0 / HD)
            sums[0, k : k + 1, :] += jnp.sum(up * unit, axis=0, keepdims=True)
            sums[1, k : k + 1, :] += jnp.sum(up, axis=0, keepdims=True)
            up = inv * (scaled - m1 - unit * m2)
        low = up.astype(BF)
        outs[k][...] = low
        sums[2, k : k + 1, :] += jnp.sum(low.astype(F32), axis=0, keepdims=True)


def norm_rope_grad(raws, kinds, plan, ups, gains, cos, sin, rows):
    n = len(raws)
    _, t, w = raws[0][0].shape
    row = pl.BlockSpec((rows, w), lambda i: (i, 0))
    s_in, s_out = head_spreads(w)
    res = pl.pallas_call(
        functools.partial(norm_rope_grad_body, kinds, plan, len(ups)),
        grid=(t // rows,),
        in_specs=[slab_spec(rows, w, s) for _, s in raws]
        + [row] * len(ups)
        + [pl.BlockSpec((n, w), lambda i: (0, 0)), row, row]
        + [pl.BlockSpec(s_in.shape, lambda i: (0, 0)), pl.BlockSpec(s_out.shape, lambda i: (0, 0))],
        out_specs=[row] * n + [pl.BlockSpec((3, n, w), lambda i: (0, 0, 0))],
        out_shape=[jax.ShapeDtypeStruct((t, w), BF)] * n + [jax.ShapeDtypeStruct((3, n, w), F32)],
        compiler_params=kernel_params(),
        name="norm_rope_grad",
    )(*[a for a, _ in raws], *ups, gains, cos, sin, s_in, s_out)
    return res[:n], res[n]


def att_forward_body(nb, *refs):
    q_ref = refs[0]
    ks, vs = refs[1 : 1 + nb], refs[1 + nb : 1 + 2 * nb]
    o_ref, lse_ref = refs[1 + 2 * nb :]
    scale = HD**-0.5
    for h in range(q_ref.shape[1] // HD):
        s = slice(h * HD, (h + 1) * HD)
        q = q_ref[:, s]
        scores = [dotf(k[:, s], q, NT) for k in ks]
        peak = functools.reduce(
            jnp.maximum, [jnp.max(x, axis=0, keepdims=True) for x in scores]
        )
        expo = [jnp.exp((x - peak) * scale) for x in scores]
        total = sum(jnp.sum(e, axis=0, keepdims=True) for e in expo)
        recip = 1.0 / total
        out = sum(dotf(v[:, s], (e * recip).astype(BF), TN) for v, e in zip(vs, expo))
        o_ref[:, s] = out.T.astype(BF)
        lse_ref[h : h + 1, :] = peak * scale + jnp.log(total)


def att_forward(q, ks, vs):
    t, w = q.shape
    return pl.pallas_call(
        functools.partial(att_forward_body, len(ks)),
        out_shape=[
            jax.ShapeDtypeStruct((t, w), BF),
            jax.ShapeDtypeStruct((w // HD, t), F32),
        ],
        compiler_params=kernel_params(),
        name="att_forward",
    )(q, *ks, *vs)


def att_backward_body(nb, *refs):
    q_ref, do_ref, lse_ref = refs[:3]
    ks, vs = refs[3 : 3 + nb], refs[3 + nb : 3 + 2 * nb]
    dq_ref = refs[3 + 2 * nb]
    dks, dvs = refs[4 + 2 * nb : 4 + 3 * nb], refs[4 + 3 * nb :]
    scale = HD**-0.5
    for h in range(q_ref.shape[1] // HD):
        s = slice(h * HD, (h + 1) * HD)
        q = q_ref[:, s]
        do = do_ref[:, s]
        lse = lse_ref[h : h + 1, :]
        probs = [jnp.exp(dotf(k[:, s], q, NT) * scale - lse) for k in ks]
        dps = [dotf(v[:, s], do, NT) for v in vs]
        delta = sum(jnp.sum(p * d, axis=0, keepdims=True) for p, d in zip(probs, dps))
        dq = None
        for i in range(nb):
            ds = (probs[i] * (dps[i] - delta)).astype(BF)
            part = dotf(ks[i][:, s], ds, TN)
            dq = part if dq is None else dq + part
            dks[i][:, s] = (dotf(ds, q, NN) * scale).astype(dks[i].dtype)
            dvs[i][:, s] = dotf(probs[i].astype(BF), do, NN).astype(dvs[i].dtype)
        dq_ref[:, s] = (dq * scale).T


def att_backward(q, do, lse, ks, vs, kinds):
    t, w = q.shape
    nb = len(ks)
    outs = [jax.ShapeDtypeStruct((t, w), F32)]
    outs += [jax.ShapeDtypeStruct(k.shape, kind) for k, kind in zip(ks, kinds)] * 2
    res = pl.pallas_call(
        functools.partial(att_backward_body, nb),
        out_shape=outs,
        compiler_params=kernel_params(),
        name="att_backward",
    )(q, do, lse, *ks, *vs)
    return res[0], res[1 : 1 + nb], res[1 + nb :]


def one_image_per_chip(
    latents,
    skip_states,
    text_states,
    time_vector,
    grid_pos,
    out_grad,
    norm0_gain,
    norm0_beta,
    skip_weight,
    skip_bias,
    mod_weight,
    mod_bias,
    norm1_gain,
    norm1_beta,
    qkv_weight,
    qkv_bias,
    qnorm_gain,
    qnorm_beta,
    knorm_gain,
    knorm_beta,
    proj_weight,
    proj_bias,
    norm3_gain,
    norm3_beta,
    cross_q_weight,
    cross_q_bias,
    cross_kv_weight,
    cross_kv_bias,
    cqnorm_gain,
    cqnorm_beta,
    cknorm_gain,
    cross_proj_weight,
    cross_proj_bias,
    norm2_gain,
    norm2_beta,
    fc1_weight,
    fc1_bias,
    fc2_weight,
    fc2_bias,
):
    z, y = lax.axis_index("z"), lax.axis_index("y")
    core, rank = lax.axis_index("context"), lax.axis_index("tensor")
    ids = jnp.stack([z, y, core]).astype(jnp.int32)
    part = latents.shape[1]
    heads_half = qkv_weight.shape[2] // HD
    width = qkv_weight.shape[2]
    x_link, y_link, z_link = Link(), Link(), Link()

    def mine(a, axis=0):
        return lax.dynamic_index_in_dim(a, rank, axis, keepdims=False)

    def other(a, axis=0):
        return lax.dynamic_index_in_dim(a, 1 - rank, axis, keepdims=False)

    def natural(own, oth):
        first = rank == 0
        return jnp.concatenate([jnp.where(first, own, oth), jnp.where(first, oth, own)], axis=-1)

    def halves(a):
        first = rank == 0
        half = a.shape[-1] // 2
        return (
            jnp.where(first, a[..., :half], a[..., half:]),
            jnp.where(first, a[..., half:], a[..., :half]),
        )

    def gather_z(piece):
        return jnp.stack([piece] + [z_link.send(lambda v, k=k: over_z(v, k), piece) for k in (1, 2, 3)])

    skip_piece = skip_weight
    qkv_piece = jnp.swapaxes(qkv_weight, 0, 1)
    mix_piece = jnp.stack([proj_weight.T, cross_q_weight, cross_proj_weight.T])
    text_piece = jnp.swapaxes(cross_kv_weight, 0, 1)
    fc1_piece = fc1_weight[None]
    fc2_piece = fc2_weight.T[None]

    states_in = x_link.send(over_x, jnp.stack([other(latents), other(skip_states)]))
    skip_z = gather_z(skip_piece)
    qkv_z = gather_z(qkv_piece)
    skip_y = y_link.send(over_y, skip_z)
    skip_x = x_link.send(over_x, skip_z)
    skip_xy = x_link.send(over_x, skip_y)
    mix_z = gather_z(mix_piece)
    qkv_x = x_link.send(over_x, qkv_z)
    qkv_y = y_link.send(over_y, qkv_z)
    qkv_xy = y_link.send(over_y, qkv_x)
    text_z = gather_z(text_piece)
    mix_x = x_link.send(over_x, mix_z)
    mix_y = y_link.send(over_y, mix_z)
    mix_xy = y_link.send(over_y, mix_x)
    fc1_z = gather_z(fc1_piece)
    text_y = y_link.send(over_y, text_z)
    text_x = x_link.send(over_x, text_z)
    text_xy = x_link.send(over_x, text_y)
    fc2_z = gather_z(fc2_piece)
    out_low = out_grad.astype(BF)
    out_in = x_link.send(over_x, out_low)
    fc1_y = y_link.send(over_y, fc1_z)
    fc2_y = y_link.send(over_y, fc2_z)

    def whole(base, by_y):
        return assemble(ids, [base, over_core(base), by_y, over_core(by_y)])

    skip_own, skip_oth = whole(skip_z, skip_y), whole(skip_x, skip_xy)
    qkv_own, qkv_oth = whole(qkv_z, qkv_y), whole(qkv_x, qkv_xy)
    mix_own, mix_oth = whole(mix_z, mix_y), whole(mix_x, mix_xy)
    text_own, text_oth = whole(text_z, text_y), whole(text_x, text_xy)
    fc1_full, fc2_full = whole(fc1_z, fc1_y), whole(fc2_z, fc2_y)

    pos_own = mine(grid_pos)
    pos = jnp.concatenate(
        [
            lax.dynamic_slice_in_dim(pos_own, rank * part, part, 0),
            lax.dynamic_slice_in_dim(pos_own, (1 - rank) * part, part, 0),
        ]
    )
    angles = rope_angles(pos)
    cos_row = jnp.repeat(jnp.cos(angles), 2, axis=-1)
    sin_half = jnp.sin(angles)
    sin_row = jnp.stack([-sin_half, sin_half], axis=-1).reshape(cos_row.shape)
    cos_tab = jnp.tile(cos_row, (1, heads_half))
    sin_tab = jnp.tile(sin_row, (1, heads_half))

    def per_head(*rows):
        return jnp.stack([jnp.tile(r, heads_half) for r in rows])

    def placement(rows):
        index = jnp.arange(8 * rows)
        block, inner = index // rows, index % rows
        zz, yy = z ^ (block % 4), y ^ (block // 4)
        cc = jnp.stack([core, 1 - core])[:, None]
        source = ((zz * 2 + yy) * 2 + cc) * rows + inner
        return (source[..., None] == jnp.arange(16 * rows)).astype(BF)

    places = placement(D // 16)
    text_places = placement(DT // 16)

    def by_feature(act):
        keep = dotf(places[0], act, NT).astype(BF)
        give = dotf(places[1], act, NT).astype(BF)
        return keep, over_core(give)

    time_all = lax.all_gather(time_vector, ("z", "y"), axis=0, tiled=True)
    silu_all = jax.nn.silu(time_all).astype(BF)
    mod_rows = mod_weight.shape[0]
    shard = (z * 2 + y) * 2 + core
    silu_rows = lax.dynamic_slice_in_dim(silu_all, shard * mod_rows, mod_rows, 1)
    shift_all = lax.psum(dotf(silu_rows, mod_weight, NN), ("z", "y", "context"))
    image = (z * 2 + y) * 2 + rank
    shift = lax.dynamic_slice_in_dim(shift_all, image, 1, 0) + mod_bias

    lat = jnp.concatenate([mine(latents), states_in[0]])
    skp = jnp.concatenate([mine(skip_states), states_in[1]])
    joined = jnp.concatenate([lat, skp], axis=-1).astype(F32)
    gain0 = norm0_gain.reshape(-1)
    out0, unit0, inv0 = norm_forward(joined, gain0, norm0_beta.reshape(-1))
    act0 = out0.astype(BF)
    none = jnp.zeros((1, 1, width), F32)
    hid_own = mm_nn(act0, skip_own.reshape(1, 2 * D, width), 0, 1, none, F32)[0]
    hid_oth = mm_nn(act0, skip_oth.reshape(1, 2 * D, width), 0, 1, none, F32)[0]
    hidden1 = natural(hid_own, hid_oth) + skip_bias

    out1, unit1, inv1 = norm_forward(hidden1, norm1_gain, norm1_beta)
    act1 = (out1 + shift).astype(BF)
    qkv_bias_oth = over_x(qkv_bias)
    raw_own = mm_nn(act1, qkv_own, 0, 3, qkv_bias[:, None], F32)
    raw_oth = mm_nn(act1, qkv_oth, 0, 3, qkv_bias_oth[:, None], F32)
    qk_gain = per_head(qnorm_gain, knorm_gain, qnorm_gain, qnorm_gain, knorm_gain, qnorm_gain)
    qk_beta = per_head(qnorm_beta, knorm_beta, qnorm_beta, qnorm_beta, knorm_beta, qnorm_beta)
    qkv_raws = [(raw_own, 0), (raw_own, 1), (raw_own, 2), (raw_oth, 0), (raw_oth, 1), (raw_oth, 2)]
    qkv_kinds = ("rope", "rope", "cast") * 2
    qkv_low = norm_rope(qkv_raws, qkv_kinds, qk_gain, qk_beta, cos_tab, sin_tab, 128)
    att, lse, keys, values = [], [], [], []
    for half in range(2):
        q, k, v = qkv_low[3 * half : 3 * half + 3]
        keys.append([k, over_core(k)])
        values.append([v, over_core(v)])
    for half in range(2):
        o, l = att_forward(qkv_low[3 * half], keys[half], values[half])
        att.append(o)
        lse.append(l)
    hidden2 = hidden1 + mm_nt([att[0]], [att[1]], mix_own, mix_oth, 0) + proj_bias

    out3, unit3, inv3 = norm_forward(hidden2, norm3_gain, norm3_beta)
    act3 = out3.astype(BF)
    small_oth = over_x(jnp.concatenate([cross_q_bias[None], cross_kv_bias]))
    craw_own = mm_nn(act3, mix_own, 1, 1, cross_q_bias[None, None], F32)
    craw_oth = mm_nn(act3, mix_oth, 1, 1, small_oth[:1, None], F32)
    craws = [(craw_own, 0), (craw_oth, 0)]
    cq_gain = per_head(cqnorm_gain, cqnorm_gain)
    cqs = norm_rope(
        craws, ("rope",) * 2, cq_gain, per_head(cqnorm_beta, cqnorm_beta), cos_tab, sin_tab, 128
    )
    text = mine(text_states)
    text_rows = text.shape[0]
    traw_own = mm_nn(text, text_own, 0, 2, cross_kv_bias[:, None], F32)
    traw_oth = mm_nn(text, text_oth, 0, 2, small_oth[1:, None], F32)
    traws = [(traw_own, 0), (traw_own, 1), (traw_oth, 0), (traw_oth, 1)]
    t_kinds = ("norm", "cast") * 2
    ck_gain = per_head(cknorm_gain, cknorm_gain, cknorm_gain, cknorm_gain)
    blank = jnp.zeros((text_rows, width), F32)
    text_low = norm_rope(
        traws, t_kinds, ck_gain, jnp.zeros_like(ck_gain), blank, blank, text_rows
    )
    catt, clse = [], []
    for half in range(2):
        o, l = att_forward(cqs[half], [text_low[2 * half]], [text_low[2 * half + 1]])
        catt.append(o)
        clse.append(l)
    hidden3 = hidden2 + mm_nt([catt[0]], [catt[1]], mix_own, mix_oth, 2) + cross_proj_bias

    out2, unit2, inv2 = norm_forward(hidden3, norm2_gain, norm2_beta)
    act2 = out2.astype(BF)
    act2_in = over_x(act2)
    post_own, slope_own = ff_up(act2, fc1_full, fc1_bias[None])
    post_oth, slope_oth = ff_up(act2_in, fc1_full, fc1_bias[None])
    down_oth = ff_down(post_oth, fc2_full, F32)
    down_own = ff_down(post_own, fc2_full, F32) + hidden3 + fc2_bias
    down_in = over_x(jnp.stack([down_own[part:], down_oth[:part]]).astype(BF))
    out_mine = (down_own[:part] + down_in[1].astype(F32)).astype(BF)
    out_other = (down_oth[part:] + down_in[0].astype(F32)).astype(BF)

    def by_image(own, oth):
        first = rank == 0
        return jnp.stack([jnp.where(first, own, oth), jnp.where(first, oth, own)])

    output = by_image(out_mine, out_other)

    gm_own = jnp.concatenate([mine(out_low), mine(out_in)])
    gm_oth = jnp.concatenate([other(out_in), other(out_low)])
    fc2_bias_grad = bias_total(gm_own)
    g_pre_oth, fc1_sum_oth = ff_up_grad(gm_oth, fc2_full, slope_oth)
    up_oth = ff_down(g_pre_oth, fc1_full, BF)
    up_in = over_x(up_oth)
    g_pre_own, fc1_sum_own = ff_up_grad(gm_own, fc2_full, slope_own)
    mlp_up = ff_down(g_pre_own, fc1_full, F32) + up_in.astype(F32)
    fc1_bias_grad = (fc1_sum_own + fc1_sum_oth)[0]

    def paired(a):
        return [a, over_core(a)]

    gm_rows = by_feature(gm_own) + by_feature(gm_oth)
    act2_rows = by_feature(act2) + by_feature(act2_in)
    fc2_near, fc2_far = ff_wgrad(gm_rows, paired(post_own) + paired(post_oth))
    fc1_near, fc1_far = ff_wgrad(act2_rows, paired(g_pre_own) + paired(g_pre_oth))

    def over_z_sum(blocks):
        total = blocks[:, 0]
        for k in (1, 2, 3):
            total = total + over_z(blocks[:, k].astype(BF), k).astype(F32)
        return total

    def reduce_y(near, far, rows):
        n, _, w = near.shape
        total = near.astype(F32) + over_y(far).astype(F32)
        return over_z_sum(total.reshape(n, 4, rows, w))

    def reduce_xy(own, oth, rows):
        n, m, w = own.shape
        total = own.astype(F32) + over_x(oth).astype(F32)
        near, far = total[:, : m // 2], total[:, m // 2 :]
        near = near + over_y(far.astype(BF)).astype(F32)
        return over_z_sum(near.reshape(n, 4, rows, w))

    def reduce_yx(near, far, rows):
        n2, m, w = near.shape
        total = near.astype(F32) + over_y(far).astype(F32)
        n = n2 // 2
        total = total[:n] + over_x(total[n:].astype(BF)).astype(F32)
        return over_z_sum(total.reshape(n, 4, rows, w))

    block = D // 16
    fc2_grad = reduce_y(fc2_near[None], fc2_far[None], block)[0].T
    fc1_grad = reduce_y(fc1_near[None], fc1_far[None], block)[0]

    norm2_in, norm2_gain_grad, norm2_beta_grad = norm_backward(mlp_up, unit2, inv2, norm2_gain)
    out_full = jnp.concatenate([mine(out_grad), mine(out_in).astype(F32)])
    grad3 = out_full + norm2_in

    gc = grad3.astype(BF)
    cross_proj_bias_grad = bias_total(gc)
    none1 = jnp.zeros((1, 1, width), F32)
    dc_own = mm_nn(gc, mix_own, 2, 1, none1, BF)[0]
    dc_oth = mm_nn(gc, mix_oth, 2, 1, none1, BF)[0]
    dcq, dtext = [], []
    for half, do in enumerate((dc_own, dc_oth)):
        dq, dk, dv = att_backward(
            cqs[half], do, clse[half], [text_low[2 * half]], [text_low[2 * half + 1]], [BF]
        )
        dcq.append(dq)
        dtext += [dk[0], dv[0]]
    dtext_in = [over_core(a) for a in dtext]
    g_text, text_sums = norm_rope_grad(
        traws,
        t_kinds,
        tuple((k, 4 + k) for k in range(4)),
        dtext + dtext_in,
        ck_gain,
        blank,
        blank,
        text_rows,
    )
    text_part = mm_nt([g_text[0], g_text[1]], [g_text[2], g_text[3]], text_own, text_oth, 0)
    text_in = over_x(text_part.astype(BF))
    text_grad = by_image(text_part, text_in.astype(F32))
    g_cq, cq_sums = norm_rope_grad(
        craws, ("rope",) * 2, ((0,), (1,)), dcq, cq_gain, cos_tab, sin_tab, 128
    )
    norm3_up = mm_nt([g_cq[0]], [g_cq[1]], mix_own, mix_oth, 1)
    text_rows_t = dotf(text_places[0], text, NT).astype(BF)
    text_half = 4 * (DT // 16)
    text_g = wgrad(
        [text_rows_t] + list(g_text),
        (
            (((0, 1),), ((0, 0), (1, 0))),
            (((0, 2),), ((0, 1), (1, 1))),
            (((0, 3),), ((0, 2), (1, 2))),
            (((0, 4),), ((0, 3), (1, 3))),
        ),
        [(4, text_half, width)] * 2,
    )
    cross_kv_grad = jnp.swapaxes(reduce_yx(text_g[0], text_g[1], DT // 16), 0, 1)
    norm3_in, norm3_gain_grad, norm3_beta_grad = norm_backward(norm3_up, unit3, inv3, norm3_gain)
    grad2 = grad3 + norm3_in

    ga = grad2.astype(BF)
    proj_bias_grad = bias_total(ga)
    da_own = mm_nn(ga, mix_own, 0, 1, none1, BF)[0]
    da_oth = mm_nn(ga, mix_oth, 0, 1, none1, BF)[0]
    ups = []
    for half, do in enumerate((da_own, da_oth)):
        dq, dk, dv = att_backward(
            qkv_low[3 * half], do, lse[half], keys[half], values[half], [F32, BF]
        )
        ups += [dq, dk[0], over_core(dk[1]), dv[0], over_core(dv[1])]
    ga_rows, act3_rows, gc_rows = by_feature(ga), by_feature(act3), by_feature(gc)
    att_p = [paired(a) for a in att]
    gcq_p = [paired(a) for a in g_cq]
    catt_p = [paired(a) for a in catt]
    arrays = [*ga_rows, *act3_rows, *gc_rows]
    for group in (att_p, gcq_p, catt_p):
        for half in group:
            arrays += half
    jobs = []
    for slab in range(3):
        for half in range(2):
            g0 = 6 + slab * 4 + half * 2
            jobs.append((((2 * slab, g0), (2 * slab + 1, g0 + 1)), ((half, slab),)))
    mix_g = wgrad(arrays, tuple(jobs), [(3, D // 2, width)] * 2)
    mix_grad = reduce_xy(mix_g[0], mix_g[1], block)

    g_qkv, qkv_sums = norm_rope_grad(
        qkv_raws,
        qkv_kinds,
        ((0,), (1, 2), (3, 4), (5,), (6, 7), (8, 9)),
        ups,
        qk_gain,
        cos_tab,
        sin_tab,
        128,
    )
    act1_rows = by_feature(act1)
    arrays = [*act1_rows]
    for g in g_qkv:
        arrays += paired(g)
    jobs = tuple(
        (((0, 2 + 2 * k), (1, 3 + 2 * k)), ((k // 3, k % 3),)) for k in range(6)
    )
    qkv_g = wgrad(arrays, jobs, [(3, D // 2, width)] * 2)
    qkv_grad = jnp.swapaxes(reduce_xy(qkv_g[0], qkv_g[1], block), 0, 1)
    g_n1 = mm_nt(list(g_qkv[:3]), list(g_qkv[3:]), qkv_own, qkv_oth, 0)
    shift_part = jnp.sum(g_n1, axis=0)
    shift_grad = lax.all_gather(shift_part + over_core(shift_part), ("z", "y", "tensor"), axis=0)
    mod_bias_grad = jnp.sum(shift_grad, axis=0)
    mod_grad = lax.dot_general(
        silu_rows.astype(F32),
        shift_grad,
        ROWS_CONTRACT,
        precision=lax.Precision.HIGHEST,
        preferred_element_type=F32,
    )
    norm1_in, norm1_gain_grad, norm1_beta_grad = norm_backward(g_n1, unit1, inv1, norm1_gain)
    grad1 = grad2 + norm1_in

    gs = grad1.astype(BF)
    skip_bias_grad = bias_total(gs)
    gs_own, gs_oth = halves(gs)
    gs_p = paired(gs_own) + paired(gs_oth)
    lat_rows, skp_rows = by_feature(act0[:, :D]), by_feature(act0[:, D:])
    arrays = [*lat_rows, *skp_rows, *gs_p]
    jobs = []
    for slab in range(2):
        for half in range(2):
            g0 = 4 + 2 * half
            jobs.append(
                (
                    ((2 * slab, g0), (2 * slab + 1, g0 + 1)),
                    ((0, 2 * half + slab), (1, 2 * half + slab)),
                )
            )
    skip_g = wgrad(arrays, tuple(jobs), [(4, D // 4, width)] * 2)
    skip_grad = reduce_yx(skip_g[0], skip_g[1], block)
    cat_up = jnp.concatenate(
        [mm_nt([gs_own], [gs_oth], skip_own, skip_oth, k) for k in range(2)], axis=-1
    )
    cat_in, norm0_gain_grad, norm0_beta_grad = norm_backward(cat_up, unit0, inv0, gain0)
    cat_nb = over_x(cat_in[part:].astype(BF)).astype(F32)
    grad_latents = by_image(cat_in[:part, :D], cat_nb[:, :D])
    grad_skip = by_image(cat_in[:part, D:], cat_nb[:, D:])

    def fold(v):
        return jnp.sum(v.reshape(-1, heads_half, HD), axis=(0, 1))

    def total_of(parts):
        flat = jnp.concatenate([p.reshape(-1) for p in parts])
        pad = -flat.shape[0] % 1024
        v = jnp.concatenate([flat, jnp.zeros((pad,), F32)]).reshape(-1, 128)
        v = v + over_core(v)
        v = v + over_x(v)
        v = v + over_y(v)
        v = v + over_z(v, 1)
        v = (v + over_z(v, 2)).reshape(-1)
        res, at = [], 0
        for p in parts:
            res.append(v[at : at + p.size].reshape(p.shape))
            at += p.size
        return res

    def widened(piece):
        blank_piece = jnp.zeros_like(piece)
        return natural(piece, blank_piece)

    share = 0.5
    early = total_of(
        [
            widened(fc1_bias_grad),
            fc2_bias_grad,
            norm2_gain_grad,
            norm2_beta_grad,
            cross_proj_bias_grad,
            norm3_gain_grad,
            norm3_beta_grad,
            natural(cq_sums[2, 0], cq_sums[2, 1]),
            natural(text_sums[2, 0:2], text_sums[2, 2:4]) * share,
            fold(cq_sums[0]),
            fold(cq_sums[1]),
            fold(text_sums[0, 0::2]) * share,
            proj_bias_grad,
        ]
    )
    late = total_of(
        [
            norm0_gain_grad.reshape(2, D),
            norm0_beta_grad.reshape(2, D),
            skip_bias_grad,
            norm1_gain_grad,
            norm1_beta_grad,
            natural(qkv_sums[2, 0:3], qkv_sums[2, 3:6]),
            fold(qkv_sums[0, 0::3]),
            fold(qkv_sums[1, 0::3]),
            fold(qkv_sums[0, 1::3]),
            fold(qkv_sums[1, 1::3]),
        ]
    )

    def narrow(a):
        return halves(a)[0]

    return (
        output,
        grad_latents,
        grad_skip,
        text_grad,
        late[0],
        late[1],
        skip_grad,
        late[2],
        mod_grad,
        mod_bias_grad,
        late[3],
        late[4],
        qkv_grad,
        narrow(late[5]),
        late[6],
        late[7],
        late[8],
        late[9],
        mix_grad[0].T,
        early[12],
        early[5],
        early[6],
        mix_grad[1],
        narrow(early[7]),
        cross_kv_grad,
        narrow(early[8]),
        early[9],
        early[10],
        early[11],
        mix_grad[2].T,
        early[4],
        early[2],
        early[3],
        fc1_grad,
        narrow(early[0]),
        fc2_grad,
        early[1],
    )


def is_spec(spec):
    return isinstance(spec, P)


def split_dp(spec):
    parts = []
    for entry in spec:
        names = entry if isinstance(entry, tuple) else (entry,)
        names = sum((("z", "y") if n == "dp" else (n,) for n in names), ())
        parts.append(names if len(names) > 1 else names[0])
    return P(*parts)


def solution(mesh):
    in_specs = (
        P("dp", ("context", "tensor"), None),
        P("dp", ("context", "tensor"), None),
        P("dp", None, None),
        P("dp", None),
        P("dp", "context", None),
        P("dp", ("context", "tensor"), None),
        P(),
        P(),
        P(None, ("dp", "context"), "tensor"),
        P(),
        P(("dp", "context"), None),
        P(),
        P(),
        P(),
        P(("dp", "context"), None, "tensor"),
        P(None, "tensor"),
        P(),
        P(),
        P(),
        P(),
        P("tensor", ("dp", "context")),
        P(),
        P(),
        P(),
        P(("dp", "context"), "tensor"),
        P("tensor"),
        P(("dp", "context"), None, "tensor"),
        P(None, "tensor"),
        P(),
        P(),
        P(),
        P("tensor", ("dp", "context")),
        P(),
        P(),
        P(),
        P(("dp", "context"), "tensor"),
        P("tensor"),
        P("tensor", ("dp", "context")),
        P(),
    )
    out_specs = (
        P("dp", ("context", "tensor"), None),
        P("dp", ("context", "tensor"), None),
        P("dp", ("context", "tensor"), None),
        P("dp", None, None),
        P(),
        P(),
        P(None, ("dp", "context"), "tensor"),
        P(),
        P(("dp", "context"), None),
        P(),
        P(),
        P(),
        P(("dp", "context"), None, "tensor"),
        P(None, "tensor"),
        P(),
        P(),
        P(),
        P(),
        P("tensor", ("dp", "context")),
        P(),
        P(),
        P(),
        P(("dp", "context"), "tensor"),
        P("tensor"),
        P(("dp", "context"), None, "tensor"),
        P(None, "tensor"),
        P(),
        P(),
        P(),
        P("tensor", ("dp", "context")),
        P(),
        P(),
        P(),
        P(("dp", "context"), "tensor"),
        P("tensor"),
        P("tensor", ("dp", "context")),
        P(),
    )
    program = on_device
    sizes = dict(mesh.shape)
    if (sizes["dp"], sizes["context"], sizes["tensor"]) == (8, 2, 2):
        program = one_image_per_chip
        mesh = Mesh(mesh.devices.reshape(4, 2, 2, 2), GRID_AXES)
        in_specs = jax.tree.map(split_dp, in_specs, is_leaf=is_spec)
        out_specs = jax.tree.map(split_dp, out_specs, is_leaf=is_spec)
    return jax.shard_map(
        program, mesh=mesh, in_specs=in_specs, out_specs=out_specs, check_vma=False
    )
```

```python
import functools

import jax
import jax.numpy as jnp
from jax import lax
from jax.experimental import pallas as pl
from jax.experimental.pallas import tpu as pltpu
from jax.sharding import Mesh
from jax.sharding import PartitionSpec as P

D = 1408
HD = 88
FF = 6144
DT = 1024


EPS = 1e-06
ROWS_CONTRACT = (((0,), (0,)), ((), ()))
COLS_CONTRACT = (((1,), (1,)), ((), ()))


def spread(values):
    return lax.all_gather(values, "tensor", axis=1, tiled=True)


def collect(values):
    return lax.psum_scatter(values, "tensor", scatter_dimension=1, tiled=True)


def weight_grad(activations, gradients):
    return lax.dot_general(
        activations, gradients, ROWS_CONTRACT, preferred_element_type=jnp.float32
    )


def input_grad(gradients, weight_mat):
    return lax.dot_general(gradients, weight_mat, COLS_CONTRACT, preferred_element_type=jnp.float32)


def norm_forward(values, norm_gain, norm_beta):
    centered = values - jnp.mean(values, axis=-1, keepdims=True)
    inv_std = lax.rsqrt(jnp.mean(centered * centered, axis=-1, keepdims=True) + EPS)
    normed = centered * inv_std
    return (normed * norm_gain + norm_beta, normed, inv_std)


def norm_backward(upstream, normed, inv_std, norm_gain):
    scaled = upstream * norm_gain
    inner_term = (
        scaled
        - jnp.mean(scaled, axis=-1, keepdims=True)
        - normed * jnp.mean(scaled * normed, axis=-1, keepdims=True)
    )
    lead_axes = tuple(range(upstream.ndim - 1))
    return (
        inv_std * inner_term,
        jnp.sum(upstream * normed, axis=lead_axes),
        jnp.sum(upstream, axis=lead_axes),
    )


def rope_angles(positions):
    quarter = HD // 4
    frequency = 10000.0 ** (-2.0 * jnp.arange(quarter, dtype=jnp.float32) / (HD // 2))
    places = positions.astype(jnp.float32)
    return jnp.concatenate([places[..., 0:1] * frequency, places[..., 1:2] * frequency], axis=-1)


def rotate(values, angles, direction):
    full_shape = values.shape
    paired = values.reshape(full_shape[:-1] + (HD // 2, 2))
    cos_part = jnp.cos(angles)[..., None, :]
    sin_part = jnp.sin(angles)[..., None, :] * direction
    former = paired[..., 0]
    latter = paired[..., 1]
    turned = jnp.stack(
        [former * cos_part - latter * sin_part, former * sin_part + latter * cos_part], axis=-1
    )
    return turned.reshape(full_shape)


def attend_forward(query_img, key_img, value_img):
    scores = jnp.einsum(
        "qhd,khd->hqk", query_img, key_img, preferred_element_type=jnp.float32
    ) * HD ** (-0.5)
    row_peak = jnp.max(scores, axis=-1, keepdims=True)
    exponent = jnp.exp(scores - row_peak)
    row_total = jnp.sum(exponent, axis=-1, keepdims=True)
    weights_low = (exponent / row_total).astype(jnp.bfloat16)
    result = jnp.einsum("hqk,khd->qhd", weights_low, value_img, preferred_element_type=jnp.float32)
    return (result, row_peak[..., 0] + jnp.log(row_total[..., 0]))


def attend_backward(query_img, key_img, value_img, logsum, grad_img):
    scores = jnp.einsum(
        "qhd,khd->hqk", query_img, key_img, preferred_element_type=jnp.float32
    ) * HD ** (-0.5)
    probs_full = jnp.exp(scores - logsum[..., None])
    grad_probs = jnp.einsum("qhd,khd->hqk", grad_img, value_img, preferred_element_type=jnp.float32)
    delta_row = jnp.sum(probs_full * grad_probs, axis=-1, keepdims=True)
    grad_scores = (probs_full * (grad_probs - delta_row)).astype(jnp.bfloat16)
    grad_query = jnp.einsum(
        "hqk,khd->qhd", grad_scores, key_img, preferred_element_type=jnp.float32
    ) * HD ** (-0.5)
    grad_key = jnp.einsum(
        "hqk,qhd->khd", grad_scores, query_img, preferred_element_type=jnp.float32
    ) * HD ** (-0.5)
    grad_value = jnp.einsum(
        "hqk,qhd->khd",
        probs_full.astype(jnp.bfloat16),
        grad_img,
        preferred_element_type=jnp.float32,
    )
    return (grad_query, grad_key, grad_value)


def bias_total(gradients):
    return jnp.sum(gradients.astype(jnp.float32).reshape(-1, gradients.shape[-1]), axis=0)


def on_device(
    latents,
    skip_states,
    text_states,
    time_vector,
    grid_pos,
    out_grad,
    norm0_gain,
    norm0_beta,
    skip_weight,
    skip_bias,
    mod_weight,
    mod_bias,
    norm1_gain,
    norm1_beta,
    qkv_weight,
    qkv_bias,
    qnorm_gain,
    qnorm_beta,
    knorm_gain,
    knorm_beta,
    proj_weight,
    proj_bias,
    norm3_gain,
    norm3_beta,
    cross_q_weight,
    cross_q_bias,
    cross_kv_weight,
    cross_kv_bias,
    cqnorm_gain,
    cqnorm_beta,
    cknorm_gain,
    cross_proj_weight,
    cross_proj_bias,
    norm2_gain,
    norm2_beta,
    fc1_weight,
    fc1_bias,
    fc2_weight,
    fc2_bias,
):
    context_count = lax.axis_size("context")
    tensor_rank = lax.axis_index("tensor")
    gathered = (
        lax.all_gather(skip_weight, ("dp", "context"), axis=1, tiled=True),
        lax.all_gather(mod_weight, ("dp", "context"), axis=0, tiled=True),
        lax.all_gather(qkv_weight, ("dp", "context"), axis=0, tiled=True),
        lax.all_gather(proj_weight, ("dp", "context"), axis=1, tiled=True),
        lax.all_gather(cross_q_weight, ("dp", "context"), axis=0, tiled=True),
        lax.all_gather(cross_kv_weight, ("dp", "context"), axis=0, tiled=True),
        lax.all_gather(cross_proj_weight, ("dp", "context"), axis=1, tiled=True),
        lax.all_gather(fc1_weight, ("dp", "context"), axis=0, tiled=True),
        lax.all_gather(fc2_weight, ("dp", "context"), axis=1, tiled=True),
    )
    (
        skip_full,
        mod_full,
        qkv_full,
        proj_full,
        crossq_full,
        crosskv_full,
        crossproj_full,
        fc1_full,
        fc2_full,
    ) = gathered
    local_width = qkv_full.shape[2]
    heads_local = local_width // HD
    images = latents.shape[0]
    group_rows = grid_pos.shape[1]
    text_rows = text_states.shape[1]
    flat_rows = images * group_rows
    angles = rope_angles(grid_pos)
    joined = jnp.concatenate(
        [latents.astype(jnp.float32), skip_states.astype(jnp.float32)], axis=-1
    )
    skip_normed, skip_unit, skip_inv = norm_forward(
        joined, norm0_gain.reshape(-1), norm0_beta.reshape(-1)
    )
    skip_act = spread(skip_normed.astype(jnp.bfloat16)).reshape(flat_rows, 2 * D)
    skip_cols = jnp.dot(
        skip_act, skip_full.reshape(2 * D, local_width), preferred_element_type=jnp.float32
    )
    hidden1 = (
        lax.all_to_all(
            skip_cols.reshape(images, group_rows, local_width),
            "tensor",
            split_axis=1,
            concat_axis=2,
            tiled=True,
        )
        + skip_bias
    )
    silu_low = jax.nn.silu(time_vector).astype(jnp.bfloat16)
    shift = jnp.dot(silu_low, mod_full, preferred_element_type=jnp.float32) + mod_bias
    norm1_out, unit_one, inv_one = norm_forward(hidden1, norm1_gain, norm1_beta)
    attn_act = spread((norm1_out + shift[:, None, :]).astype(jnp.bfloat16)).reshape(flat_rows, D)
    merged = jnp.dot(
        attn_act, qkv_full.reshape(D, 3 * local_width), preferred_element_type=jnp.float32
    ) + qkv_bias.reshape(-1)
    merged = merged.reshape(images, group_rows, 3, heads_local, HD)
    query_norm, query_unit, query_inv = norm_forward(merged[:, :, 0], qnorm_gain, qnorm_beta)
    key_norm, key_unit, key_inv = norm_forward(merged[:, :, 1], knorm_gain, knorm_beta)
    queries = rotate(query_norm, angles, 1.0).astype(jnp.bfloat16)
    keys_low = rotate(key_norm, angles, 1.0).astype(jnp.bfloat16)
    values_low = merged[:, :, 2].astype(jnp.bfloat16)
    keys_all, values_all = (
        lax.all_gather(
            keys_low.reshape(images, group_rows, local_width), "context", axis=1, tiled=True
        ),
        lax.all_gather(
            values_low.reshape(images, group_rows, local_width), "context", axis=1, tiled=True
        ),
    )
    keys_all = keys_all.reshape(images, -1, heads_local, HD)
    values_all = values_all.reshape(images, -1, heads_local, HD)
    attn_out, attn_lse = lax.map(
        lambda packed: attend_forward(*packed), (queries, keys_all, values_all)
    )
    attn_low = attn_out.reshape(flat_rows, local_width).astype(jnp.bfloat16)
    hidden2 = (
        hidden1
        + collect(
            jnp.dot(attn_low, proj_full, preferred_element_type=jnp.float32).reshape(
                images, group_rows, D
            )
        )
        + proj_bias
    )
    norm3_out, unit_three, inv_three = norm_forward(hidden2, norm3_gain, norm3_beta)
    cross_act = spread(norm3_out.astype(jnp.bfloat16)).reshape(flat_rows, D)
    cross_raw = (
        jnp.dot(cross_act, crossq_full, preferred_element_type=jnp.float32) + cross_q_bias
    ).reshape(images, group_rows, heads_local, HD)
    cquery_norm, cquery_unit, cquery_inv = norm_forward(cross_raw, cqnorm_gain, cqnorm_beta)
    cross_queries = rotate(cquery_norm, angles, 1.0).astype(jnp.bfloat16)
    text_low = text_states.reshape(images * text_rows, DT)
    text_kv = jnp.dot(
        text_low, crosskv_full.reshape(DT, 2 * local_width), preferred_element_type=jnp.float32
    ) + cross_kv_bias.reshape(-1)
    text_kv = text_kv.reshape(images, text_rows, 2, heads_local, HD)
    ckey_norm, ckey_unit, ckey_inv = norm_forward(text_kv[:, :, 0], cknorm_gain, 0.0)
    cross_keys = ckey_norm.astype(jnp.bfloat16)
    cross_values = text_kv[:, :, 1].astype(jnp.bfloat16)
    cross_out, cross_lse = lax.map(
        lambda packed: attend_forward(*packed), (cross_queries, cross_keys, cross_values)
    )
    cross_low = cross_out.reshape(flat_rows, local_width).astype(jnp.bfloat16)
    hidden3 = (
        hidden2
        + collect(
            jnp.dot(cross_low, crossproj_full, preferred_element_type=jnp.float32).reshape(
                images, group_rows, D
            )
        )
        + cross_proj_bias
    )
    norm2_out, unit_two, inv_two = norm_forward(hidden3, norm2_gain, norm2_beta)
    mlp_act = spread(norm2_out.astype(jnp.bfloat16)).reshape(flat_rows, D)
    pre_act = jnp.dot(mlp_act, fc1_full, preferred_element_type=jnp.float32) + fc1_bias
    post_low = jax.nn.gelu(pre_act, approximate=True).astype(jnp.bfloat16)
    output = (
        hidden3
        + collect(
            jnp.dot(post_low, fc2_full, preferred_element_type=jnp.float32).reshape(
                images, group_rows, D
            )
        )
        + fc2_bias
    )
    out_low = out_grad.astype(jnp.bfloat16)
    fc2_bias_grad = bias_total(out_low)
    out_all = spread(out_low).reshape(flat_rows, D)
    fc2_grad = weight_grad(post_low, out_all)
    post_grad = input_grad(out_all, fc2_full)
    gelu_pull = jax.vjp(lambda inputs: jax.nn.gelu(inputs, approximate=True), pre_act)[1]
    pre_low = gelu_pull(post_grad)[0].astype(jnp.bfloat16)
    fc1_grad = weight_grad(mlp_act, pre_low)
    fc1_bias_grad = bias_total(pre_low)
    mlp_up = collect(input_grad(pre_low, fc1_full).reshape(images, group_rows, D))
    norm2_in, norm2_gain_grad, norm2_beta_grad = norm_backward(
        mlp_up, unit_two, inv_two, norm2_gain
    )
    grad_three = out_grad + norm2_in
    cross_grad_low = grad_three.astype(jnp.bfloat16)
    cross_proj_bias_grad = bias_total(cross_grad_low)
    cross_grad_all = spread(cross_grad_low).reshape(flat_rows, D)
    cross_proj_grad = weight_grad(cross_low, cross_grad_all)
    cross_o_grad = (
        input_grad(cross_grad_all, crossproj_full)
        .astype(jnp.bfloat16)
        .reshape(images, group_rows, heads_local, HD)
    )
    cq_grad, ck_grad, cv_grad = lax.map(
        lambda packed: attend_backward(*packed),
        (cross_queries, cross_keys, cross_values, cross_lse, cross_o_grad),
    )
    ck_grad, cv_grad = (
        lax.psum(ck_grad.astype(jnp.bfloat16), "context").astype(jnp.float32),
        lax.psum(cv_grad.astype(jnp.bfloat16), "context").astype(jnp.float32),
    )
    share = 1.0 / context_count
    ck_in, cknorm_gain_grad, cknorm_unused = norm_backward(
        ck_grad, ckey_unit, ckey_inv, cknorm_gain
    )
    text_grad_low = (
        jnp.stack([ck_in, cv_grad], axis=2)
        .reshape(images * text_rows, 2 * local_width)
        .astype(jnp.bfloat16)
    )
    cross_kv_grad = weight_grad(text_low, text_grad_low).reshape(DT, 2, local_width) * share
    cross_kv_bias_grad = bias_total(text_grad_low).reshape(2, local_width) * share
    text_part = input_grad(text_grad_low, crosskv_full.reshape(DT, 2 * local_width)).reshape(
        images, text_rows, DT
    )
    cq_raw, cqnorm_gain_grad, cqnorm_beta_grad = norm_backward(
        rotate(cq_grad, angles, -1.0), cquery_unit, cquery_inv, cqnorm_gain
    )
    cq_low = cq_raw.reshape(flat_rows, local_width).astype(jnp.bfloat16)
    cross_q_grad = weight_grad(cross_act, cq_low)
    cross_q_bias_grad = bias_total(cq_low)
    norm3_up = collect(input_grad(cq_low, crossq_full).reshape(images, group_rows, D))
    norm3_in, norm3_gain_grad, norm3_beta_grad = norm_backward(
        norm3_up, unit_three, inv_three, norm3_gain
    )
    grad_two = grad_three + norm3_in
    attn_grad_low = grad_two.astype(jnp.bfloat16)
    proj_bias_grad = bias_total(attn_grad_low)
    attn_grad_all = spread(attn_grad_low).reshape(flat_rows, D)
    proj_grad = weight_grad(attn_low, attn_grad_all)
    attn_o_grad = (
        input_grad(attn_grad_all, proj_full)
        .astype(jnp.bfloat16)
        .reshape(images, group_rows, heads_local, HD)
    )
    q_grad, k_all_grad, v_all_grad = lax.map(
        lambda packed: attend_backward(*packed),
        (queries, keys_all, values_all, attn_lse, attn_o_grad),
    )
    k_grad, v_grad = (
        lax.psum_scatter(
            k_all_grad.reshape(images, -1, local_width).astype(jnp.bfloat16),
            "context",
            scatter_dimension=1,
            tiled=True,
        ).astype(jnp.float32),
        lax.psum_scatter(
            v_all_grad.reshape(images, -1, local_width).astype(jnp.bfloat16),
            "context",
            scatter_dimension=1,
            tiled=True,
        ).astype(jnp.float32),
    )
    q_raw, qnorm_gain_grad, qnorm_beta_grad = norm_backward(
        rotate(q_grad, angles, -1.0), query_unit, query_inv, qnorm_gain
    )
    k_raw, knorm_gain_grad, knorm_beta_grad = norm_backward(
        rotate(k_grad.reshape(images, group_rows, heads_local, HD), angles, -1.0),
        key_unit,
        key_inv,
        knorm_gain,
    )
    merged_low = jnp.stack(
        [q_raw, k_raw, v_grad.reshape(images, group_rows, heads_local, HD)], axis=2
    )
    merged_low = merged_low.reshape(flat_rows, 3 * local_width).astype(jnp.bfloat16)
    qkv_grad = weight_grad(attn_act, merged_low).reshape(D, 3, local_width)
    qkv_bias_grad = bias_total(merged_low).reshape(3, local_width)
    norm1_up = collect(
        input_grad(merged_low, qkv_full.reshape(D, 3 * local_width)).reshape(images, group_rows, D)
    )
    shift_part = jnp.sum(norm1_up, axis=1)
    mod_bias_grad = jnp.sum(shift_part, axis=0)
    text_grad, shift_grad = (
        lax.psum(text_part.astype(jnp.bfloat16), "tensor").astype(jnp.float32),
        lax.psum(shift_part.astype(jnp.bfloat16), "tensor").astype(jnp.float32),
    )
    mod_grad = lax.dot_general(
        silu_low.astype(jnp.float32),
        shift_grad,
        ROWS_CONTRACT,
        precision=lax.Precision.HIGHEST,
        preferred_element_type=jnp.float32,
    )
    norm1_in, norm1_gain_grad, norm1_beta_grad = norm_backward(
        norm1_up, unit_one, inv_one, norm1_gain
    )
    grad_one = grad_two + norm1_in
    skip_grad_low = grad_one.astype(jnp.bfloat16)
    skip_bias_grad = bias_total(skip_grad_low)
    skip_cols_grad = lax.all_to_all(
        skip_grad_low, "tensor", split_axis=2, concat_axis=1, tiled=True
    ).reshape(flat_rows, local_width)
    skip_grad = weight_grad(skip_act, skip_cols_grad).reshape(2, D, local_width)
    cat_up = collect(
        input_grad(skip_cols_grad, skip_full.reshape(2 * D, local_width)).reshape(
            images, group_rows, 2 * D
        )
    )
    cat_in, norm0_gain_grad, norm0_beta_grad = norm_backward(
        cat_up, skip_unit, skip_inv, norm0_gain.reshape(-1)
    )
    grad_latents = cat_in[..., :D]
    grad_skip = cat_in[..., D:]

    def widen(piece, total_width):
        blank = jnp.zeros(piece.shape[:-1] + (total_width,), jnp.float32)
        return lax.dynamic_update_slice_in_dim(
            blank, piece, tensor_rank * piece.shape[-1], piece.ndim - 1
        )

    summed = lax.psum(
        (
            norm0_gain_grad,
            norm0_beta_grad,
            skip_bias_grad,
            mod_bias_grad,
            norm1_gain_grad,
            norm1_beta_grad,
            widen(qkv_bias_grad, D),
            qnorm_gain_grad,
            qnorm_beta_grad,
            knorm_gain_grad,
            knorm_beta_grad,
            proj_bias_grad,
            norm3_gain_grad,
            norm3_beta_grad,
            widen(cross_q_bias_grad, D),
            widen(cross_kv_bias_grad, D),
            cqnorm_gain_grad,
            cqnorm_beta_grad,
            cknorm_gain_grad * share,
            cross_proj_bias_grad,
            norm2_gain_grad,
            norm2_beta_grad,
            widen(fc1_bias_grad, FF),
            fc2_bias_grad,
        ),
        ("dp", "context", "tensor"),
    )

    def narrow(whole, piece_width):
        return lax.dynamic_slice_in_dim(
            whole, tensor_rank * piece_width, piece_width, whole.ndim - 1
        )

    weight_sums = (
        lax.psum_scatter(
            skip_grad.astype(jnp.bfloat16), ("dp", "context"), scatter_dimension=1, tiled=True
        ).astype(jnp.float32),
        lax.psum_scatter(
            mod_grad.astype(jnp.bfloat16), ("dp", "context"), scatter_dimension=0, tiled=True
        ).astype(jnp.float32),
        lax.psum_scatter(
            qkv_grad.astype(jnp.bfloat16), ("dp", "context"), scatter_dimension=0, tiled=True
        ).astype(jnp.float32),
        lax.psum_scatter(
            proj_grad.astype(jnp.bfloat16), ("dp", "context"), scatter_dimension=1, tiled=True
        ).astype(jnp.float32),
        lax.psum_scatter(
            cross_q_grad.astype(jnp.bfloat16), ("dp", "context"), scatter_dimension=0, tiled=True
        ).astype(jnp.float32),
        lax.psum_scatter(
            cross_kv_grad.astype(jnp.bfloat16), ("dp", "context"), scatter_dimension=0, tiled=True
        ).astype(jnp.float32),
        lax.psum_scatter(
            cross_proj_grad.astype(jnp.bfloat16), ("dp", "context"), scatter_dimension=1, tiled=True
        ).astype(jnp.float32),
        lax.psum_scatter(
            fc1_grad.astype(jnp.bfloat16), ("dp", "context"), scatter_dimension=0, tiled=True
        ).astype(jnp.float32),
        lax.psum_scatter(
            fc2_grad.astype(jnp.bfloat16), ("dp", "context"), scatter_dimension=1, tiled=True
        ).astype(jnp.float32),
    )
    return (
        output.astype(jnp.bfloat16),
        grad_latents,
        grad_skip,
        text_grad,
        summed[0].reshape(2, D),
        summed[1].reshape(2, D),
        weight_sums[0],
        summed[2],
        weight_sums[1],
        summed[3],
        summed[4],
        summed[5],
        weight_sums[2],
        narrow(summed[6], local_width),
        summed[7],
        summed[8],
        summed[9],
        summed[10],
        weight_sums[3],
        summed[11],
        summed[12],
        summed[13],
        weight_sums[4],
        narrow(summed[14], local_width),
        weight_sums[5],
        narrow(summed[15], local_width),
        summed[16],
        summed[17],
        summed[18],
        weight_sums[6],
        summed[19],
        summed[20],
        summed[21],
        weight_sums[7],
        narrow(summed[22], fc1_bias.shape[0]),
        weight_sums[8],
        summed[23],
    )


F32 = jnp.float32
BF = jnp.bfloat16
VMEM_BYTES = 60 << 20
NN = (((1,), (0,)), ((), ()))
NT = (((1,), (1,)), ((), ()))
TN = (((0,), (0,)), ((), ()))
GRID_AXES = ("z", "y", "context", "tensor")
SWAP = [(0, 1), (1, 0)]
GELU_C = (2.0 / 3.141592653589793) ** 0.5
LANES = 128


def dotf(a, b, dims):
    return lax.dot_general(a, b, dims, preferred_element_type=F32)


STEP_US = {
    "assemble": 8,
    "norm0": 5,
    "mm_norm": 9,
    "mm_heads": 16,
    "att_forward": 16,
    "ff_up": 12,
    "ff_up_grad": 10,
    "ff_down": 10,
    "ff_wgrad": 17,
    "norm_grad": 8,
    "mm_nn": 6,
    "mm_nt": 6,
    "att_backward": 24,
    "wgrad": 11,
    "heads_grad": 14,
    "mm_norm_grad": 14,
    "norm0_grad": 15,
}


def call(body, name, **kw):
    return pl.pallas_call(
        body,
        name=name,
        compiler_params=pltpu.CompilerParams(vmem_limit_bytes=VMEM_BYTES),
        cost_estimate=pl.CostEstimate(
            flops=STEP_US[name] * 3 * 10**9 + 1000, bytes_accessed=1000, transcendentals=0
        ),
        **kw,
    )


def shaped(shape, dtype):
    return jax.ShapeDtypeStruct(shape, dtype)


def fixed(*shape):
    return pl.BlockSpec(shape, lambda *_: (0,) * len(shape))


def scalars():
    return pl.BlockSpec(memory_space=pltpu.SMEM)


def over_x(v):
    return lax.ppermute(v, "tensor", SWAP)


def over_core(v):
    return lax.ppermute(v, "context", SWAP)


def over_y(v):
    return lax.ppermute(v, "y", SWAP)


def all_z(v):
    copies = jnp.broadcast_to(v[None], (4,) + v.shape)
    return lax.all_to_all(copies, "z", split_axis=0, concat_axis=0, tiled=True)


def over_z(v, k):
    return lax.ppermute(v, "z", [(i, i ^ k) for i in range(4)])


def after(value, *deps):
    return lax.optimization_barrier((value, deps))[0]


class Order:
    def __init__(self):
        self.last = None

    def gate(self, value):
        return value if self.last is None else after(value, self.last)

    def mark(self, value):
        self.last = value
        return value

    def pin(self, value):
        return self.mark(self.gate(value))


def assemble_body(halves, ids, *refs):
    o = refs[-1]
    for half in range(halves):
        for k in range(4):
            slot = (ids[1] ^ (k >> 1)) * 2 + (ids[2] ^ (k & 1))
            piece = refs[4 * half + k][0]
            if halves == 1:
                o[:, 0, slot] = piece
            else:
                w = piece.shape[-1]
                o[:, 0, slot, :, half * w : (half + 1) * w] = piece


def assemble(ids, groups):
    _, n, r, w = groups[0][0].shape
    halves = len(groups)
    spec = pl.BlockSpec((1, n, r, w), lambda s, i: (s, 0, 0, 0))
    wide = halves * w
    out = call(
        functools.partial(assemble_body, halves),
        "assemble",
        out_shape=shaped((n, 4, 4, r, wide), groups[0][0].dtype),
        grid_spec=pltpu.PrefetchScalarGridSpec(
            num_scalar_prefetch=1,
            grid=(4,),
            in_specs=[spec] * (4 * halves),
            out_specs=pl.BlockSpec((n, 1, 4, r, wide), lambda s, i: (0, s, 0, 0, 0)),
        ),
    )(ids, *[p for g in groups for p in g])
    return out.reshape(n, 16 * r, wide)


def row_unit(v):
    centered = v - jnp.mean(v, axis=-1, keepdims=True)
    inv = lax.rsqrt(jnp.mean(centered * centered, axis=-1, keepdims=True) + EPS)
    return centered * inv, inv


def norm0_body(lat, skp, gain, beta, o):
    a, b = lat[...].astype(F32), skp[...].astype(F32)
    n = 2.0 * a.shape[1]
    mean = (jnp.sum(a, -1, keepdims=True) + jnp.sum(b, -1, keepdims=True)) / n
    a, b = a - mean, b - mean
    var = (jnp.sum(a * a, -1, keepdims=True) + jnp.sum(b * b, -1, keepdims=True)) / n
    inv = lax.rsqrt(var + EPS)
    o[0] = (a * inv * gain[0:1, :] + beta[0:1, :]).astype(BF)
    o[1] = (b * inv * gain[1:2, :] + beta[1:2, :]).astype(BF)


def norm0(lat, skp, gain, beta, rows):
    t, w = lat.shape
    row = pl.BlockSpec((rows, w), lambda i: (i, 0))
    return call(
        norm0_body,
        "norm0",
        grid=(t // rows,),
        in_specs=[row, row, fixed(2, w), fixed(2, w)],
        out_specs=pl.BlockSpec((2, rows, w), lambda i: (0, i, 0)),
        out_shape=shaped((2, t, w), BF),
    )(lat, skp, gain, beta)


def mm_norm_body(dims, turn, has_res, *refs):
    ids, act, w, bias, gain, beta = refs[:6]
    res = refs[6] if has_res else None
    hidden, low, acc = refs[-3:]
    s = pl.program_id(0)
    part = dotf(act[0], w[0], dims)

    @pl.when(s == 0)
    def _():
        acc[...] = part

    @pl.when(s > 0)
    def _():
        acc[...] += part

    @pl.when(s == pl.num_programs(0) - 1)
    def _():
        v = acc[...]
        if turn:
            v = pltpu.roll(v, ids[3] * (v.shape[1] // 2), 1)
        v = v + bias[...]
        if has_res:
            v = v + res[...]
        hidden[...] = v
        unit, _ = row_unit(v)
        low[...] = (unit * gain[...] + beta[...]).astype(BF)


def mm_norm(ids, act, w, first, dims, turn, bias, gain, beta, res):
    n, t, k = act.shape
    _, a, b = w.shape
    out = b if dims == NN else a
    vec = fixed(1, out)
    big = fixed(t, out)
    extra = [] if res is None else [res]
    return call(
        functools.partial(mm_norm_body, dims, turn, res is not None),
        "mm_norm",
        grid=(n,),
        in_specs=[
            scalars(),
            pl.BlockSpec((1, t, k), lambda s: (s, 0, 0)),
            pl.BlockSpec((1, a, b), lambda s: (first + s, 0, 0)),
            vec,
            vec,
            vec,
        ]
        + [big] * len(extra),
        out_specs=[big, big],
        out_shape=[shaped((t, out), F32), shaped((t, out), BF)],
        scratch_shapes=[pltpu.VMEM((t, out), F32)],
    )(ids, act, w, bias[None], gain[None], beta[None], *extra)


def norm_grad_tail(up, hidden, res, gain, total, low, sums):
    unit, inv = row_unit(hidden)
    scaled = up * gain
    inner = (
        scaled
        - jnp.mean(scaled, axis=-1, keepdims=True)
        - unit * jnp.mean(scaled * unit, axis=-1, keepdims=True)
    )
    g = res + inv * inner
    total[...] = g
    rounded = g.astype(BF)
    low[...] = rounded
    sums[0:1, :] = jnp.sum(up * unit, axis=0, keepdims=True)
    sums[1:2, :] = jnp.sum(up, axis=0, keepdims=True)
    sums[2:3, :] = jnp.sum(rounded.astype(F32), axis=0, keepdims=True)
    return rounded


def norm_grad_body(up, up_in, hidden, res, gain, total, low, sums):
    norm_grad_tail(
        up[...] + up_in[...].astype(F32), hidden[...], res[...], gain[...], total, low, sums
    )


def norm_grad(up, up_in, hidden, res, gain):
    t, w = up.shape
    return call(
        norm_grad_body,
        "norm_grad",
        out_shape=[shaped((t, w), F32), shaped((t, w), BF), shaped((3, w), F32)],
    )(up, up_in, hidden, res, gain[None])


def mm_norm_grad_body(turn, ids, g, w, hidden, res, gain, *refs):
    total, low, sums = refs[:3]
    acc = refs[-1]
    s = pl.program_id(0)
    part = dotf(g[0], w[0], NT)

    @pl.when(s == 0)
    def _():
        acc[...] = part

    @pl.when(s > 0)
    def _():
        acc[...] += part

    @pl.when(s == pl.num_programs(0) - 1)
    def _():
        rounded = norm_grad_tail(
            acc[...], hidden[...], res[...], gain[...], total, low, sums
        )
        if turn:
            shift = ids[3] * (rounded.shape[1] // 2)
            refs[3][...] = pltpu.roll(rounded.astype(F32), shift, 1).astype(BF)


def mm_norm_grad(ids, g, w, first, hidden, res, gain, turn):
    n, t, k = g.shape
    out = w.shape[1]
    big = fixed(t, out)
    return call(
        functools.partial(mm_norm_grad_body, turn),
        "mm_norm_grad",
        grid=(n,),
        in_specs=[
            scalars(),
            pl.BlockSpec((1, t, k), lambda s: (s, 0, 0)),
            pl.BlockSpec((1, out, k), lambda s: (first + s, 0, 0)),
            big,
            big,
            fixed(1, out),
        ],
        out_specs=[big, big, fixed(3, out)] + [big] * turn,
        out_shape=[shaped((t, out), F32), shaped((t, out), BF), shaped((3, out), F32)]
        + [shaped((t, out), BF)] * turn,
        scratch_shapes=[pltpu.VMEM((t, out), F32)],
    )(ids, g, w, hidden, res, gain[None])


def norm0_grad_body(g, w, lat, skp, gain, d_lat, d_skp, sums, ups):
    s = pl.program_id(0)
    ups[s] = dotf(g[...], w[0], NT)

    @pl.when(s == 1)
    def _():
        a, b = lat[...].astype(F32), skp[...].astype(F32)
        n = 2.0 * a.shape[1]
        mean = (jnp.sum(a, -1, keepdims=True) + jnp.sum(b, -1, keepdims=True)) / n
        a, b = a - mean, b - mean
        var = (jnp.sum(a * a, -1, keepdims=True) + jnp.sum(b * b, -1, keepdims=True)) / n
        inv = lax.rsqrt(var + EPS)
        a, b = a * inv, b * inv
        ua, ub = ups[0], ups[1]
        sums[0:1, :] = jnp.sum(ua * a, axis=0, keepdims=True)
        sums[1:2, :] = jnp.sum(ub * b, axis=0, keepdims=True)
        sums[2:3, :] = jnp.sum(ua, axis=0, keepdims=True)
        sums[3:4, :] = jnp.sum(ub, axis=0, keepdims=True)
        ua, ub = ua * gain[0:1, :], ub * gain[1:2, :]
        m1 = (jnp.sum(ua, -1, keepdims=True) + jnp.sum(ub, -1, keepdims=True)) / n
        m2 = (jnp.sum(ua * a, -1, keepdims=True) + jnp.sum(ub * b, -1, keepdims=True)) / n
        d_lat[...] = inv * (ua - m1 - a * m2)
        d_skp[...] = inv * (ub - m1 - b * m2)


def norm0_grad(g, w, lat, skp, gain):
    t, d = lat.shape
    big = fixed(t, d)
    return call(
        norm0_grad_body,
        "norm0_grad",
        grid=(2,),
        in_specs=[big, pl.BlockSpec((1,) + w.shape[1:], lambda s: (s, 0, 0)), big, big, fixed(2, d)],
        out_specs=[big, big, fixed(4, d)],
        out_shape=[shaped((t, d), F32), shaped((t, d), F32), shaped((4, d), F32)],
        scratch_shapes=[pltpu.VMEM((2, t, d), F32)],
    )(g, w, lat, skp, gain)


def mm_body(dims, act, w, o):
    o[...] = dotf(act[...], w[0], dims).astype(o.dtype)


def mm_nn(act, w, first):
    t, k = act.shape
    out = w.shape[2]
    return call(
        functools.partial(mm_body, NN),
        "mm_nn",
        grid=(1,),
        in_specs=[fixed(t, k), pl.BlockSpec((1, k, out), lambda s: (first, 0, 0))],
        out_specs=fixed(t, out),
        out_shape=shaped((t, out), BF),
    )(act, w)


def mm_nt_body(g, w, o):
    part = dotf(g[0], w[0], NT)

    @pl.when(pl.program_id(0) == 0)
    def _():
        o[...] = part

    @pl.when(pl.program_id(0) > 0)
    def _():
        o[...] += part


def mm_nt(g, w):
    n, t, k = g.shape
    out = w.shape[1]
    return call(
        mm_nt_body,
        "mm_nt",
        grid=(n,),
        in_specs=[
            pl.BlockSpec((1, t, k), lambda s: (s, 0, 0)),
            pl.BlockSpec((1, out, k), lambda s: (s, 0, 0)),
        ],
        out_specs=fixed(t, out),
        out_shape=shaped((t, out), F32),
    )(g, w)


def ff_up_body(act, w, b, post, slope):
    v = dotf(act[...], w[0], NN) + b[...]
    inner = jnp.tanh(GELU_C * (v + 0.044715 * v * v * v))
    half = 0.5 * (1.0 + inner)
    post[...] = (v * half).astype(BF)
    slope[...] = (
        half + 0.5 * v * (1.0 - inner * inner) * (GELU_C * (1.0 + 0.134145 * v * v))
    ).astype(BF)


def ff_tile(width):
    return 768 if width % 768 == 0 else width


def ff_up(act, w, bias):
    t, k = act.shape
    width = w.shape[2]
    tile = ff_tile(width)
    col = pl.BlockSpec((t, tile), lambda j: (0, j))
    return call(
        ff_up_body,
        "ff_up",
        grid=(width // tile,),
        in_specs=[
            fixed(t, k),
            pl.BlockSpec((1, k, tile), lambda j: (0, 0, j)),
            pl.BlockSpec((1, tile), lambda j: (0, j)),
        ],
        out_specs=[col, col],
        out_shape=[shaped((t, width), BF)] * 2,
    )(act, w, bias)


def ff_up_grad_body(gm, w, slope, g, total):
    low = (dotf(gm[...], w[0], NN) * slope[...].astype(F32)).astype(BF)
    g[...] = low
    total[...] = jnp.sum(low.astype(F32), axis=0, keepdims=True)


def ff_up_grad(gm, w, slope):
    t, k = gm.shape
    width = w.shape[2]
    tile = ff_tile(width)
    col = pl.BlockSpec((t, tile), lambda j: (0, j))
    return call(
        ff_up_grad_body,
        "ff_up_grad",
        grid=(width // tile,),
        in_specs=[fixed(t, k), pl.BlockSpec((1, k, tile), lambda j: (0, 0, j)), col],
        out_specs=[col, pl.BlockSpec((1, tile), lambda j: (0, j))],
        out_shape=[shaped((t, width), BF), shaped((1, width), F32)],
    )(gm, w, slope)


def ff_down_body(h, w, o, acc):
    part = dotf(h[...], w[0], NT)
    step = pl.program_id(0)

    @pl.when(step == 0)
    def _():
        acc[...] = part

    @pl.when(step > 0)
    def _():
        acc[...] += part

    @pl.when(step == pl.num_programs(0) - 1)
    def _():
        o[...] = acc[...].astype(o.dtype)


def ff_down(h, w, dtype):
    t, width = h.shape
    k = w.shape[1]
    tile = ff_tile(width)
    return call(
        ff_down_body,
        "ff_down",
        grid=(width // tile,),
        in_specs=[
            pl.BlockSpec((t, tile), lambda j: (0, j)),
            pl.BlockSpec((1, k, tile), lambda j: (0, 0, j)),
        ],
        out_specs=fixed(t, k),
        out_shape=shaped((t, k), dtype),
        scratch_shapes=[pltpu.VMEM((t, k), F32)],
    )(h, w)


def core_half(ids, a):
    half = a.shape[1] // 2
    return jnp.where(ids[2] == 0, a[:, :half].astype(F32), a[:, half:].astype(F32)).astype(BF)


def split_rows(ids, acc, far):
    quarter = acc.shape[0] // 4
    at = pl.multiple_of((ids[1] ^ far) * quarter, 8)
    return jnp.concatenate(
        [acc[pl.ds(at, quarter), :], acc[pl.ds(2 * quarter + at, quarter), :]], axis=0
    )


def wgrad_body(jobs, n_in, ids, *refs):
    ins = refs[:n_in]
    outs = refs[n_in:-1]
    acc = refs[-1]
    cache = {}
    for pairs, places in jobs:
        total = None
        for a, (g, slab) in pairs:
            if a not in cache:
                cache[a] = core_half(ids, ins[a][...])
            grad = ins[g][...] if slab is None else ins[g][slab]
            part = dotf(cache[a], grad, TN)
            total = part if total is None else total + part
        acc[...] = total
        half = total.shape[1] // 2
        for far in (0, 1):
            rows = split_rows(ids, acc, far)
            for oth in (0, 1):
                out, at = places[2 * oth + far]
                outs[out][at] = rows[:, oth * half : (oth + 1) * half].astype(BF)


def wgrad(ids, arrays, jobs, out_shapes):
    a0 = arrays[0]
    g = arrays[jobs[0][0][0][1][0]]
    return call(
        functools.partial(wgrad_body, jobs, len(arrays)),
        "wgrad",
        in_specs=[scalars()] + [pl.BlockSpec(memory_space=pltpu.VMEM)] * len(arrays),
        out_shape=[shaped(s, BF) for s in out_shapes],
        scratch_shapes=[pltpu.VMEM((a0.shape[1] // 2, g.shape[-1]), F32)],
    )(ids, *arrays)


def ff_wgrad_body(n, ids, *refs):
    acts, gs = refs[:n], refs[n : 2 * n]
    near, far, turned, acc = refs[2 * n :]

    @pl.when(pl.program_id(0) == 0)
    def _():
        for k in range(n):
            t = acts[k].shape[0]
            turned[:, k * t : (k + 1) * t] = core_half(ids, acts[k][...]).T

    total = None
    for k in range(n):
        t = acts[k].shape[0]
        part = dotf(turned[:, k * t : (k + 1) * t], gs[k][...], NN)
        total = part if total is None else total + part
    acc[...] = total
    near[...] = split_rows(ids, acc, 0).astype(BF)
    far[...] = split_rows(ids, acc, 1).astype(BF)


def ff_wgrad(ids, acts, gs):
    n = len(acts)
    t, k = acts[0].shape
    width = gs[0].shape[1]
    tile = ff_tile(width)
    col = pl.BlockSpec((k // 4, tile), lambda j: (0, j))
    return call(
        functools.partial(ff_wgrad_body, n),
        "ff_wgrad",
        grid=(width // tile,),
        in_specs=[scalars()]
        + [fixed(t, k)] * n
        + [pl.BlockSpec((t, tile), lambda j: (0, j))] * n,
        out_specs=[col, col],
        out_shape=[shaped((k // 4, width), BF)] * 2,
        scratch_shapes=[pltpu.VMEM((k // 2, n * t), BF), pltpu.VMEM((k // 2, tile), F32)],
    )(ids, *acts, *gs)


def two_dots(v, onehot):
    high = v.astype(BF)
    low = (v - high.astype(F32)).astype(BF)
    return dotf(high, onehot, NN) + dotf(low, onehot, NN)


def head_unit(v, s_in, s_out):
    centered = v - two_dots(two_dots(v, s_in) * (1.0 / HD), s_out)
    inv = lax.rsqrt(two_dots(centered * centered, s_in) * (1.0 / HD) + EPS)
    return centered * two_dots(inv, s_out), inv


def swap_pairs(v):
    even = lax.broadcasted_iota(jnp.int32, v.shape, 1) % 2 == 0
    return jnp.where(even, pltpu.roll(v, v.shape[1] - 1, 1), pltpu.roll(v, 1, 1))


def head_spreads(width):
    lanes = jnp.arange(width) // HD
    into = (lanes[:, None] == jnp.arange(LANES)[None, :]).astype(BF)
    return into, into.T


def mm_heads_body(kinds, act, w, bias, gain, beta, cos, sin, s_in, s_out, *refs):
    units, invs = refs[:2]
    for k, kind in enumerate(kinds):

        @pl.when(pl.program_id(0) == k)
        def _(k=k, kind=kind):
            v = dotf(act[...], w[0], NN) + bias[0]
            if kind != "cast":
                unit, inv = head_unit(v, s_in[...], s_out[...])
                units[0] = unit
                invs[0] = inv
                v = unit * gain[k : k + 1, :] + beta[k : k + 1, :]
                if kind == "rope":
                    v = v * cos[...] + swap_pairs(v) * sin[...]
            if k == 0:
                refs[2][...] = v.astype(BF)
            else:
                refs[3][0] = v.astype(BF)


def mm_heads(act, w, first, kinds, bias, gains, betas, tabs, spreads):
    n = len(kinds)
    t, k = act.shape
    out = w.shape[2]
    normed = sum(kind != "cast" for kind in kinds)
    slab = pl.BlockSpec((1, t, out), lambda s: (jnp.minimum(s, normed - 1), 0, 0))
    few = pl.BlockSpec((1, t, LANES), lambda s: (jnp.minimum(s, normed - 1), 0, 0))
    rest = pl.BlockSpec((1, t, out), lambda s: (jnp.maximum(s - 1, 0), 0, 0))
    return call(
        functools.partial(mm_heads_body, kinds),
        "mm_heads",
        grid=(n,),
        in_specs=[
            fixed(t, k),
            pl.BlockSpec((1, k, out), lambda s: (first + s, 0, 0)),
            pl.BlockSpec((1, 1, out), lambda s: (s, 0, 0)),
            fixed(n, out),
            fixed(n, out),
        ]
        + [fixed(*a.shape) for a in tabs + spreads],
        out_specs=[slab, few, fixed(t, out)] + [rest] * (n > 1),
        out_shape=[
            shaped((normed, t, out), F32),
            shaped((normed, t, LANES), F32),
            shaped((t, out), BF),
        ]
        + [shaped((n - 1, t, out), BF)] * (n > 1),
    )(act, w, bias[:, None], gains, betas, *tabs, *spreads)


def heads_grad_body(kinds, plan, n_up, units, invs, *refs):
    ups = refs[:n_up]
    gain, cos, sin, s_in, s_out, out, sums = refs[n_up:]

    @pl.when(pl.program_id(0) == 0)
    def _():
        sums[...] = jnp.zeros_like(sums)

    for k, kind in enumerate(kinds):
        up = None
        for ref, slab in plan[k]:
            piece = (ups[ref][...] if slab is None else ups[ref][slab]).astype(F32)
            up = piece if up is None else up + piece
        if kind != "cast":
            if kind == "rope":
                up = up * cos[...] - swap_pairs(up) * sin[...]
            unit = units[k]
            inv = two_dots(invs[k], s_out[...])
            scaled = up * gain[k : k + 1, :]
            m1 = two_dots(two_dots(scaled, s_in[...]) * (1.0 / HD), s_out[...])
            m2 = two_dots(two_dots(scaled * unit, s_in[...]) * (1.0 / HD), s_out[...])
            sums[0, k : k + 1, :] += jnp.sum(up * unit, axis=0, keepdims=True)
            sums[1, k : k + 1, :] += jnp.sum(up, axis=0, keepdims=True)
            up = inv * (scaled - m1 - unit * m2)
        low = up.astype(BF)
        out[k] = low
        sums[2, k : k + 1, :] += jnp.sum(low.astype(F32), axis=0, keepdims=True)


def heads_grad(norms, kinds, plan, ups, gains, tabs, spreads, rows):
    n = len(kinds)
    _, t, w = norms[0].shape

    def block(a):
        if a.ndim == 2:
            return pl.BlockSpec((rows, a.shape[1]), lambda i: (i, 0))
        return pl.BlockSpec((a.shape[0], rows, a.shape[2]), lambda i: (0, i, 0))

    tab_specs = [block(a) if a.shape[0] == t else fixed(*a.shape) for a in tabs]
    return call(
        functools.partial(heads_grad_body, kinds, plan, len(ups)),
        "heads_grad",
        grid=(t // rows,),
        in_specs=[block(a) for a in norms]
        + [block(u) for u in ups]
        + [fixed(n, w)]
        + tab_specs
        + [fixed(*a.shape) for a in spreads],
        out_specs=[pl.BlockSpec((n, rows, w), lambda i: (0, i, 0)), fixed(3, n, w)],
        out_shape=[shaped((n, t, w), BF), shaped((3, n, w), F32)],
    )(*norms, *ups, gains, *tabs, *spreads)


def att_forward_body(nb, used, *refs):
    q_ref = refs[0]
    kvs = refs[1 : 1 + nb]
    o_ref, lse_ref = refs[1 + nb :]
    scale = HD**-0.5
    for h in range(q_ref.shape[1] // HD):
        s = slice(h * HD, (h + 1) * HD)
        q = q_ref[:, s]
        scores = [dotf(kv[0, :used, s], q, NT) for kv in kvs]
        peak = functools.reduce(
            jnp.maximum, [jnp.max(x, axis=0, keepdims=True) for x in scores]
        )
        expo = [jnp.exp((x - peak) * scale) for x in scores]
        total = sum(jnp.sum(e, axis=0, keepdims=True) for e in expo)
        recip = 1.0 / total
        out = sum(dotf(kv[1, :used, s], (e * recip).astype(BF), TN) for kv, e in zip(kvs, expo))
        o_ref[0, :, s] = out.T.astype(BF)
        lse_ref[h : h + 1, :] = peak * scale + jnp.log(total)


def att_forward(q, kvs, used):
    t, w = q.shape
    return call(
        functools.partial(att_forward_body, len(kvs), used),
        "att_forward",
        out_shape=[shaped((1, t, w), BF), shaped((w // HD, t), F32)],
    )(q, *kvs)


def att_backward_body(nb, used, *refs):
    q_ref, do_ref, lse_ref = refs[:3]
    kvs = refs[3 : 3 + nb]
    dq_ref = refs[3 + nb]
    dkvs = refs[4 + nb :]
    scale = HD**-0.5
    for kv, dkv in zip(kvs, dkvs):
        if used < kv.shape[1]:
            dkv[...] = jnp.zeros_like(dkv)
    for h in range(q_ref.shape[1] // HD):
        s = slice(h * HD, (h + 1) * HD)
        q = q_ref[:, s]
        do = do_ref[:, s]
        lse = lse_ref[h : h + 1, :]
        probs = [jnp.exp(dotf(kv[0, :used, s], q, NT) * scale - lse) for kv in kvs]
        dps = [dotf(kv[1, :used, s], do, NT) for kv in kvs]
        delta = sum(jnp.sum(p * d, axis=0, keepdims=True) for p, d in zip(probs, dps))
        dq = None
        for i in range(nb):
            ds = (probs[i] * (dps[i] - delta)).astype(BF)
            part = dotf(kvs[i][0, :used, s], ds, TN)
            dq = part if dq is None else dq + part
            dkvs[i][0, :used, s] = (dotf(ds, q, NN) * scale).astype(dkvs[i].dtype)
            dkvs[i][1, :used, s] = dotf(probs[i].astype(BF), do, NN).astype(dkvs[i].dtype)
        dq_ref[:, s] = (dq * scale).T


def att_backward(q, do, lse, kvs, kinds, used):
    t, w = q.shape
    nb = len(kvs)
    return call(
        functools.partial(att_backward_body, nb, used),
        "att_backward",
        out_shape=[shaped((t, w), F32)] + [shaped(kv.shape, d) for kv, d in zip(kvs, kinds)],
    )(q, do, lse, *kvs)


def one_image_per_chip(
    latents,
    skip_states,
    text_states,
    time_vector,
    grid_pos,
    out_grad,
    norm0_gain,
    norm0_beta,
    skip_weight,
    skip_bias,
    mod_weight,
    mod_bias,
    norm1_gain,
    norm1_beta,
    qkv_weight,
    qkv_bias,
    qnorm_gain,
    qnorm_beta,
    knorm_gain,
    knorm_beta,
    proj_weight,
    proj_bias,
    norm3_gain,
    norm3_beta,
    cross_q_weight,
    cross_q_bias,
    cross_kv_weight,
    cross_kv_bias,
    cqnorm_gain,
    cqnorm_beta,
    cknorm_gain,
    cross_proj_weight,
    cross_proj_bias,
    norm2_gain,
    norm2_beta,
    fc1_weight,
    fc1_bias,
    fc2_weight,
    fc2_bias,
):
    z, y = lax.axis_index("z"), lax.axis_index("y")
    core, rank = lax.axis_index("context"), lax.axis_index("tensor")
    ids = jnp.stack([z, y, core, rank]).astype(jnp.int32)
    part = latents.shape[1]
    width = qkv_weight.shape[2]
    heads = 2 * width // HD
    block, text_block = D // 16, DT // 16
    order = Order()
    gate, mark, pin = order.gate, order.mark, order.pin

    def mine(a, axis=0):
        return lax.dynamic_index_in_dim(a, rank, axis, keepdims=False)

    def other(a, axis=0):
        return lax.dynamic_index_in_dim(a, 1 - rank, axis, keepdims=False)

    def by_rank(own, oth, axis=0):
        first = rank == 0
        return jnp.stack([jnp.where(first, own, oth), jnp.where(first, oth, own)], axis=axis)

    def natural(a):
        half = a.shape[-1] // 2
        return jnp.where(rank == 0, a, jnp.concatenate([a[..., half:], a[..., :half]], axis=-1))

    time_y = over_y(time_vector)
    bias_pack = jnp.concatenate([qkv_bias, cross_q_bias[None], cross_kv_bias])
    bias_in = over_x(bias_pack)
    time_pair = jnp.stack(
        [jnp.where(y == 0, time_vector, time_y), jnp.where(y == 0, time_y, time_vector)]
    )
    time_z = pin(all_z(time_pair))
    states_in = over_x(after(jnp.stack([other(latents), other(skip_states)]), bias_in))
    skip_z = all_z(gate(skip_weight))
    silu_all = jax.nn.silu(time_z.reshape(-1, D)).astype(BF)
    mod_rows = mod_weight.shape[0]
    image = (z * 2 + y) * 2 + rank
    silu_rows = lax.dynamic_slice_in_dim(
        silu_all, ((z * 2 + y) * 2 + core) * mod_rows, mod_rows, 1
    )
    mod_part = mark(dotf(silu_rows, mod_weight, NN))

    pos_own = mine(grid_pos)
    pos = jnp.concatenate(
        [
            lax.dynamic_slice_in_dim(pos_own, rank * part, part, 0),
            lax.dynamic_slice_in_dim(pos_own, (1 - rank) * part, part, 0),
        ]
    )
    angles = rope_angles(pos)
    cos_row = jnp.repeat(jnp.cos(angles), 2, axis=-1)
    sin_half = jnp.sin(angles)
    sin_row = jnp.stack([-sin_half, sin_half], axis=-1).reshape(cos_row.shape)
    tabs = [jnp.tile(cos_row, (1, heads)), jnp.tile(sin_row, (1, heads))]
    no_tabs = [jnp.zeros((8, LANES), F32)] * 2
    spreads = list(head_spreads(2 * width))

    def per_head(*rows):
        return jnp.stack([jnp.tile(r, heads) for r in rows])

    qk_gain = per_head(qnorm_gain, knorm_gain, knorm_gain)
    qk_beta = per_head(qnorm_beta, knorm_beta, knorm_beta)
    cq_gain, cq_beta = per_head(cqnorm_gain), per_head(cqnorm_beta)
    ck_gain = per_head(cknorm_gain, cknorm_gain)
    biases = jnp.concatenate([bias_pack, bias_in], axis=-1)
    text_used = text_states.shape[1]
    text_fill = -text_used % 16
    text = jnp.pad(mine(text_states), ((0, text_fill), (0, 0)))

    tabs = mark(gate(tabs))
    qkv_piece = jnp.swapaxes(qkv_weight, 0, 1)
    mix_piece = jnp.stack([proj_weight.T, cross_q_weight, cross_proj_weight.T])
    text_piece = jnp.swapaxes(cross_kv_weight, 0, 1)
    fc2_piece = fc2_weight.T[None]
    qkv_piece, mix_piece, text_piece, fc2_piece = pin(
        (qkv_piece, mix_piece, text_piece, fc2_piece)
    )
    skip_z = pin(skip_z)
    mod_z = pin(
        lax.all_to_all(mod_part.reshape(4, 4, D), "z", split_axis=0, concat_axis=0, tiled=True)
    )
    mod_z = jnp.sum(mod_z, axis=0).reshape(2, 2, D)
    mod_y = over_y(lax.dynamic_index_in_dim(mod_z, 1 - y, 0, False))
    skip_y, skip_x, skip_zc = over_y(skip_z), over_x(skip_z), over_core(skip_z)
    qkv_z = all_z(gate(qkv_piece))
    states_in = pin(states_in)
    lat = jnp.concatenate([mine(latents), states_in[0]])
    skp = jnp.concatenate([mine(skip_states), states_in[1]])
    act0 = mark(norm0(lat, skp, norm0_gain, norm0_beta, 128))
    skip_zc = pin(skip_zc)
    mod_y = lax.dynamic_index_in_dim(mod_z, y, 0, False) + pin(mod_y)
    mod_c = over_core(mod_y)
    skip_y, mod_c = pin((skip_y, mod_c))
    skip_xy, skip_yc = over_x(skip_y), over_core(skip_y)
    skip_x = pin(skip_x)
    skip_xc = over_core(skip_x)
    qkv_z = pin(qkv_z)
    qkv_y, qkv_x = over_y(qkv_z), over_x(qkv_z)
    mix_z = all_z(gate(mix_piece))
    skip_yc, skip_xc = pin((skip_yc, skip_xc))
    qkv_zc = over_core(gate(qkv_z))
    skip_xy = pin(skip_xy)
    skip_xyc = over_core(skip_xy)
    qkv_zc = pin(qkv_zc)
    skip_full = mark(
        assemble(ids, [[skip_z, skip_zc, skip_y, skip_yc], [skip_x, skip_xc, skip_xy, gate(skip_xyc)]])
    )
    shift = mine(mod_y + mod_c) + mod_bias
    hidden1, act1 = mark(
        mm_norm(
            ids, act0, skip_full, 0, NN, True, skip_bias, norm1_gain, norm1_beta + shift, None
        )
    )
    qkv_y = pin(qkv_y)
    qkv_xy, qkv_yc = over_x(qkv_y), over_core(qkv_y)
    mix_z = pin(mix_z)
    mix_y, mix_zc = over_y(mix_z), over_core(mix_z)
    text_z = all_z(gate(text_piece))
    qkv_x = pin(qkv_x)
    qkv_xc = over_core(qkv_x)
    qkv_yc = pin(qkv_yc)
    text_z = pin(text_z)
    fc1_z = all_z(gate(fc1_weight[None]))
    mix_zc, qkv_xc = pin((mix_zc, qkv_xc))
    mix_y = pin(mix_y)
    mix_x, text_y, mix_yc = over_x(gate(mix_z)), over_y(gate(text_z)), over_core(mix_y)
    qkv_xy = pin(qkv_xy)
    qkv_xyc = over_core(qkv_xy)
    mix_yc = pin(mix_yc)
    qkv_full = mark(
        assemble(ids, [[qkv_z, qkv_zc, qkv_y, qkv_yc], [qkv_x, qkv_xc, qkv_xy, gate(qkv_xyc)]])
    )

    text_y = pin(text_y)
    qkv_kinds = ("rope", "rope", "cast")
    fc1_z = pin(fc1_z)
    fc1_y, text_zc = over_y(fc1_z), over_core(gate(text_z))
    fc2_z = all_z(gate(fc2_piece))
    *qkv_norms, q_low, kv_low = mark(
        mm_heads(gate(act1), qkv_full, 0, qkv_kinds, biases[:3], qk_gain, qk_beta, tabs, spreads)
    )
    text_zc = pin(text_zc)
    kv_in = over_core(kv_low)
    mix_x = pin(mix_x)
    mix_xy = over_x(gate(mix_y))
    out_low = out_grad.astype(BF)
    kv_in = pin(kv_in)
    mix_xc = over_core(mix_x)
    att, lse = mark(att_forward(gate(q_low), [kv_low, kv_in], kv_low.shape[1]))
    mix_xc = pin(mix_xc)
    text_x, text_yc = over_x(gate(text_z)), over_core(gate(text_y))
    fc2_z, fc1_y = pin((fc2_z, fc1_y))
    fc2_y = over_y(fc2_z)
    text_yc = pin(text_yc)
    fc1_zc = over_core(gate(fc1_z))
    mix_xy = pin(mix_xy)
    mix_xyc = over_core(mix_xy)
    fc1_zc = pin(fc1_zc)
    mix_full = mark(
        assemble(ids, [[mix_z, mix_zc, mix_y, mix_yc], [mix_x, mix_xc, mix_xy, gate(mix_xyc)]])
    )
    text_xy, fc1_yc = over_x(gate(text_y)), over_core(gate(fc1_y))
    out_in = over_x(gate(out_low))
    hidden2, act3 = mark(
        mm_norm(
            ids, gate(att), mix_full, 0, NT, False, proj_bias, norm3_gain, norm3_beta, hidden1
        )
    )

    t_kinds = ("norm", "cast")
    text_x, fc1_yc = pin((text_x, fc1_yc))
    text_xc = over_core(text_x)
    *cq_norms, cq = mark(
        mm_heads(
            gate(act3), mix_full, 1, ("rope",), biases[3:4], cq_gain, cq_beta, tabs, spreads
        )
    )
    text_xc, text_xy = pin((text_xc, text_xy))
    text_xyc = over_core(text_xy)
    fc1_full = mark(assemble(ids, [[gate(fc1_z), fc1_zc, fc1_y, fc1_yc]]))
    text_full = mark(
        assemble(ids, [[text_z, text_zc, text_y, text_yc], [text_x, text_xc, text_xy, gate(text_xyc)]])
    )
    fc2_zc = over_core(gate(fc2_z))
    *t_norms, tk, tv = mark(
        mm_heads(
            text, text_full, 0, t_kinds, biases[4:], ck_gain, jnp.zeros_like(ck_gain), no_tabs, spreads
        )
    )
    fc2_zc = pin(fc2_zc)
    tkv = jnp.concatenate([tk[None], tv])
    act1_cp = over_core(gate(act1))
    catt, clse = mark(att_forward(gate(cq), [tkv], text_used))
    fc2_y, act1_cp = pin((fc2_y, act1_cp))
    fc2_yc = over_core(fc2_y)
    hidden3, act2 = mark(
        mm_norm(
            ids, gate(catt), mix_full, 2, NT, False, cross_proj_bias, norm2_gain, norm2_beta, hidden2
        )
    )

    fc2_yc, out_in = pin((fc2_yc, out_in))
    act2_in, act2_cp = over_x(act2), over_core(gate(act2))
    gm_own = jnp.concatenate([mine(out_low), mine(out_in)])
    gm_oth = jnp.concatenate([other(out_in), other(out_low)])
    fc2_bias_grad = bias_total(gm_own)
    post_own, slope_own = mark(ff_up(gate(act2), fc1_full, fc1_bias[None]))
    act2_cp = pin(act2_cp)
    post_own_cp = over_core(post_own)
    fc2_full = mark(assemble(ids, [[gate(fc2_z), fc2_zc, fc2_y, fc2_yc]]))
    post_own_cp = pin(post_own_cp)
    gm_own_cp = over_core(gate(gm_own))
    down_own = mark(ff_down(gate(post_own), fc2_full, F32))
    act2_in = pin(act2_in)
    post_oth, slope_oth = mark(ff_up(act2_in, fc1_full, fc1_bias[None]))
    gm_own_cp = pin(gm_own_cp)
    post_oth_cp = over_core(post_oth)

    both = ("z", "context")
    far_pair = [
        (2 * zz + cc, 2 * (zz ^ 2) + cc) for zz in range(4) for cc in range(2) if zz // 2 != cc
    ]
    in_pair = [
        (2 * zz + cc, 2 * (zz ^ 1) + cc) for zz in range(4) for cc in range(2) if zz // 2 == cc
    ]
    hand = [(2 * zz + zz // 2, 2 * zz + 1 - zz // 2) for zz in range(4)]

    def z_first(total):
        return total, lax.ppermute(total.astype(BF), both, far_pair)

    def z_second(held, r):
        total, got = held
        n, _, w = total.shape
        blocks = (total + got.astype(F32)).reshape(n, 2, 2 * r, w)
        same = lax.dynamic_index_in_dim(blocks, z & 1, 1, False)
        flip = lax.dynamic_index_in_dim(blocks, 1 - (z & 1), 1, False).astype(BF)
        return same, lax.ppermute(flip, both, in_pair)

    def z_third(held, r):
        same, got = held
        n, _, w = same.shape
        done = (same + got.astype(F32)).reshape(n, 2, r, w)
        keep = lax.dynamic_index_in_dim(done, core, 1, False)
        give = lax.dynamic_index_in_dim(done, 1 - core, 1, False).astype(BF)
        return keep, lax.ppermute(give, both, hand)

    def land(held):
        return jnp.where(z // 2 == core, held[0], held[1].astype(F32))

    g_pre_oth, fc1_sum_oth = mark(ff_up_grad(gate(gm_oth), fc2_full, slope_oth))
    post_oth_cp = pin(post_oth_cp)
    g_oth_cp = over_core(g_pre_oth)
    up_oth = mark(ff_down(gate(g_pre_oth), fc1_full, BF))
    g_oth_cp = pin(g_oth_cp)
    up_in, gm_oth_cp = over_x(up_oth), over_core(gate(gm_oth))
    g_pre_own, fc1_sum_own = mark(ff_up_grad(gate(gm_own), fc2_full, slope_own))
    gm_oth_cp = pin(gm_oth_cp)
    g_own_cp = over_core(g_pre_own)
    fc2_near, fc2_far = mark(
        ff_wgrad(
            ids,
            [gm_own, gm_own_cp, gm_oth, gm_oth_cp],
            [gate(post_own), post_own_cp, post_oth, post_oth_cp],
        )
    )
    g_own_cp = pin(g_own_cp)
    fc2_in = over_y(fc2_far)
    act2_in_cp = over_core(gate(act2_in))
    up_own = mark(ff_down(gate(g_pre_own), fc1_full, F32))
    fc1_bias_grad = (fc1_sum_own + fc1_sum_oth)[0]
    act2_in_cp = pin(act2_in_cp)
    catt_cp = over_core(gate(catt[0]))
    fc1_near, fc1_far = mark(
        ff_wgrad(
            ids,
            [gate(act2), act2_cp, act2_in, act2_in_cp],
            [g_pre_own, g_own_cp, g_pre_oth, g_oth_cp],
        )
    )
    fc1_in = over_y(fc1_far)
    catt_cp, up_in = pin((catt_cp, up_in))
    out_full = jnp.concatenate([mine(out_grad), mine(out_in).astype(F32)])
    grad3, gc, sums2 = mark(norm_grad(gate(up_own), up_in, hidden3, out_full, norm2_gain))
    gc_cp = over_core(gc)
    dc = mark(mm_nn(gate(gc), mix_full, 2))

    gc_cp, fc2_in = pin((gc_cp, fc2_in))
    fc2_held = z_first((fc2_near.astype(F32) + fc2_in.astype(F32))[None])
    mark(fc2_held[0])
    dcq, dtkv = mark(att_backward(cq, gate(dc), clse, [tkv], [BF], text_used))
    dtkv_in = over_core(dtkv)
    cproj_keep, cproj_send = mark(
        wgrad(
            ids,
            [gate(gc), gc_cp, catt, catt_cp],
            ((((0, (2, 0)), (1, (3, None))), ((0, 0), (0, 1), (1, 0), (1, 1))),),
            [(2, D // 4, width)] * 2,
        )
    )
    dtkv_in = pin(dtkv_in)
    cproj_in, att_cp = over_x(cproj_send), over_core(gate(att[0]))
    g_cq, cq_sums = mark(
        heads_grad(
            cq_norms, ("rope",), (((0, None),),), [gate(dcq)], cq_gain, tabs, spreads, 128
        )
    )
    att_cp = pin(att_cp)
    g_cq_cp = over_core(g_cq)
    grad2, ga, sums3 = mark(
        mm_norm_grad(ids, gate(g_cq), mix_full, 1, hidden2, grad3, norm3_gain, False)
    )
    g_cq_cp = pin(g_cq_cp)
    ga_cp = over_core(ga)
    fc2_held = z_second(pin(fc2_held), block)
    mark(fc2_held[0])
    fc1_in = pin(fc1_in)
    fc1_held = z_first((fc1_near.astype(F32) + fc1_in.astype(F32))[None])
    mark(fc1_held[0])
    g_text, text_sums = mark(
        heads_grad(
            t_norms,
            t_kinds,
            (((0, 0), (1, 0)), ((0, 1), (1, 1))),
            [gate(dtkv), dtkv_in],
            ck_gain,
            no_tabs,
            spreads,
            text.shape[0],
        )
    )
    ga_cp = pin(ga_cp)
    act3_cp = over_core(gate(act3))
    text_near, text_far = mark(
        wgrad(
            ids,
            [text, gate(g_text)],
            (
                (((0, (1, 0)),), ((0, 0), (1, 0), (0, 2), (1, 2))),
                (((0, (1, 1)),), ((0, 1), (1, 1), (0, 3), (1, 3))),
            ),
            [(4, DT // 4, width)] * 2,
        )
    )
    text_in_y = over_y(text_far.reshape(16, text_block, width))
    fc2_held = z_third(pin(fc2_held), block)
    act3_cp = pin(act3_cp)
    text_part = mark(mm_nt(gate(g_text), text_full))[:text_used]
    cproj_in = pin(cproj_in)
    text_in = over_x(text_part.astype(BF))
    cproj_sum = cproj_keep.astype(F32) + cproj_in.astype(F32)
    cproj_in_y = over_y(cproj_sum[1:].astype(BF))

    down_oth = mark(ff_down(gate(post_oth), fc2_full, F32))
    fc2_held = pin(fc2_held)
    down_own = down_own + hidden3 + fc2_bias
    down_send = mark(jnp.stack([down_own[part:], down_oth[:part]]).astype(BF))
    text_in, text_in_y = pin((text_in, text_in_y))
    down_in = over_x(down_send)

    da = mark(mm_nn(gate(ga), mix_full, 0))
    text_total = text_near.astype(F32) + text_in_y.reshape(text_near.shape).astype(F32)
    text_in_x = over_x(text_total[2:].astype(BF).reshape(8, text_block, width))
    cproj_in_y = pin(cproj_in_y)
    cproj_held = z_first(cproj_sum[:1] + cproj_in_y.astype(F32))
    mark(cproj_held[0])
    act0_cp = over_core(gate(act0))
    dq, dkv, dkv_give = mark(
        att_backward(q_low, gate(da), lse, [kv_low, kv_in], [F32, BF], kv_low.shape[1])
    )
    act0_cp, down_in = pin((act0_cp, down_in))
    dkv_in = over_core(dkv_give)
    fc1_held = z_second(pin(fc1_held), block)
    mark(fc1_held[0])
    cproj_held = z_second(pin(cproj_held), block)
    mark(cproj_held[0])
    pair_keep, pair_send = mark(
        wgrad(
            ids,
            [gate(ga), ga_cp, act3, act3_cp, att, att_cp, g_cq, g_cq_cp],
            (
                (((0, (4, 0)), (1, (5, None))), ((0, 0), (0, 2), (1, 0), (1, 2))),
                (((2, (6, 0)), (3, (7, 0))), ((0, 1), (0, 3), (1, 1), (1, 3))),
            ),
            [(4, D // 4, width)] * 2,
        )
    )
    dkv_in = pin(dkv_in)
    fc1_held = z_third(pin(fc1_held), block)
    text_in_x = pin(text_in_x)
    pair_in = over_x(pair_send)
    g_qkv, qkv_sums = mark(
        heads_grad(
            qkv_norms,
            qkv_kinds,
            (((0, None),), ((1, 0), (2, 0)), ((1, 1), (2, 1))),
            [gate(dq), dkv, dkv_in],
            qk_gain,
            tabs,
            spreads,
            128,
        )
    )
    fc1_held = pin(fc1_held)
    g_qkv_cp = over_core(g_qkv)
    text_held = z_first(
        text_total[:2] + text_in_x.reshape(2, DT // 4, width).astype(F32)
    )
    mark(text_held[0])
    cproj_held = z_third(pin(cproj_held), block)
    grad1, gs, sums1, gs_turned = mark(
        mm_norm_grad(ids, gate(g_qkv), qkv_full, 0, hidden1, grad2, norm1_gain, True)
    )
    cproj_held = pin(cproj_held)
    g_qkv_cp = pin(g_qkv_cp)
    gs_cp = over_core(gs_turned)
    pair_in = pin(pair_in)
    pair_total = pair_keep.astype(F32) + pair_in.astype(F32)
    pair_in_y = over_y(pair_total[2:].astype(BF))
    text_held = z_second(pin(text_held), text_block)
    mark(text_held[0])
    qkv_near, qkv_far = mark(
        wgrad(
            ids,
            [gate(act1), act1_cp, g_qkv, g_qkv_cp],
            tuple(
                (((0, (2, k)), (1, (3, k))), ((0, k), (1, k), (0, 3 + k), (1, 3 + k)))
                for k in range(3)
            ),
            [(6, D // 4, width)] * 2,
        )
    )
    gs_cp = pin(gs_cp)
    text_held = z_third(pin(text_held), text_block)
    qkv_in_y = over_y(qkv_far)
    pair_in_y = pin(pair_in_y)
    pair_held = z_first(pair_total[:2] + pair_in_y.astype(F32))
    mark(pair_held[0])

    lat_keep, lat_send, skp_near, skp_far = mark(
        wgrad(
            ids,
            [gate(act0[0]), act0_cp[0], act0[1], act0_cp[1], gs_turned, gs_cp],
            (
                (((0, (4, None)), (1, (5, None))), ((0, 0), (0, 1), (1, 0), (1, 1))),
                (((2, (4, None)), (3, (5, None))), ((2, 0), (3, 0), (2, 1), (3, 1))),
            ),
            [(2, D // 4, width)] * 4,
        )
    )
    text_held = pin(text_held)
    lat_in_x = over_x(lat_send)
    d_lat, d_skp, sums0 = mark(norm0_grad(gate(gs_turned), skip_full, lat, skp, norm0_gain))
    skp_in_y = over_y(gate(skp_far))
    d_send = mark(jnp.stack([d_lat[part:], d_skp[part:]]).astype(BF))
    lat_in_x = pin(lat_in_x)
    d_in = over_x(gate(d_send))
    lat_total = lat_keep.astype(F32) + lat_in_x.astype(F32)

    pair_held = z_second(pin(pair_held), block)
    mark(pair_held[0])
    qkv_in_y = pin(qkv_in_y)
    qkv_total = qkv_near.astype(F32) + qkv_in_y.astype(F32)
    qkv_in_x = over_x(qkv_total[3:].astype(BF))
    lat_in_y = over_y(gate(lat_total[1:].astype(BF)))
    pair_held = z_third(pin(pair_held), block)
    skp_in_y = pin(skp_in_y)
    skp_total = skp_near.astype(F32) + skp_in_y.astype(F32)
    skp_in_x = over_x(skp_total[1:].astype(BF))
    d_in = pin(d_in)
    qkv_in_x = pin(qkv_in_x)
    qkv_held = z_first(qkv_total[:3] + qkv_in_x.astype(F32))
    mark(qkv_held[0])
    lat_in_y, skp_in_x = pin((lat_in_y, skp_in_x))
    skip_held = z_first(
        jnp.concatenate(
            [lat_total[:1] + lat_in_y.astype(F32), skp_total[:1] + skp_in_x.astype(F32)]
        )
    )
    qkv_held = z_second(pin(qkv_held), block)
    skip_held = z_second(pin(skip_held), block)
    qkv_held = z_third(qkv_held, block)
    skip_held = z_third(skip_held, block)
    skip_grad = land(skip_held)
    qkv_grad = jnp.swapaxes(land(qkv_held), 0, 1)
    fc2_grad, fc1_grad = land(fc2_held)[0].T, land(fc1_held)[0]
    cproj_grad, pair_grad = land(cproj_held), land(pair_held)
    cross_kv_grad = jnp.swapaxes(land(text_held), 0, 1)

    out_mine = (down_own[:part] + down_in[1].astype(F32)).astype(BF)
    out_other = (down_oth[part:] + down_in[0].astype(F32)).astype(BF)
    output = by_rank(out_mine, out_other)
    text_grad = by_rank(text_part, text_in.astype(F32))
    grad_latents = by_rank(d_lat[:part], d_in[0].astype(F32))
    grad_skip = by_rank(d_skp[:part], d_in[1].astype(F32))

    def fold(v):
        return jnp.sum(v.reshape(-1, heads, HD), axis=(0, 1))

    def total_of(parts):
        flat = jnp.concatenate([p.reshape(-1) for p in parts])
        pad = -flat.shape[0] % 1024
        v = jnp.concatenate([flat, jnp.zeros((pad,), F32)]).reshape(-1, LANES)
        v = v + over_core(v)
        v = v + over_x(v)
        v = v + over_z(v, 1)
        v = v + over_z(v, 2)
        v = (v + over_y(v)).reshape(-1)
        res, at = [], 0
        for p in parts:
            res.append(v[at : at + p.size].reshape(p.shape))
            at += p.size
        return res

    share = 0.5
    fc1_wide = jnp.concatenate([fc1_bias_grad, jnp.zeros_like(fc1_bias_grad)])
    early = total_of(
        [
            natural(fc1_wide),
            fc2_bias_grad,
            sums2[0],
            sums2[1],
            sums2[2],
            sums3[0],
            sums3[1],
            natural(cq_sums[2, 0]),
            natural(text_sums[2]) * share,
            fold(cq_sums[0]),
            fold(cq_sums[1]),
            fold(text_sums[0, 0]) * share,
            sums3[2],
        ]
    )
    rows = (jnp.arange(16) == image).astype(F32)
    middle = total_of(
        [
            sums1[0],
            sums1[1],
            sums1[2],
            natural(qkv_sums[2]),
            fold(qkv_sums[0, 0]),
            fold(qkv_sums[1, 0]),
            fold(qkv_sums[0, 1]),
            fold(qkv_sums[1, 1]),
            rows[:, None] * sums1[1][None],
        ]
    )
    late = total_of([sums0[:2], sums0[2:]])
    mod_grad = lax.dot_general(
        silu_rows.astype(F32),
        middle[8],
        ROWS_CONTRACT,
        precision=lax.Precision.HIGHEST,
        preferred_element_type=F32,
    )

    def narrow(a):
        return mine(a.reshape(a.shape[:-1] + (2, -1)), a.ndim - 1)

    return (
        output,
        grad_latents,
        grad_skip,
        text_grad,
        late[0],
        late[1],
        skip_grad,
        middle[2],
        mod_grad,
        middle[1],
        middle[0],
        middle[1],
        qkv_grad,
        narrow(middle[3]),
        middle[4],
        middle[5],
        middle[6],
        middle[7],
        pair_grad[0].T,
        early[12],
        early[5],
        early[6],
        pair_grad[1],
        narrow(early[7]),
        cross_kv_grad,
        narrow(early[8]),
        early[9],
        early[10],
        early[11],
        cproj_grad[0].T,
        early[4],
        early[2],
        early[3],
        fc1_grad,
        narrow(early[0]),
        fc2_grad,
        early[1],
    )


def is_spec(spec):
    return isinstance(spec, P)


def split_dp(spec):
    parts = []
    for entry in spec:
        names = entry if isinstance(entry, tuple) else (entry,)
        names = sum((("z", "y") if n == "dp" else (n,) for n in names), ())
        parts.append(names if len(names) > 1 else names[0])
    return P(*parts)


def solution(mesh):
    in_specs = (
        P("dp", ("context", "tensor"), None),
        P("dp", ("context", "tensor"), None),
        P("dp", None, None),
        P("dp", None),
        P("dp", "context", None),
        P("dp", ("context", "tensor"), None),
        P(),
        P(),
        P(None, ("dp", "context"), "tensor"),
        P(),
        P(("dp", "context"), None),
        P(),
        P(),
        P(),
        P(("dp", "context"), None, "tensor"),
        P(None, "tensor"),
        P(),
        P(),
        P(),
        P(),
        P("tensor", ("dp", "context")),
        P(),
        P(),
        P(),
        P(("dp", "context"), "tensor"),
        P("tensor"),
        P(("dp", "context"), None, "tensor"),
        P(None, "tensor"),
        P(),
        P(),
        P(),
        P("tensor", ("dp", "context")),
        P(),
        P(),
        P(),
        P(("dp", "context"), "tensor"),
        P("tensor"),
        P("tensor", ("dp", "context")),
        P(),
    )
    out_specs = (
        P("dp", ("context", "tensor"), None),
        P("dp", ("context", "tensor"), None),
        P("dp", ("context", "tensor"), None),
        P("dp", None, None),
        P(),
        P(),
        P(None, ("dp", "context"), "tensor"),
        P(),
        P(("dp", "context"), None),
        P(),
        P(),
        P(),
        P(("dp", "context"), None, "tensor"),
        P(None, "tensor"),
        P(),
        P(),
        P(),
        P(),
        P("tensor", ("dp", "context")),
        P(),
        P(),
        P(),
        P(("dp", "context"), "tensor"),
        P("tensor"),
        P(("dp", "context"), None, "tensor"),
        P(None, "tensor"),
        P(),
        P(),
        P(),
        P("tensor", ("dp", "context")),
        P(),
        P(),
        P(),
        P(("dp", "context"), "tensor"),
        P("tensor"),
        P("tensor", ("dp", "context")),
        P(),
    )
    program = on_device
    sizes = dict(mesh.shape)
    if (sizes["dp"], sizes["context"], sizes["tensor"]) == (8, 2, 2):
        program = one_image_per_chip
        mesh = Mesh(mesh.devices.reshape(4, 2, 2, 2), GRID_AXES)
        in_specs = jax.tree.map(split_dp, in_specs, is_leaf=is_spec)
        out_specs = jax.tree.map(split_dp, out_specs, is_leaf=is_spec)
    return jax.shard_map(
        program, mesh=mesh, in_specs=in_specs, out_specs=out_specs, check_vma=False
    )
```

```python
import functools

import jax
import jax.numpy as jnp
from jax import lax
from jax.experimental import pallas as pl
from jax.experimental.pallas import tpu as pltpu
from jax.sharding import Mesh
from jax.sharding import PartitionSpec as P

DP, CORE, RANK = "dp", "context", "tensor"

D = 1408
HD = 88
FF = 6144
DT = 1024


EPS = 1e-06
ROWS_CONTRACT = (((0,), (0,)), ((), ()))
COLS_CONTRACT = (((1,), (1,)), ((), ()))


def spread(values):
    return lax.all_gather(values, RANK, axis=1, tiled=True)


def collect(values):
    return lax.psum_scatter(values, RANK, scatter_dimension=1, tiled=True)


def weight_grad(activations, gradients):
    return lax.dot_general(
        activations, gradients, ROWS_CONTRACT, preferred_element_type=jnp.float32
    )


def input_grad(gradients, weight_mat):
    return lax.dot_general(gradients, weight_mat, COLS_CONTRACT, preferred_element_type=jnp.float32)


def norm_forward(values, norm_gain, norm_beta):
    centered = values - jnp.mean(values, axis=-1, keepdims=True)
    inv_std = lax.rsqrt(jnp.mean(centered * centered, axis=-1, keepdims=True) + EPS)
    normed = centered * inv_std
    return (normed * norm_gain + norm_beta, normed, inv_std)


def norm_backward(upstream, normed, inv_std, norm_gain):
    scaled = upstream * norm_gain
    inner_term = (
        scaled
        - jnp.mean(scaled, axis=-1, keepdims=True)
        - normed * jnp.mean(scaled * normed, axis=-1, keepdims=True)
    )
    lead_axes = tuple(range(upstream.ndim - 1))
    return (
        inv_std * inner_term,
        jnp.sum(upstream * normed, axis=lead_axes),
        jnp.sum(upstream, axis=lead_axes),
    )


def rope_angles(positions):
    quarter = HD // 4
    frequency = 10000.0 ** (-2.0 * jnp.arange(quarter, dtype=jnp.float32) / (HD // 2))
    places = positions.astype(jnp.float32)
    return jnp.concatenate([places[..., 0:1] * frequency, places[..., 1:2] * frequency], axis=-1)


def rotate(values, angles, direction):
    full_shape = values.shape
    paired = values.reshape(full_shape[:-1] + (HD // 2, 2))
    cos_part = jnp.cos(angles)[..., None, :]
    sin_part = jnp.sin(angles)[..., None, :] * direction
    former = paired[..., 0]
    latter = paired[..., 1]
    turned = jnp.stack(
        [former * cos_part - latter * sin_part, former * sin_part + latter * cos_part], axis=-1
    )
    return turned.reshape(full_shape)


def attend_forward(query_img, key_img, value_img):
    scores = jnp.einsum(
        "qhd,khd->hqk", query_img, key_img, preferred_element_type=jnp.float32
    ) * HD ** (-0.5)
    row_peak = jnp.max(scores, axis=-1, keepdims=True)
    exponent = jnp.exp(scores - row_peak)
    row_total = jnp.sum(exponent, axis=-1, keepdims=True)
    weights_low = (exponent / row_total).astype(jnp.bfloat16)
    result = jnp.einsum("hqk,khd->qhd", weights_low, value_img, preferred_element_type=jnp.float32)
    return (result, row_peak[..., 0] + jnp.log(row_total[..., 0]))


def attend_backward(query_img, key_img, value_img, logsum, grad_img):
    scores = jnp.einsum(
        "qhd,khd->hqk", query_img, key_img, preferred_element_type=jnp.float32
    ) * HD ** (-0.5)
    probs_full = jnp.exp(scores - logsum[..., None])
    grad_probs = jnp.einsum("qhd,khd->hqk", grad_img, value_img, preferred_element_type=jnp.float32)
    delta_row = jnp.sum(probs_full * grad_probs, axis=-1, keepdims=True)
    grad_scores = (probs_full * (grad_probs - delta_row)).astype(jnp.bfloat16)
    grad_query = jnp.einsum(
        "hqk,khd->qhd", grad_scores, key_img, preferred_element_type=jnp.float32
    ) * HD ** (-0.5)
    grad_key = jnp.einsum(
        "hqk,qhd->khd", grad_scores, query_img, preferred_element_type=jnp.float32
    ) * HD ** (-0.5)
    grad_value = jnp.einsum(
        "hqk,qhd->khd",
        probs_full.astype(jnp.bfloat16),
        grad_img,
        preferred_element_type=jnp.float32,
    )
    return (grad_query, grad_key, grad_value)


def bias_total(gradients):
    return jnp.sum(gradients.astype(jnp.float32).reshape(-1, gradients.shape[-1]), axis=0)


def on_device(
    latents,
    skip_states,
    text_states,
    time_vector,
    grid_pos,
    out_grad,
    norm0_gain,
    norm0_beta,
    skip_weight,
    skip_bias,
    mod_weight,
    mod_bias,
    norm1_gain,
    norm1_beta,
    qkv_weight,
    qkv_bias,
    qnorm_gain,
    qnorm_beta,
    knorm_gain,
    knorm_beta,
    proj_weight,
    proj_bias,
    norm3_gain,
    norm3_beta,
    cross_q_weight,
    cross_q_bias,
    cross_kv_weight,
    cross_kv_bias,
    cqnorm_gain,
    cqnorm_beta,
    cknorm_gain,
    cross_proj_weight,
    cross_proj_bias,
    norm2_gain,
    norm2_beta,
    fc1_weight,
    fc1_bias,
    fc2_weight,
    fc2_bias,
):
    context_count = lax.axis_size(CORE)
    tensor_rank = lax.axis_index(RANK)
    gathered = (
        lax.all_gather(skip_weight, (DP, CORE), axis=1, tiled=True),
        lax.all_gather(mod_weight, (DP, CORE), axis=0, tiled=True),
        lax.all_gather(qkv_weight, (DP, CORE), axis=0, tiled=True),
        lax.all_gather(proj_weight, (DP, CORE), axis=1, tiled=True),
        lax.all_gather(cross_q_weight, (DP, CORE), axis=0, tiled=True),
        lax.all_gather(cross_kv_weight, (DP, CORE), axis=0, tiled=True),
        lax.all_gather(cross_proj_weight, (DP, CORE), axis=1, tiled=True),
        lax.all_gather(fc1_weight, (DP, CORE), axis=0, tiled=True),
        lax.all_gather(fc2_weight, (DP, CORE), axis=1, tiled=True),
    )
    (
        skip_full,
        mod_full,
        qkv_full,
        proj_full,
        crossq_full,
        crosskv_full,
        crossproj_full,
        fc1_full,
        fc2_full,
    ) = gathered
    local_width = qkv_full.shape[2]
    heads_local = local_width // HD
    images = latents.shape[0]
    group_rows = grid_pos.shape[1]
    text_rows = text_states.shape[1]
    flat_rows = images * group_rows
    angles = rope_angles(grid_pos)
    joined = jnp.concatenate(
        [latents.astype(jnp.float32), skip_states.astype(jnp.float32)], axis=-1
    )
    skip_normed, skip_unit, skip_inv = norm_forward(
        joined, norm0_gain.reshape(-1), norm0_beta.reshape(-1)
    )
    skip_act = spread(skip_normed.astype(jnp.bfloat16)).reshape(flat_rows, 2 * D)
    skip_cols = jnp.dot(
        skip_act, skip_full.reshape(2 * D, local_width), preferred_element_type=jnp.float32
    )
    hidden1 = (
        lax.all_to_all(
            skip_cols.reshape(images, group_rows, local_width),
            RANK,
            split_axis=1,
            concat_axis=2,
            tiled=True,
        )
        + skip_bias
    )
    silu_low = jax.nn.silu(time_vector).astype(jnp.bfloat16)
    shift = jnp.dot(silu_low, mod_full, preferred_element_type=jnp.float32) + mod_bias
    norm1_out, unit_one, inv_one = norm_forward(hidden1, norm1_gain, norm1_beta)
    attn_act = spread((norm1_out + shift[:, None, :]).astype(jnp.bfloat16)).reshape(flat_rows, D)
    merged = jnp.dot(
        attn_act, qkv_full.reshape(D, 3 * local_width), preferred_element_type=jnp.float32
    ) + qkv_bias.reshape(-1)
    merged = merged.reshape(images, group_rows, 3, heads_local, HD)
    query_norm, query_unit, query_inv = norm_forward(merged[:, :, 0], qnorm_gain, qnorm_beta)
    key_norm, key_unit, key_inv = norm_forward(merged[:, :, 1], knorm_gain, knorm_beta)
    queries = rotate(query_norm, angles, 1.0).astype(jnp.bfloat16)
    keys_low = rotate(key_norm, angles, 1.0).astype(jnp.bfloat16)
    values_low = merged[:, :, 2].astype(jnp.bfloat16)
    keys_all, values_all = (
        lax.all_gather(
            keys_low.reshape(images, group_rows, local_width), CORE, axis=1, tiled=True
        ),
        lax.all_gather(
            values_low.reshape(images, group_rows, local_width), CORE, axis=1, tiled=True
        ),
    )
    keys_all = keys_all.reshape(images, -1, heads_local, HD)
    values_all = values_all.reshape(images, -1, heads_local, HD)
    attn_out, attn_lse = lax.map(
        lambda packed: attend_forward(*packed), (queries, keys_all, values_all)
    )
    attn_low = attn_out.reshape(flat_rows, local_width).astype(jnp.bfloat16)
    hidden2 = (
        hidden1
        + collect(
            jnp.dot(attn_low, proj_full, preferred_element_type=jnp.float32).reshape(
                images, group_rows, D
            )
        )
        + proj_bias
    )
    norm3_out, unit_three, inv_three = norm_forward(hidden2, norm3_gain, norm3_beta)
    cross_act = spread(norm3_out.astype(jnp.bfloat16)).reshape(flat_rows, D)
    cross_raw = (
        jnp.dot(cross_act, crossq_full, preferred_element_type=jnp.float32) + cross_q_bias
    ).reshape(images, group_rows, heads_local, HD)
    cquery_norm, cquery_unit, cquery_inv = norm_forward(cross_raw, cqnorm_gain, cqnorm_beta)
    cross_queries = rotate(cquery_norm, angles, 1.0).astype(jnp.bfloat16)
    text_low = text_states.reshape(images * text_rows, DT)
    text_kv = jnp.dot(
        text_low, crosskv_full.reshape(DT, 2 * local_width), preferred_element_type=jnp.float32
    ) + cross_kv_bias.reshape(-1)
    text_kv = text_kv.reshape(images, text_rows, 2, heads_local, HD)
    ckey_norm, ckey_unit, ckey_inv = norm_forward(text_kv[:, :, 0], cknorm_gain, 0.0)
    cross_keys = ckey_norm.astype(jnp.bfloat16)
    cross_values = text_kv[:, :, 1].astype(jnp.bfloat16)
    cross_out, cross_lse = lax.map(
        lambda packed: attend_forward(*packed), (cross_queries, cross_keys, cross_values)
    )
    cross_low = cross_out.reshape(flat_rows, local_width).astype(jnp.bfloat16)
    hidden3 = (
        hidden2
        + collect(
            jnp.dot(cross_low, crossproj_full, preferred_element_type=jnp.float32).reshape(
                images, group_rows, D
            )
        )
        + cross_proj_bias
    )
    norm2_out, unit_two, inv_two = norm_forward(hidden3, norm2_gain, norm2_beta)
    mlp_act = spread(norm2_out.astype(jnp.bfloat16)).reshape(flat_rows, D)
    pre_act = jnp.dot(mlp_act, fc1_full, preferred_element_type=jnp.float32) + fc1_bias
    post_low = jax.nn.gelu(pre_act, approximate=True).astype(jnp.bfloat16)
    output = (
        hidden3
        + collect(
            jnp.dot(post_low, fc2_full, preferred_element_type=jnp.float32).reshape(
                images, group_rows, D
            )
        )
        + fc2_bias
    )
    out_low = out_grad.astype(jnp.bfloat16)
    fc2_bias_grad = bias_total(out_low)
    out_all = spread(out_low).reshape(flat_rows, D)
    fc2_grad = weight_grad(post_low, out_all)
    post_grad = input_grad(out_all, fc2_full)
    gelu_pull = jax.vjp(lambda inputs: jax.nn.gelu(inputs, approximate=True), pre_act)[1]
    pre_low = gelu_pull(post_grad)[0].astype(jnp.bfloat16)
    fc1_grad = weight_grad(mlp_act, pre_low)
    fc1_bias_grad = bias_total(pre_low)
    mlp_up = collect(input_grad(pre_low, fc1_full).reshape(images, group_rows, D))
    norm2_in, norm2_gain_grad, norm2_beta_grad = norm_backward(
        mlp_up, unit_two, inv_two, norm2_gain
    )
    grad_three = out_grad + norm2_in
    cross_grad_low = grad_three.astype(jnp.bfloat16)
    cross_proj_bias_grad = bias_total(cross_grad_low)
    cross_grad_all = spread(cross_grad_low).reshape(flat_rows, D)
    cross_proj_grad = weight_grad(cross_low, cross_grad_all)
    cross_o_grad = (
        input_grad(cross_grad_all, crossproj_full)
        .astype(jnp.bfloat16)
        .reshape(images, group_rows, heads_local, HD)
    )
    cq_grad, ck_grad, cv_grad = lax.map(
        lambda packed: attend_backward(*packed),
        (cross_queries, cross_keys, cross_values, cross_lse, cross_o_grad),
    )
    ck_grad, cv_grad = (
        lax.psum(ck_grad.astype(jnp.bfloat16), CORE).astype(jnp.float32),
        lax.psum(cv_grad.astype(jnp.bfloat16), CORE).astype(jnp.float32),
    )
    share = 1.0 / context_count
    ck_in, cknorm_gain_grad, cknorm_unused = norm_backward(
        ck_grad, ckey_unit, ckey_inv, cknorm_gain
    )
    text_grad_low = (
        jnp.stack([ck_in, cv_grad], axis=2)
        .reshape(images * text_rows, 2 * local_width)
        .astype(jnp.bfloat16)
    )
    cross_kv_grad = weight_grad(text_low, text_grad_low).reshape(DT, 2, local_width) * share
    cross_kv_bias_grad = bias_total(text_grad_low).reshape(2, local_width) * share
    text_part = input_grad(text_grad_low, crosskv_full.reshape(DT, 2 * local_width)).reshape(
        images, text_rows, DT
    )
    cq_raw, cqnorm_gain_grad, cqnorm_beta_grad = norm_backward(
        rotate(cq_grad, angles, -1.0), cquery_unit, cquery_inv, cqnorm_gain
    )
    cq_low = cq_raw.reshape(flat_rows, local_width).astype(jnp.bfloat16)
    cross_q_grad = weight_grad(cross_act, cq_low)
    cross_q_bias_grad = bias_total(cq_low)
    norm3_up = collect(input_grad(cq_low, crossq_full).reshape(images, group_rows, D))
    norm3_in, norm3_gain_grad, norm3_beta_grad = norm_backward(
        norm3_up, unit_three, inv_three, norm3_gain
    )
    grad_two = grad_three + norm3_in
    attn_grad_low = grad_two.astype(jnp.bfloat16)
    proj_bias_grad = bias_total(attn_grad_low)
    attn_grad_all = spread(attn_grad_low).reshape(flat_rows, D)
    proj_grad = weight_grad(attn_low, attn_grad_all)
    attn_o_grad = (
        input_grad(attn_grad_all, proj_full)
        .astype(jnp.bfloat16)
        .reshape(images, group_rows, heads_local, HD)
    )
    q_grad, k_all_grad, v_all_grad = lax.map(
        lambda packed: attend_backward(*packed),
        (queries, keys_all, values_all, attn_lse, attn_o_grad),
    )
    k_grad, v_grad = (
        lax.psum_scatter(
            k_all_grad.reshape(images, -1, local_width).astype(jnp.bfloat16),
            CORE,
            scatter_dimension=1,
            tiled=True,
        ).astype(jnp.float32),
        lax.psum_scatter(
            v_all_grad.reshape(images, -1, local_width).astype(jnp.bfloat16),
            CORE,
            scatter_dimension=1,
            tiled=True,
        ).astype(jnp.float32),
    )
    q_raw, qnorm_gain_grad, qnorm_beta_grad = norm_backward(
        rotate(q_grad, angles, -1.0), query_unit, query_inv, qnorm_gain
    )
    k_raw, knorm_gain_grad, knorm_beta_grad = norm_backward(
        rotate(k_grad.reshape(images, group_rows, heads_local, HD), angles, -1.0),
        key_unit,
        key_inv,
        knorm_gain,
    )
    merged_low = jnp.stack(
        [q_raw, k_raw, v_grad.reshape(images, group_rows, heads_local, HD)], axis=2
    )
    merged_low = merged_low.reshape(flat_rows, 3 * local_width).astype(jnp.bfloat16)
    qkv_grad = weight_grad(attn_act, merged_low).reshape(D, 3, local_width)
    qkv_bias_grad = bias_total(merged_low).reshape(3, local_width)
    norm1_up = collect(
        input_grad(merged_low, qkv_full.reshape(D, 3 * local_width)).reshape(images, group_rows, D)
    )
    shift_part = jnp.sum(norm1_up, axis=1)
    mod_bias_grad = jnp.sum(shift_part, axis=0)
    text_grad, shift_grad = (
        lax.psum(text_part.astype(jnp.bfloat16), RANK).astype(jnp.float32),
        lax.psum(shift_part.astype(jnp.bfloat16), RANK).astype(jnp.float32),
    )
    mod_grad = lax.dot_general(
        silu_low.astype(jnp.float32),
        shift_grad,
        ROWS_CONTRACT,
        precision=lax.Precision.HIGHEST,
        preferred_element_type=jnp.float32,
    )
    norm1_in, norm1_gain_grad, norm1_beta_grad = norm_backward(
        norm1_up, unit_one, inv_one, norm1_gain
    )
    grad_one = grad_two + norm1_in
    skip_grad_low = grad_one.astype(jnp.bfloat16)
    skip_bias_grad = bias_total(skip_grad_low)
    skip_cols_grad = lax.all_to_all(
        skip_grad_low, RANK, split_axis=2, concat_axis=1, tiled=True
    ).reshape(flat_rows, local_width)
    skip_grad = weight_grad(skip_act, skip_cols_grad).reshape(2, D, local_width)
    cat_up = collect(
        input_grad(skip_cols_grad, skip_full.reshape(2 * D, local_width)).reshape(
            images, group_rows, 2 * D
        )
    )
    cat_in, norm0_gain_grad, norm0_beta_grad = norm_backward(
        cat_up, skip_unit, skip_inv, norm0_gain.reshape(-1)
    )
    grad_latents = cat_in[..., :D]
    grad_skip = cat_in[..., D:]

    def widen(piece, total_width):
        blank = jnp.zeros(piece.shape[:-1] + (total_width,), jnp.float32)
        return lax.dynamic_update_slice_in_dim(
            blank, piece, tensor_rank * piece.shape[-1], piece.ndim - 1
        )

    summed = lax.psum(
        (
            norm0_gain_grad,
            norm0_beta_grad,
            skip_bias_grad,
            mod_bias_grad,
            norm1_gain_grad,
            norm1_beta_grad,
            widen(qkv_bias_grad, D),
            qnorm_gain_grad,
            qnorm_beta_grad,
            knorm_gain_grad,
            knorm_beta_grad,
            proj_bias_grad,
            norm3_gain_grad,
            norm3_beta_grad,
            widen(cross_q_bias_grad, D),
            widen(cross_kv_bias_grad, D),
            cqnorm_gain_grad,
            cqnorm_beta_grad,
            cknorm_gain_grad * share,
            cross_proj_bias_grad,
            norm2_gain_grad,
            norm2_beta_grad,
            widen(fc1_bias_grad, FF),
            fc2_bias_grad,
        ),
        (DP, CORE, RANK),
    )

    def narrow(whole, piece_width):
        return lax.dynamic_slice_in_dim(
            whole, tensor_rank * piece_width, piece_width, whole.ndim - 1
        )

    weight_sums = (
        lax.psum_scatter(
            skip_grad.astype(jnp.bfloat16), (DP, CORE), scatter_dimension=1, tiled=True
        ).astype(jnp.float32),
        lax.psum_scatter(
            mod_grad.astype(jnp.bfloat16), (DP, CORE), scatter_dimension=0, tiled=True
        ).astype(jnp.float32),
        lax.psum_scatter(
            qkv_grad.astype(jnp.bfloat16), (DP, CORE), scatter_dimension=0, tiled=True
        ).astype(jnp.float32),
        lax.psum_scatter(
            proj_grad.astype(jnp.bfloat16), (DP, CORE), scatter_dimension=1, tiled=True
        ).astype(jnp.float32),
        lax.psum_scatter(
            cross_q_grad.astype(jnp.bfloat16), (DP, CORE), scatter_dimension=0, tiled=True
        ).astype(jnp.float32),
        lax.psum_scatter(
            cross_kv_grad.astype(jnp.bfloat16), (DP, CORE), scatter_dimension=0, tiled=True
        ).astype(jnp.float32),
        lax.psum_scatter(
            cross_proj_grad.astype(jnp.bfloat16), (DP, CORE), scatter_dimension=1, tiled=True
        ).astype(jnp.float32),
        lax.psum_scatter(
            fc1_grad.astype(jnp.bfloat16), (DP, CORE), scatter_dimension=0, tiled=True
        ).astype(jnp.float32),
        lax.psum_scatter(
            fc2_grad.astype(jnp.bfloat16), (DP, CORE), scatter_dimension=1, tiled=True
        ).astype(jnp.float32),
    )
    return (
        output.astype(jnp.bfloat16),
        grad_latents,
        grad_skip,
        text_grad,
        summed[0].reshape(2, D),
        summed[1].reshape(2, D),
        weight_sums[0],
        summed[2],
        weight_sums[1],
        summed[3],
        summed[4],
        summed[5],
        weight_sums[2],
        narrow(summed[6], local_width),
        summed[7],
        summed[8],
        summed[9],
        summed[10],
        weight_sums[3],
        summed[11],
        summed[12],
        summed[13],
        weight_sums[4],
        narrow(summed[14], local_width),
        weight_sums[5],
        narrow(summed[15], local_width),
        summed[16],
        summed[17],
        summed[18],
        weight_sums[6],
        summed[19],
        summed[20],
        summed[21],
        weight_sums[7],
        narrow(summed[22], fc1_bias.shape[0]),
        weight_sums[8],
        summed[23],
    )


F32 = jnp.float32
BF = jnp.bfloat16
VMEM_BYTES = 60 << 20
NN = (((1,), (0,)), ((), ()))
NT = (((1,), (1,)), ((), ()))
TN = (((0,), (0,)), ((), ()))
GRID_AXES = ("z", "y", CORE, RANK)
SWAP = [(0, 1), (1, 0)]
GELU_C = (2.0 / 3.141592653589793) ** 0.5
LANES = 128
ROPE, NORM, CAST = 2, 1, 0


def dotf(a, b, dims):
    return lax.dot_general(a, b, dims, preferred_element_type=F32)


def call(body, **kw):
    inner = body.func if isinstance(body, functools.partial) else body
    return pl.pallas_call(
        body,
        name=inner.__name__,
        compiler_params=pltpu.CompilerParams(vmem_limit_bytes=VMEM_BYTES),
        cost_estimate=pl.CostEstimate(flops=1000, bytes_accessed=1000, transcendentals=0),
        **kw,
    )


def shaped(shape, dtype):
    return jax.ShapeDtypeStruct(shape, dtype)


def fixed(*shape):
    return pl.BlockSpec(shape, lambda *_: (0,) * len(shape))


def scalars():
    return pl.BlockSpec(memory_space=pltpu.SMEM)


def over_x(v):
    return lax.ppermute(v, RANK, SWAP)


def over_core(v):
    return lax.ppermute(v, CORE, SWAP)


def over_y(v):
    return lax.ppermute(v, "y", SWAP)


def swap_z(v):
    return lax.all_to_all(v, "z", split_axis=0, concat_axis=0, tiled=True)


def swap_zy(v):
    return lax.all_to_all(v, ("z", "y"), split_axis=0, concat_axis=0, tiled=True)


def copies(v, n):
    return jnp.broadcast_to(v[None], (n,) + v.shape)


def all_z(v):
    return swap_z(copies(v, 4))


def over_z(v, k):
    return lax.ppermute(v, "z", [(i, i ^ k) for i in range(4)])


def after(value, *deps):
    return lax.optimization_barrier((value, deps))[0]


class Order:
    def __init__(self):
        self.last = None

    def gate(self, value):
        return value if self.last is None else after(value, self.last)

    def mark(self, value):
        self.last = value
        return value

    def pin(self, value):
        return self.mark(self.gate(value))


def assemble_body(halves, ids, *refs):
    o = refs[-1]
    for half in range(halves):
        for k in range(4):
            slot = (ids[1] ^ (k >> 1)) * 2 + (ids[2] ^ (k & 1))
            piece = refs[4 * half + k][0]
            if halves == 1:
                o[:, 0, slot] = piece
            else:
                w = piece.shape[-1]
                o[:, 0, slot, :, half * w : (half + 1) * w] = piece


def assemble(ids, groups):
    _, n, r, w = groups[0][0].shape
    halves = len(groups)
    spec = pl.BlockSpec((1, n, r, w), lambda s, i: (s, 0, 0, 0))
    wide = halves * w
    out = call(
        functools.partial(assemble_body, halves),
        out_shape=shaped((n, 4, 4, r, wide), groups[0][0].dtype),
        grid_spec=pltpu.PrefetchScalarGridSpec(
            num_scalar_prefetch=1,
            grid=(4,),
            in_specs=[spec] * (4 * halves),
            out_specs=pl.BlockSpec((n, 1, 4, r, wide), lambda s, i: (0, s, 0, 0, 0)),
        ),
    )(ids, *[p for g in groups for p in g])
    return out.reshape(n, 16 * r, wide)


def row_unit(v):
    centered = v - jnp.mean(v, axis=-1, keepdims=True)
    inv = lax.rsqrt(jnp.mean(centered * centered, axis=-1, keepdims=True) + EPS)
    return centered * inv, inv


def norm0_body(lat, skp, gain, beta, o):
    a, b = lat[...].astype(F32), skp[...].astype(F32)
    n = 2.0 * a.shape[1]
    mean = (jnp.sum(a, -1, keepdims=True) + jnp.sum(b, -1, keepdims=True)) / n
    a, b = a - mean, b - mean
    var = (jnp.sum(a * a, -1, keepdims=True) + jnp.sum(b * b, -1, keepdims=True)) / n
    inv = lax.rsqrt(var + EPS)
    o[0] = (a * inv * gain[0:1, :] + beta[0:1, :]).astype(BF)
    o[1] = (b * inv * gain[1:2, :] + beta[1:2, :]).astype(BF)


def norm0(lat, skp, gain, beta, rows):
    t, w = lat.shape
    row = pl.BlockSpec((rows, w), lambda i: (i, 0))
    return call(
        norm0_body,
        grid=(t // rows,),
        in_specs=[row, row, fixed(2, w), fixed(2, w)],
        out_specs=pl.BlockSpec((2, rows, w), lambda i: (0, i, 0)),
        out_shape=shaped((2, t, w), BF),
    )(lat, skp, gain, beta)


def mm_norm_body(dims, turn, has_res, *refs):
    ids, act, w, bias, gain, beta = refs[:6]
    res = refs[6] if has_res else None
    hidden, low, acc = refs[-3:]
    s = pl.program_id(0)
    part = dotf(act[0], w[0], dims)

    @pl.when(s == 0)
    def _():
        acc[...] = part

    @pl.when(s > 0)
    def _():
        acc[...] += part

    @pl.when(s == pl.num_programs(0) - 1)
    def _():
        v = acc[...]
        if turn:
            v = pltpu.roll(v, ids[3] * (v.shape[1] // 2), 1)
        v = v + bias[...]
        if has_res:
            v = v + res[...]
        hidden[...] = v
        unit, _ = row_unit(v)
        low[...] = (unit * gain[...] + beta[...]).astype(BF)


def mm_norm(ids, act, w, first, dims, turn, bias, gain, beta, res):
    n, t, k = act.shape
    _, a, b = w.shape
    out = b if dims == NN else a
    vec = fixed(1, out)
    big = fixed(t, out)
    extra = [] if res is None else [res]
    return call(
        functools.partial(mm_norm_body, dims, turn, res is not None),
        grid=(n,),
        in_specs=[
            scalars(),
            pl.BlockSpec((1, t, k), lambda s: (s, 0, 0)),
            pl.BlockSpec((1, a, b), lambda s: (first + s, 0, 0)),
            vec,
            vec,
            vec,
        ]
        + [big] * len(extra),
        out_specs=[big, big],
        out_shape=[shaped((t, out), F32), shaped((t, out), BF)],
        scratch_shapes=[pltpu.VMEM((t, out), F32)],
    )(ids, act, w, bias[None], gain[None], beta[None], *extra)


def norm_grad_tail(up, hidden, res, gain, total, low, sums):
    unit, inv = row_unit(hidden)
    scaled = up * gain
    inner = (
        scaled
        - jnp.mean(scaled, axis=-1, keepdims=True)
        - unit * jnp.mean(scaled * unit, axis=-1, keepdims=True)
    )
    g = res + inv * inner
    total[...] = g
    rounded = g.astype(BF)
    low[...] = rounded
    sums[0:1, :] = jnp.sum(up * unit, axis=0, keepdims=True)
    sums[1:2, :] = jnp.sum(up, axis=0, keepdims=True)
    sums[2:3, :] = jnp.sum(rounded.astype(F32), axis=0, keepdims=True)
    return rounded


def norm_grad_body(up, up_in, hidden, res, gain, total, low, sums):
    norm_grad_tail(
        up[...] + up_in[...].astype(F32), hidden[...], res[...], gain[...], total, low, sums
    )


def norm_grad(up, up_in, hidden, res, gain):
    t, w = up.shape
    return call(
        norm_grad_body,
        out_shape=[shaped((t, w), F32), shaped((t, w), BF), shaped((3, w), F32)],
    )(up, up_in, hidden, res, gain[None])


def mm_norm_grad_body(turn, ids, g, w, hidden, res, gain, *refs):
    total, low, sums = refs[:3]
    acc = refs[-1]
    s = pl.program_id(0)
    part = dotf(g[0], w[0], NT)

    @pl.when(s == 0)
    def _():
        acc[...] = part

    @pl.when(s > 0)
    def _():
        acc[...] += part

    @pl.when(s == pl.num_programs(0) - 1)
    def _():
        rounded = norm_grad_tail(
            acc[...], hidden[...], res[...], gain[...], total, low, sums
        )
        if turn:
            shift = ids[3] * (rounded.shape[1] // 2)
            refs[3][...] = pltpu.roll(rounded.astype(F32), shift, 1).astype(BF)


def mm_norm_grad(ids, g, w, first, hidden, res, gain, turn):
    n, t, k = g.shape
    out = w.shape[1]
    big = fixed(t, out)
    return call(
        functools.partial(mm_norm_grad_body, turn),
        grid=(n,),
        in_specs=[
            scalars(),
            pl.BlockSpec((1, t, k), lambda s: (s, 0, 0)),
            pl.BlockSpec((1, out, k), lambda s: (first + s, 0, 0)),
            big,
            big,
            fixed(1, out),
        ],
        out_specs=[big, big, fixed(3, out)] + [big] * turn,
        out_shape=[shaped((t, out), F32), shaped((t, out), BF), shaped((3, out), F32)]
        + [shaped((t, out), BF)] * turn,
        scratch_shapes=[pltpu.VMEM((t, out), F32)],
    )(ids, g, w, hidden, res, gain[None])


def norm0_grad_body(g, w, lat, skp, gain, d_lat, d_skp, sums, ups):
    s = pl.program_id(0)
    ups[s] = dotf(g[...], w[0], NT)

    @pl.when(s == 1)
    def _():
        a, b = lat[...].astype(F32), skp[...].astype(F32)
        n = 2.0 * a.shape[1]
        mean = (jnp.sum(a, -1, keepdims=True) + jnp.sum(b, -1, keepdims=True)) / n
        a, b = a - mean, b - mean
        var = (jnp.sum(a * a, -1, keepdims=True) + jnp.sum(b * b, -1, keepdims=True)) / n
        inv = lax.rsqrt(var + EPS)
        a, b = a * inv, b * inv
        ua, ub = ups[0], ups[1]
        sums[0:1, :] = jnp.sum(ua * a, axis=0, keepdims=True)
        sums[1:2, :] = jnp.sum(ub * b, axis=0, keepdims=True)
        sums[2:3, :] = jnp.sum(ua, axis=0, keepdims=True)
        sums[3:4, :] = jnp.sum(ub, axis=0, keepdims=True)
        ua, ub = ua * gain[0:1, :], ub * gain[1:2, :]
        m1 = (jnp.sum(ua, -1, keepdims=True) + jnp.sum(ub, -1, keepdims=True)) / n
        m2 = (jnp.sum(ua * a, -1, keepdims=True) + jnp.sum(ub * b, -1, keepdims=True)) / n
        d_lat[...] = inv * (ua - m1 - a * m2)
        d_skp[...] = inv * (ub - m1 - b * m2)


def norm0_grad(g, w, lat, skp, gain):
    t, d = lat.shape
    big = fixed(t, d)
    return call(
        norm0_grad_body,
        grid=(2,),
        in_specs=[big, pl.BlockSpec((1,) + w.shape[1:], lambda s: (s, 0, 0)), big, big, fixed(2, d)],
        out_specs=[big, big, fixed(4, d)],
        out_shape=[shaped((t, d), F32), shaped((t, d), F32), shaped((4, d), F32)],
        scratch_shapes=[pltpu.VMEM((2, t, d), F32)],
    )(g, w, lat, skp, gain)


def mm_body(dims, act, w, o):
    o[...] = dotf(act[...], w[0], dims).astype(o.dtype)


def mm_nn(act, w, first):
    t, k = act.shape
    out = w.shape[2]
    return call(
        functools.partial(mm_body, NN),
        grid=(1,),
        in_specs=[fixed(t, k), pl.BlockSpec((1, k, out), lambda s: (first, 0, 0))],
        out_specs=fixed(t, out),
        out_shape=shaped((t, out), BF),
    )(act, w)


def mm_nt_body(g, w, o):
    part = dotf(g[0], w[0], NT)

    @pl.when(pl.program_id(0) == 0)
    def _():
        o[...] = part

    @pl.when(pl.program_id(0) > 0)
    def _():
        o[...] += part


def mm_nt(g, w):
    n, t, k = g.shape
    out = w.shape[1]
    return call(
        mm_nt_body,
        grid=(n,),
        in_specs=[
            pl.BlockSpec((1, t, k), lambda s: (s, 0, 0)),
            pl.BlockSpec((1, out, k), lambda s: (s, 0, 0)),
        ],
        out_specs=fixed(t, out),
        out_shape=shaped((t, out), F32),
    )(g, w)


def ff_up_body(act, w, b, post, slope):
    v = dotf(act[...], w[0], NN) + b[...]
    inner = jnp.tanh(GELU_C * (v + 0.044715 * v * v * v))
    half = 0.5 * (1.0 + inner)
    post[...] = (v * half).astype(BF)
    slope[...] = (
        half + 0.5 * v * (1.0 - inner * inner) * (GELU_C * (1.0 + 0.134145 * v * v))
    ).astype(BF)


def ff_tile(width):
    return 768 if width % 768 == 0 else width


def ff_up(act, w, bias):
    t, k = act.shape
    width = w.shape[2]
    tile = ff_tile(width)
    col = pl.BlockSpec((t, tile), lambda j: (0, j))
    return call(
        ff_up_body,
        grid=(width // tile,),
        in_specs=[
            fixed(t, k),
            pl.BlockSpec((1, k, tile), lambda j: (0, 0, j)),
            pl.BlockSpec((1, tile), lambda j: (0, j)),
        ],
        out_specs=[col, col],
        out_shape=[shaped((t, width), BF)] * 2,
    )(act, w, bias)


def ff_up_grad_body(gm, w, slope, g, total):
    low = (dotf(gm[...], w[0], NN) * slope[...].astype(F32)).astype(BF)
    g[...] = low
    total[...] = jnp.sum(low.astype(F32), axis=0, keepdims=True)


def ff_up_grad(gm, w, slope):
    t, k = gm.shape
    width = w.shape[2]
    tile = ff_tile(width)
    col = pl.BlockSpec((t, tile), lambda j: (0, j))
    return call(
        ff_up_grad_body,
        grid=(width // tile,),
        in_specs=[fixed(t, k), pl.BlockSpec((1, k, tile), lambda j: (0, 0, j)), col],
        out_specs=[col, pl.BlockSpec((1, tile), lambda j: (0, j))],
        out_shape=[shaped((t, width), BF), shaped((1, width), F32)],
    )(gm, w, slope)


def ff_down_body(h, w, o, acc):
    part = dotf(h[...], w[0], NT)
    step = pl.program_id(0)

    @pl.when(step == 0)
    def _():
        acc[...] = part

    @pl.when(step > 0)
    def _():
        acc[...] += part

    @pl.when(step == pl.num_programs(0) - 1)
    def _():
        o[...] = acc[...].astype(o.dtype)


def ff_down(h, w, dtype):
    t, width = h.shape
    k = w.shape[1]
    tile = ff_tile(width)
    return call(
        ff_down_body,
        grid=(width // tile,),
        in_specs=[
            pl.BlockSpec((t, tile), lambda j: (0, j)),
            pl.BlockSpec((1, k, tile), lambda j: (0, 0, j)),
        ],
        out_specs=fixed(t, k),
        out_shape=shaped((t, k), dtype),
        scratch_shapes=[pltpu.VMEM((t, k), F32)],
    )(h, w)


def core_half(ids, a):
    half = a.shape[1] // 2
    return jnp.where(ids[2] == 0, a[:, :half].astype(F32), a[:, half:].astype(F32)).astype(BF)


def split_rows(ids, acc, far):
    quarter = acc.shape[0] // 4
    at = pl.multiple_of((ids[1] ^ far) * quarter, 8)
    return jnp.concatenate(
        [acc[pl.ds(at, quarter), :], acc[pl.ds(2 * quarter + at, quarter), :]], axis=0
    )


def wgrad_body(jobs, n_in, ids, *refs):
    ins = refs[:n_in]
    outs = refs[n_in:-1]
    acc = refs[-1]
    cache = {}
    for pairs, places in jobs:
        total = None
        for a, (g, slab) in pairs:
            if a not in cache:
                cache[a] = core_half(ids, ins[a][...])
            grad = ins[g][...] if slab is None else ins[g][slab]
            part = dotf(cache[a], grad, TN)
            total = part if total is None else total + part
        acc[...] = total
        half = total.shape[1] // 2
        for far in (0, 1):
            rows = split_rows(ids, acc, far)
            for oth in (0, 1):
                out, at = places[2 * oth + far]
                outs[out][at] = rows[:, oth * half : (oth + 1) * half].astype(BF)


def wgrad(ids, arrays, jobs, out_shapes):
    a0 = arrays[0]
    g = arrays[jobs[0][0][0][1][0]]
    return call(
        functools.partial(wgrad_body, jobs, len(arrays)),
        in_specs=[scalars()] + [pl.BlockSpec(memory_space=pltpu.VMEM)] * len(arrays),
        out_shape=[shaped(s, BF) for s in out_shapes],
        scratch_shapes=[pltpu.VMEM((a0.shape[1] // 2, g.shape[-1]), F32)],
    )(ids, *arrays)


def ff_wgrad_body(n, ids, *refs):
    acts, gs = refs[:n], refs[n : 2 * n]
    near, far, turned, acc = refs[2 * n :]

    @pl.when(pl.program_id(0) == 0)
    def _():
        for k in range(n):
            t = acts[k].shape[0]
            turned[:, k * t : (k + 1) * t] = core_half(ids, acts[k][...]).T

    total = None
    for k in range(n):
        t = acts[k].shape[0]
        part = dotf(turned[:, k * t : (k + 1) * t], gs[k][...], NN)
        total = part if total is None else total + part
    acc[...] = total
    near[...] = split_rows(ids, acc, 0).astype(BF)
    far[...] = split_rows(ids, acc, 1).astype(BF)


def ff_wgrad(ids, acts, gs):
    n = len(acts)
    t, k = acts[0].shape
    width = gs[0].shape[1]
    tile = ff_tile(width)
    col = pl.BlockSpec((k // 4, tile), lambda j: (0, j))
    return call(
        functools.partial(ff_wgrad_body, n),
        grid=(width // tile,),
        in_specs=[scalars()]
        + [fixed(t, k)] * n
        + [pl.BlockSpec((t, tile), lambda j: (0, j))] * n,
        out_specs=[col, col],
        out_shape=[shaped((k // 4, width), BF)] * 2,
        scratch_shapes=[pltpu.VMEM((k // 2, n * t), BF), pltpu.VMEM((k // 2, tile), F32)],
    )(ids, *acts, *gs)


def two_dots(v, onehot):
    high = v.astype(BF)
    low = (v - high.astype(F32)).astype(BF)
    return dotf(high, onehot, NN) + dotf(low, onehot, NN)


def head_unit(v, s_in, s_out):
    centered = v - two_dots(two_dots(v, s_in) * (1.0 / HD), s_out)
    inv = lax.rsqrt(two_dots(centered * centered, s_in) * (1.0 / HD) + EPS)
    return centered * two_dots(inv, s_out), inv


def swap_pairs(v):
    even = lax.broadcasted_iota(jnp.int32, v.shape, 1) % 2 == 0
    return jnp.where(even, pltpu.roll(v, v.shape[1] - 1, 1), pltpu.roll(v, 1, 1))


def head_spreads(width):
    lanes = jnp.arange(width) // HD
    into = (lanes[:, None] == jnp.arange(LANES)[None, :]).astype(BF)
    return into, into.T


def mm_heads_body(kinds, act, w, bias, gain, beta, cos, sin, s_in, s_out, *refs):
    units, invs = refs[:2]
    for k, kind in enumerate(kinds):

        @pl.when(pl.program_id(0) == k)
        def _(k=k, kind=kind):
            v = dotf(act[...], w[0], NN) + bias[0]
            if kind != CAST:
                unit, inv = head_unit(v, s_in[...], s_out[...])
                units[0] = unit
                invs[0] = inv
                v = unit * gain[k : k + 1, :] + beta[k : k + 1, :]
                if kind == ROPE:
                    v = v * cos[...] + swap_pairs(v) * sin[...]
            if k == 0:
                refs[2][...] = v.astype(BF)
            else:
                refs[3][0] = v.astype(BF)


def mm_heads(act, w, first, kinds, bias, gains, betas, tabs, spreads):
    n = len(kinds)
    t, k = act.shape
    out = w.shape[2]
    normed = sum(kind != CAST for kind in kinds)
    slab = pl.BlockSpec((1, t, out), lambda s: (jnp.minimum(s, normed - 1), 0, 0))
    few = pl.BlockSpec((1, t, LANES), lambda s: (jnp.minimum(s, normed - 1), 0, 0))
    rest = pl.BlockSpec((1, t, out), lambda s: (jnp.maximum(s - 1, 0), 0, 0))
    return call(
        functools.partial(mm_heads_body, kinds),
        grid=(n,),
        in_specs=[
            fixed(t, k),
            pl.BlockSpec((1, k, out), lambda s: (first + s, 0, 0)),
            pl.BlockSpec((1, 1, out), lambda s: (s, 0, 0)),
            fixed(n, out),
            fixed(n, out),
        ]
        + [fixed(*a.shape) for a in tabs + spreads],
        out_specs=[slab, few, fixed(t, out)] + [rest] * (n > 1),
        out_shape=[
            shaped((normed, t, out), F32),
            shaped((normed, t, LANES), F32),
            shaped((t, out), BF),
        ]
        + [shaped((n - 1, t, out), BF)] * (n > 1),
    )(act, w, bias[:, None], gains, betas, *tabs, *spreads)


def heads_grad_body(kinds, plan, n_up, units, invs, *refs):
    ups = refs[:n_up]
    gain, cos, sin, s_in, s_out, out, sums = refs[n_up:]

    @pl.when(pl.program_id(0) == 0)
    def _():
        sums[...] = jnp.zeros_like(sums)

    for k, kind in enumerate(kinds):
        up = None
        for ref, slab in plan[k]:
            piece = (ups[ref][...] if slab is None else ups[ref][slab]).astype(F32)
            up = piece if up is None else up + piece
        if kind != CAST:
            if kind == ROPE:
                up = up * cos[...] - swap_pairs(up) * sin[...]
            unit = units[k]
            inv = two_dots(invs[k], s_out[...])
            scaled = up * gain[k : k + 1, :]
            m1 = two_dots(two_dots(scaled, s_in[...]) * (1.0 / HD), s_out[...])
            m2 = two_dots(two_dots(scaled * unit, s_in[...]) * (1.0 / HD), s_out[...])
            sums[0, k : k + 1, :] += jnp.sum(up * unit, axis=0, keepdims=True)
            sums[1, k : k + 1, :] += jnp.sum(up, axis=0, keepdims=True)
            up = inv * (scaled - m1 - unit * m2)
        low = up.astype(BF)
        out[k] = low
        sums[2, k : k + 1, :] += jnp.sum(low.astype(F32), axis=0, keepdims=True)


def heads_grad(norms, kinds, plan, ups, gains, tabs, spreads, rows):
    n = len(kinds)
    _, t, w = norms[0].shape

    def block(a):
        if a.ndim == 2:
            return pl.BlockSpec((rows, a.shape[1]), lambda i: (i, 0))
        return pl.BlockSpec((a.shape[0], rows, a.shape[2]), lambda i: (0, i, 0))

    tab_specs = [block(a) if a.shape[0] == t else fixed(*a.shape) for a in tabs]
    return call(
        functools.partial(heads_grad_body, kinds, plan, len(ups)),
        grid=(t // rows,),
        in_specs=[block(a) for a in norms]
        + [block(u) for u in ups]
        + [fixed(n, w)]
        + tab_specs
        + [fixed(*a.shape) for a in spreads],
        out_specs=[pl.BlockSpec((n, rows, w), lambda i: (0, i, 0)), fixed(3, n, w)],
        out_shape=[shaped((n, t, w), BF), shaped((3, n, w), F32)],
    )(*norms, *ups, gains, *tabs, *spreads)


def att_forward_body(nb, used, *refs):
    q_ref = refs[0]
    kvs = refs[1 : 1 + nb]
    o_ref, lse_ref = refs[1 + nb :]
    scale = HD**-0.5
    for h in range(q_ref.shape[1] // HD):
        s = slice(h * HD, (h + 1) * HD)
        q = q_ref[:, s]
        scores = [dotf(kv[0, :used, s], q, NT) for kv in kvs]
        peak = functools.reduce(
            jnp.maximum, [jnp.max(x, axis=0, keepdims=True) for x in scores]
        )
        expo = [jnp.exp((x - peak) * scale) for x in scores]
        total = sum(jnp.sum(e, axis=0, keepdims=True) for e in expo)
        recip = 1.0 / total
        out = sum(dotf(kv[1, :used, s], (e * recip).astype(BF), TN) for kv, e in zip(kvs, expo))
        o_ref[0, :, s] = out.T.astype(BF)
        lse_ref[h : h + 1, :] = peak * scale + jnp.log(total)


def att_forward(q, kvs, used):
    t, w = q.shape
    return call(
        functools.partial(att_forward_body, len(kvs), used),
        out_shape=[shaped((1, t, w), BF), shaped((w // HD, t), F32)],
    )(q, *kvs)


def att_backward_body(nb, used, *refs):
    q_ref, do_ref, lse_ref = refs[:3]
    kvs = refs[3 : 3 + nb]
    dq_ref = refs[3 + nb]
    dkvs = refs[4 + nb :]
    scale = HD**-0.5
    for kv, dkv in zip(kvs, dkvs):
        if used < kv.shape[1]:
            dkv[...] = jnp.zeros_like(dkv)
    for h in range(q_ref.shape[1] // HD):
        s = slice(h * HD, (h + 1) * HD)
        q = q_ref[:, s]
        do = do_ref[:, s]
        lse = lse_ref[h : h + 1, :]
        probs = [jnp.exp(dotf(kv[0, :used, s], q, NT) * scale - lse) for kv in kvs]
        dps = [dotf(kv[1, :used, s], do, NT) for kv in kvs]
        delta = sum(jnp.sum(p * d, axis=0, keepdims=True) for p, d in zip(probs, dps))
        dq = None
        for i in range(nb):
            ds = (probs[i] * (dps[i] - delta)).astype(BF)
            part = dotf(kvs[i][0, :used, s], ds, TN)
            dq = part if dq is None else dq + part
            dkvs[i][0, :used, s] = (dotf(ds, q, NN) * scale).astype(dkvs[i].dtype)
            dkvs[i][1, :used, s] = dotf(probs[i].astype(BF), do, NN).astype(dkvs[i].dtype)
        dq_ref[:, s] = (dq * scale).T


def att_backward(q, do, lse, kvs, kinds, used):
    t, w = q.shape
    nb = len(kvs)
    return call(
        functools.partial(att_backward_body, nb, used),
        out_shape=[shaped((t, w), F32)] + [shaped(kv.shape, d) for kv, d in zip(kvs, kinds)],
    )(q, do, lse, *kvs)


def one_image_per_chip(
    latents,
    skip_states,
    text_states,
    time_vector,
    grid_pos,
    out_grad,
    norm0_gain,
    norm0_beta,
    skip_weight,
    skip_bias,
    mod_weight,
    mod_bias,
    norm1_gain,
    norm1_beta,
    qkv_weight,
    qkv_bias,
    qnorm_gain,
    qnorm_beta,
    knorm_gain,
    knorm_beta,
    proj_weight,
    proj_bias,
    norm3_gain,
    norm3_beta,
    cross_q_weight,
    cross_q_bias,
    cross_kv_weight,
    cross_kv_bias,
    cqnorm_gain,
    cqnorm_beta,
    cknorm_gain,
    cross_proj_weight,
    cross_proj_bias,
    norm2_gain,
    norm2_beta,
    fc1_weight,
    fc1_bias,
    fc2_weight,
    fc2_bias,
):
    z, y = lax.axis_index("z"), lax.axis_index("y")
    core, rank = lax.axis_index(CORE), lax.axis_index(RANK)
    ids = jnp.stack([z, y, core, rank]).astype(jnp.int32)
    part = latents.shape[1]
    width = qkv_weight.shape[2]
    heads = 2 * width // HD
    block, text_block = D // 16, DT // 16
    order = Order()
    gate, mark, pin = order.gate, order.mark, order.pin

    def mine(a, axis=0):
        return lax.dynamic_index_in_dim(a, rank, axis, keepdims=False)

    def other(a, axis=0):
        return lax.dynamic_index_in_dim(a, 1 - rank, axis, keepdims=False)

    def by_rank(own, oth, axis=0):
        first = rank == 0
        return jnp.stack([jnp.where(first, own, oth), jnp.where(first, oth, own)], axis=axis)

    def natural(a):
        half = a.shape[-1] // 2
        return jnp.where(rank == 0, a, jnp.concatenate([a[..., half:], a[..., :half]], axis=-1))

    time_all = swap_zy(copies(time_vector, 8))
    bias_pack = jnp.concatenate([qkv_bias, cross_q_bias[None], cross_kv_bias])
    bias_in = over_x(bias_pack)
    states_in = over_x(jnp.stack([other(latents), other(skip_states)]))
    time_all = pin(time_all)
    skip_z = all_z(gate(skip_weight))
    silu_all = jax.nn.silu(time_all.reshape(-1, D)).astype(BF)
    mod_rows = mod_weight.shape[0]
    image = (z * 2 + y) * 2 + rank
    silu_rows = lax.dynamic_slice_in_dim(
        silu_all, ((z * 2 + y) * 2 + core) * mod_rows, mod_rows, 1
    )
    mod_part = mark(dotf(silu_rows, mod_weight, NN))

    pos_own = mine(grid_pos)
    pos = jnp.concatenate(
        [
            lax.dynamic_slice_in_dim(pos_own, rank * part, part, 0),
            lax.dynamic_slice_in_dim(pos_own, (1 - rank) * part, part, 0),
        ]
    )
    angles = rope_angles(pos)
    cos_row = jnp.repeat(jnp.cos(angles), 2, axis=-1)
    sin_half = jnp.sin(angles)
    sin_row = jnp.stack([-sin_half, sin_half], axis=-1).reshape(cos_row.shape)
    tabs = [jnp.tile(cos_row, (1, heads)), jnp.tile(sin_row, (1, heads))]
    no_tabs = [jnp.zeros((8, LANES), F32)] * 2
    spreads = list(head_spreads(2 * width))

    def per_head(*rows):
        return jnp.stack([jnp.tile(r, heads) for r in rows])

    qk_gain = per_head(qnorm_gain, knorm_gain, knorm_gain)
    qk_beta = per_head(qnorm_beta, knorm_beta, knorm_beta)
    cq_gain, cq_beta = per_head(cqnorm_gain), per_head(cqnorm_beta)
    ck_gain = per_head(cknorm_gain, cknorm_gain)
    biases = jnp.concatenate([bias_pack, bias_in], axis=-1)
    text_used = text_states.shape[1]
    text_fill = -text_used % 16
    text = jnp.pad(mine(text_states), ((0, text_fill), (0, 0)))

    tabs, qk_gain, qk_beta, cq_gain, cq_beta, ck_gain, biases, text = pin(
        (tabs, qk_gain, qk_beta, cq_gain, cq_beta, ck_gain, biases, text)
    )
    pieces = pin(
        (
            jnp.swapaxes(qkv_weight, 0, 1),
            jnp.stack([proj_weight.T, cross_q_weight, cross_proj_weight.T]),
            jnp.swapaxes(cross_kv_weight, 0, 1),
            fc2_weight.T[None],
            out_grad.astype(BF),
        )
    )
    qkv_piece, mix_piece, text_piece, fc2_piece, out_low = pieces
    skip_z, states_in = pin((skip_z, states_in))
    skip_y, skip_x, skip_zc = over_y(skip_z), over_x(skip_z), over_core(skip_z)
    qkv_z = all_z(gate(qkv_piece))
    lat = jnp.concatenate([mine(latents), states_in[0]])
    skp = jnp.concatenate([mine(skip_states), states_in[1]])
    act0 = mark(norm0(lat, skp, norm0_gain, norm0_beta, 128))
    skip_y, skip_x, skip_zc = pin((skip_y, skip_x, skip_zc))
    skip_xy, skip_yc, skip_xc = over_x(skip_y), over_core(skip_y), over_core(skip_x)
    skip_yc, skip_xc, qkv_z = pin((skip_yc, skip_xc, qkv_z))
    qkv_y, qkv_x, mod_z = over_y(qkv_z), over_x(qkv_z), swap_zy(gate(mod_part).reshape(8, 2, D))
    skip_xy, mod_z = pin((skip_xy, mod_z))
    mod_sum = jnp.sum(mod_z, axis=0)
    skip_xyc, mod_c = over_core(skip_xy), over_core(mod_sum)
    mix_z = all_z(gate(mix_piece))
    skip_xyc, mod_c = pin((skip_xyc, mod_c))
    shift = mine(mod_sum + mod_c) + mod_bias
    skip_full = mark(
        assemble(ids, [[skip_z, skip_zc, skip_y, skip_yc], [skip_x, skip_xc, skip_xy, skip_xyc]])
    )
    hidden1, act1 = mark(
        mm_norm(
            ids, act0, skip_full, 0, NN, True, skip_bias, norm1_gain, norm1_beta + shift, None
        )
    )
    qkv_y, qkv_x = pin((qkv_y, qkv_x))
    qkv_zc, qkv_yc, qkv_xc = over_core(gate(qkv_z)), over_core(qkv_y), over_core(qkv_x)
    qkv_xy = over_y(qkv_x)
    mix_z, qkv_zc, qkv_yc, qkv_xc = pin((mix_z, qkv_zc, qkv_yc, qkv_xc))
    mix_x, text_z = over_x(mix_z), all_z(gate(text_piece))
    qkv_xy = pin(qkv_xy)
    qkv_xyc, mix_y = over_core(qkv_xy), over_y(gate(mix_z))
    qkv_xyc, text_z = pin((qkv_xyc, text_z))
    fc1_z = all_z(gate(fc1_weight[None]))
    mix_zc = over_core(gate(mix_z))
    qkv_full = mark(
        assemble(ids, [[qkv_z, qkv_zc, qkv_y, qkv_yc], [qkv_x, qkv_xc, qkv_xy, qkv_xyc]])
    )

    qkv_kinds = (ROPE, ROPE, CAST)
    *qkv_norms, q_low, kv_low = mark(
        mm_heads(act1, qkv_full, 0, qkv_kinds, biases[:3], qk_gain, qk_beta, tabs, spreads)
    )
    mix_x, mix_y, mix_zc, fc1_z = pin((mix_x, mix_y, mix_zc, fc1_z))
    kv_in, mix_xy, text_y = over_core(gate(kv_low)), over_x(mix_y), over_y(gate(text_z))
    fc2_z = all_z(gate(fc2_piece))
    kv_in = pin(kv_in)
    mix_xc, mix_yc = over_core(gate(mix_x)), over_core(gate(mix_y))
    att, lse = mark(att_forward(gate(q_low), [kv_low, kv_in], kv_low.shape[1]))
    text_y, mix_xc, mix_yc, mix_xy = pin((text_y, mix_xc, mix_yc, mix_xy))
    fc1_y, text_x = over_y(gate(fc1_z)), over_x(gate(text_z))
    mix_xyc, text_zc, text_yc = over_core(mix_xy), over_core(gate(text_z)), over_core(text_y)
    mix_xyc, text_zc, text_yc = pin((mix_xyc, text_zc, text_yc))
    mix_full = mark(
        assemble(ids, [[mix_z, mix_zc, mix_y, mix_yc], [mix_x, mix_xc, mix_xy, mix_xyc]])
    )
    hidden2, act3 = mark(
        mm_norm(
            ids, gate(att), mix_full, 0, NT, False, proj_bias, norm3_gain, norm3_beta, hidden1
        )
    )
    text_x = pin(text_x)
    text_xy, text_xc = over_x(gate(text_y)), over_core(text_x)
    fc1_zc = over_core(gate(fc1_z))

    t_kinds = (NORM, CAST)
    *cq_norms, cq = mark(
        mm_heads(
            gate(act3), mix_full, 1, (ROPE,), biases[3:4], cq_gain, cq_beta, tabs, spreads
        )
    )
    text_xy, text_xc, fc1_zc, fc2_z, fc1_y = pin((text_xy, text_xc, fc1_zc, fc2_z, fc1_y))
    fc2_y, out_in, text_xyc = over_y(fc2_z), over_x(gate(out_low)), over_core(text_xy)
    fc1_yc, fc2_zc = over_core(fc1_y), over_core(fc2_z)
    text_xyc, fc1_yc, fc2_zc = pin((text_xyc, fc1_yc, fc2_zc))
    text_full = mark(
        assemble(
            ids, [[gate(text_z), text_zc, text_y, text_yc], [text_x, text_xc, text_xy, text_xyc]]
        )
    )
    *t_norms, tk, tv = mark(
        mm_heads(
            text, text_full, 0, t_kinds, biases[4:], ck_gain, jnp.zeros_like(ck_gain), no_tabs, spreads
        )
    )
    act1_cp, act0_cp, att_cp = over_core(gate(act1)), over_core(gate(act0)), over_core(gate(att[0]))
    tkv = jnp.concatenate([tk[None], tv])
    fc1_full = mark(assemble(ids, [[gate(fc1_z), fc1_zc, fc1_y, fc1_yc]]))
    catt, clse = mark(att_forward(gate(cq), [tkv], text_used))
    hidden3, act2 = mark(
        mm_norm(
            ids, gate(catt), mix_full, 2, NT, False, cross_proj_bias, norm2_gain, norm2_beta, hidden2
        )
    )

    act1_cp, act0_cp, att_cp, out_in, fc2_y = pin((act1_cp, act0_cp, att_cp, out_in, fc2_y))
    act2_in, act2_cp, fc2_yc = over_x(act2), over_core(gate(act2)), over_core(fc2_y)
    act3_cp = over_core(gate(act3))
    gm_own = jnp.concatenate([mine(out_low), mine(out_in)])
    gm_oth = jnp.concatenate([other(out_in), other(out_low)])
    fc2_bias_grad = bias_total(gm_own)
    post_own, slope_own = mark(ff_up(gate(act2), fc1_full, fc1_bias[None]))
    act2_cp, act3_cp, fc2_yc = pin((act2_cp, act3_cp, fc2_yc))
    post_own_cp, gm_own_cp, gm_oth_cp, catt_cp = (
        over_core(gate(v)) for v in (post_own, gm_own, gm_oth, catt[0])
    )
    fc2_full = mark(assemble(ids, [[gate(fc2_z), fc2_zc, fc2_y, fc2_yc]]))
    down_own = mark(ff_down(gate(post_own), fc2_full, F32))
    post_own_cp, gm_own_cp, gm_oth_cp, catt_cp, act2_in = pin(
        (post_own_cp, gm_own_cp, gm_oth_cp, catt_cp, act2_in)
    )
    act2_in_cp = over_core(act2_in)
    post_oth, slope_oth = mark(ff_up(act2_in, fc1_full, fc1_bias[None]))
    post_oth_cp = over_core(gate(post_oth))

    both = ("z", CORE)
    far_pair = [
        (2 * zz + cc, 2 * (zz ^ 2) + cc) for zz in range(4) for cc in range(2) if zz // 2 != cc
    ]
    in_pair = [
        (2 * zz + cc, 2 * (zz ^ 1) + cc) for zz in range(4) for cc in range(2) if zz // 2 == cc
    ]
    hand = [(2 * zz + zz // 2, 2 * zz + 1 - zz // 2) for zz in range(4)]

    def z_first(total):
        total = total.astype(BF)
        return total, lax.ppermute(total, both, far_pair)

    def z_second(held, r):
        total, got = held
        n, _, w = total.shape
        blocks = (total.astype(F32) + got.astype(F32)).astype(BF).reshape(n, 2, 2 * r, w)
        same = lax.dynamic_index_in_dim(blocks, z & 1, 1, False)
        flip = lax.dynamic_index_in_dim(blocks, 1 - (z & 1), 1, False)
        return same, lax.ppermute(flip, both, in_pair)

    def z_third(held, r):
        same, got = held
        n, _, w = same.shape
        done = (same.astype(F32) + got.astype(F32)).reshape(n, 2, r, w)
        keep = lax.dynamic_index_in_dim(done, core, 1, False)
        give = lax.dynamic_index_in_dim(done, 1 - core, 1, False).astype(BF)
        return keep, lax.ppermute(give, both, hand)

    def land(held):
        return jnp.where(z // 2 == core, held[0], held[1].astype(F32))

    g_pre_oth, fc1_sum_oth = mark(ff_up_grad(gate(gm_oth), fc2_full, slope_oth))
    g_oth_cp = over_core(g_pre_oth)
    up_oth = mark(ff_down(gate(g_pre_oth), fc1_full, BF))
    post_oth_cp, g_oth_cp, act2_in_cp = pin((post_oth_cp, g_oth_cp, act2_in_cp))
    up_in = over_x(up_oth)
    g_pre_own, fc1_sum_own = mark(ff_up_grad(gate(gm_own), fc2_full, slope_own))
    g_own_cp = over_core(g_pre_own)
    fc2_near, fc2_far = mark(
        ff_wgrad(
            ids,
            [gm_own, gm_own_cp, gm_oth, gm_oth_cp],
            [gate(post_own), post_own_cp, post_oth, post_oth_cp],
        )
    )
    fc2_in = over_y(fc2_far)
    up_own = mark(ff_down(gate(g_pre_own), fc1_full, F32))
    fc1_bias_grad = (fc1_sum_own + fc1_sum_oth)[0]
    g_own_cp = pin(g_own_cp)
    fc1_near, fc1_far = mark(
        ff_wgrad(
            ids,
            [gate(act2), act2_cp, act2_in, act2_in_cp],
            [g_pre_own, g_own_cp, g_pre_oth, g_oth_cp],
        )
    )
    fc1_in = over_y(fc1_far)
    up_in = pin(up_in)
    out_full = jnp.concatenate([mine(out_grad), mine(out_in).astype(F32)])
    grad3, gc, sums2 = mark(norm_grad(gate(up_own), up_in, hidden3, out_full, norm2_gain))
    gc_cp = over_core(gc)
    dc = mark(mm_nn(gate(gc), mix_full, 2))

    gc_cp, fc2_in = pin((gc_cp, fc2_in))
    fc2_held = z_first((fc2_near.astype(F32) + fc2_in.astype(F32))[None])
    mark(fc2_held[0])
    dcq, dtkv = mark(att_backward(cq, gate(dc), clse, [tkv], [BF], text_used))
    dtkv_in = over_core(dtkv)
    cproj_keep, cproj_send = mark(
        wgrad(
            ids,
            [gate(gc), gc_cp, catt, catt_cp],
            ((((0, (2, 0)), (1, (3, None))), ((0, 0), (0, 1), (1, 0), (1, 1))),),
            [(2, D // 4, width)] * 2,
        )
    )
    cproj_in = over_x(cproj_send)
    g_cq, cq_sums = mark(
        heads_grad(
            cq_norms, (ROPE,), (((0, None),),), [gate(dcq)], cq_gain, tabs, spreads, 128
        )
    )
    g_cq_cp = over_core(g_cq)
    grad2, ga, sums3 = mark(
        mm_norm_grad(ids, gate(g_cq), mix_full, 1, hidden2, grad3, norm3_gain, False)
    )
    ga_cp = over_core(gate(ga))
    dtkv_in, g_cq_cp, fc2_held, fc1_in = pin((dtkv_in, g_cq_cp, fc2_held, fc1_in))
    fc2_held = z_second(fc2_held, block)
    mark(fc2_held[0])
    fc1_held = z_first((fc1_near.astype(F32) + fc1_in.astype(F32))[None])
    mark(fc1_held[0])
    g_text, text_sums = mark(
        heads_grad(
            t_norms,
            t_kinds,
            (((0, 0), (1, 0)), ((0, 1), (1, 1))),
            [gate(dtkv), dtkv_in],
            ck_gain,
            no_tabs,
            spreads,
            text.shape[0],
        )
    )
    text_near, text_far = mark(
        wgrad(
            ids,
            [text, gate(g_text)],
            (
                (((0, (1, 0)),), ((0, 0), (1, 0), (0, 2), (1, 2))),
                (((0, (1, 1)),), ((0, 1), (1, 1), (0, 3), (1, 3))),
            ),
            [(4, DT // 4, width)] * 2,
        )
    )
    text_in_y = over_y(text_far.reshape(16, text_block, width))
    text_part = mark(mm_nt(gate(g_text), text_full))[:text_used]
    fc2_held, cproj_in, ga_cp = pin((fc2_held, cproj_in, ga_cp))
    fc2_held = z_third(fc2_held, block)
    text_in = over_x(text_part.astype(BF))
    cproj_sum = cproj_keep.astype(F32) + cproj_in.astype(F32)
    cproj_in_y = over_y(cproj_sum[1:].astype(BF))

    pair_keep, pair_send = mark(
        wgrad(
            ids,
            [gate(ga), ga_cp, act3, act3_cp, att, att_cp, g_cq, g_cq_cp],
            (
                (((0, (4, 0)), (1, (5, None))), ((0, 0), (0, 2), (1, 0), (1, 2))),
                (((2, (6, 0)), (3, (7, 0))), ((0, 1), (0, 3), (1, 1), (1, 3))),
            ),
            [(4, D // 4, width)] * 2,
        )
    )
    pair_in = over_x(pair_send)
    da = mark(mm_nn(gate(ga), mix_full, 0))
    fc2_held, text_in, text_in_y = pin((fc2_held, text_in, text_in_y))
    text_total = text_near.astype(F32) + text_in_y.reshape(text_near.shape).astype(F32)
    text_in_x = over_x(text_total[2:].astype(BF).reshape(8, text_block, width))
    dq, dkv, dkv_give = mark(
        att_backward(q_low, gate(da), lse, [kv_low, kv_in], [F32, BF], kv_low.shape[1])
    )
    pair_in = pin(pair_in)
    dkv_in = over_core(gate(dkv_give))

    down_oth = mark(ff_down(gate(post_oth), fc2_full, F32))
    down_own = down_own + hidden3 + fc2_bias
    down_send = mark(jnp.stack([down_own[part:], down_oth[:part]]).astype(BF))
    dkv_in, fc1_held, cproj_in_y = pin((dkv_in, fc1_held, cproj_in_y))
    pair_total = pair_keep.astype(F32) + pair_in.astype(F32)
    pair_in_y, down_in = over_y(pair_total[2:].astype(BF)), over_x(down_send)
    fc1_held = z_second(fc1_held, block)
    cproj_held = z_first(cproj_sum[:1] + cproj_in_y.astype(F32))
    g_qkv, qkv_sums = mark(
        heads_grad(
            qkv_norms,
            qkv_kinds,
            (((0, None),), ((1, 0), (2, 0)), ((1, 1), (2, 1))),
            [gate(dq), dkv, dkv_in],
            qk_gain,
            tabs,
            spreads,
            128,
        )
    )
    g_qkv_cp = over_core(g_qkv)
    text_in_x, cproj_held, fc1_held = pin((text_in_x, cproj_held, fc1_held))
    text_held = z_first(text_total[:2] + text_in_x.reshape(2, DT // 4, width).astype(F32))
    cproj_held, fc1_held = z_second(cproj_held, block), z_third(fc1_held, block)
    grad1, gs, sums1, gs_turned = mark(
        mm_norm_grad(ids, gate(g_qkv), qkv_full, 0, hidden1, grad2, norm1_gain, True)
    )
    g_qkv_cp, pair_in_y, text_held, cproj_held, fc1_held = pin(
        (g_qkv_cp, pair_in_y, text_held, cproj_held, fc1_held)
    )
    gs_cp = over_core(gate(gs_turned))
    pair_held = z_first(pair_total[:2] + pair_in_y.astype(F32))
    text_held, cproj_held = z_second(text_held, text_block), z_third(cproj_held, block)

    def one(k, places):
        return (((0, (2, k)), (1, (3, k))), places)

    q_near, q_far, k_near, k_far = mark(
        wgrad(
            ids,
            [gate(act1), act1_cp, g_qkv, g_qkv_cp],
            (
                one(0, ((0, 0), (1, 0), (0, 1), (1, 1))),
                one(1, ((2, 0), (3, 0), (2, 1), (3, 1))),
            ),
            [(2, D // 4, width)] * 4,
        )
    )
    gs_cp, pair_held, text_held, cproj_held = pin((gs_cp, pair_held, text_held, cproj_held))
    q_in, k_in = over_y(q_far), over_y(gate(k_far))
    pair_held, text_held = z_second(pair_held, block), z_third(text_held, text_block)
    v_near, v_far = mark(
        wgrad(
            ids,
            [gate(act1), act1_cp, g_qkv, g_qkv_cp],
            (one(2, ((0, 0), (1, 0), (0, 1), (1, 1))),),
            [(2, D // 4, width)] * 2,
        )
    )

    lat_keep, lat_send, skp_near, skp_far = mark(
        wgrad(
            ids,
            [gate(act0[0]), act0_cp[0], act0[1], act0_cp[1], gs_turned, gs_cp],
            (
                (((0, (4, None)), (1, (5, None))), ((0, 0), (0, 1), (1, 0), (1, 1))),
                (((2, (4, None)), (3, (5, None))), ((2, 0), (3, 0), (2, 1), (3, 1))),
            ),
            [(2, D // 4, width)] * 4,
        )
    )
    lat_in = over_x(lat_send)
    d_lat, d_skp, sums0 = mark(norm0_grad(gate(gs_turned), skip_full, lat, skp, norm0_gain))
    d_send = mark(jnp.stack([d_lat[part:], d_skp[part:]]).astype(BF))

    def fold(v):
        return jnp.sum(v.reshape(-1, heads, HD), axis=(0, 1))

    share = 0.5
    small_shapes = []

    def small_sums():
        wide = jnp.concatenate([fc1_bias_grad, jnp.zeros_like(fc1_bias_grad)])
        rows = (jnp.arange(16) == image).astype(F32)
        parts = [
            natural(wide),
            fc2_bias_grad,
            sums2[0],
            sums2[1],
            sums2[2],
            sums3[0],
            sums3[1],
            natural(cq_sums[2, 0]),
            natural(text_sums[2]) * share,
            fold(cq_sums[0]),
            fold(cq_sums[1]),
            fold(text_sums[0, 0]) * share,
            sums3[2],
            sums1[0],
            sums1[1],
            sums1[2],
            natural(qkv_sums[2]),
            fold(qkv_sums[0, 0]),
            fold(qkv_sums[1, 0]),
            fold(qkv_sums[0, 1]),
            fold(qkv_sums[1, 1]),
            rows[:, None] * sums1[1][None],
            sums0[:2],
            sums0[2:],
        ]
        small_shapes.extend(p.shape for p in parts)
        flat = jnp.concatenate([p.reshape(-1) for p in parts])
        pad = -flat.shape[0] % 1024
        return jnp.concatenate([flat, jnp.zeros((pad,), F32)]).reshape(-1, LANES)

    def first_half(keep, got):
        total = keep.astype(F32) + got.astype(F32)
        return total[:1], total[1:].astype(BF)

    def second_half(total, got):
        return total + got.astype(F32)

    pair_held, text_held, down_in, q_in = pin((pair_held, text_held, down_in, q_in))
    q_sum, q_give = first_half(q_near, q_in)
    q_in, v_in = over_x(gate(q_give)), over_y(gate(v_far))
    pair_held = z_third(pair_held, block)
    small = mark(small_sums())
    small_in = over_core(small)
    lat_in, small_in, pair_held = pin((lat_in, small_in, pair_held))
    small = small + small_in
    d_in, small_in = over_x(gate(d_send)), over_z(small, 1)
    lat_sum, lat_give = first_half(lat_keep, lat_in)
    k_in, small_in = pin((k_in, small_in))
    small = small + small_in
    k_sum, k_give = first_half(k_near, k_in)
    skp_in, small_in = over_y(gate(skp_far)), over_z(small, 2)
    q_in, small_in = pin((q_in, small_in))
    small = small + small_in
    k_in = over_x(gate(k_give))
    q_held = z_first(second_half(q_sum, q_in))
    v_in = pin(v_in)
    v_sum, v_give = first_half(v_near, v_in)
    lat_in, small_in = over_y(gate(lat_give)), over_y(gate(small))
    q_held, d_in = pin((q_held, d_in))
    v_in, q_held = over_x(gate(v_give)), z_second(q_held, block)
    k_in = pin(k_in)
    k_held = z_first(second_half(k_sum, k_in))
    q_held, skp_in = pin((q_held, skp_in))
    skp_sum, skp_give = first_half(skp_near, skp_in)
    skp_in, q_held = over_x(gate(skp_give)), z_third(q_held, block)
    lat_in, small_in, k_held = pin((lat_in, small_in, k_held))
    small = small + small_in
    small_in, k_held = over_x(small), z_second(k_held, block)
    v_in = pin(v_in)
    v_held = z_first(
        jnp.concatenate([second_half(v_sum, v_in), second_half(lat_sum, lat_in)])
    )
    k_held, skp_in, q_held = pin((k_held, skp_in, q_held))
    k_held = z_third(k_held, block)
    skp_held = z_first(second_half(skp_sum, skp_in))
    v_held, small_in = pin((v_held, small_in))
    small = small + small_in
    v_held = z_second(v_held, block)
    skp_held = z_second(pin(skp_held), block)
    v_held = z_third(pin(v_held), block)
    skp_held = z_third(pin(skp_held), block)
    v_lat, skip_b = land(v_held), land(skp_held)
    skip_grad = jnp.concatenate([v_lat[1:], skip_b])
    qkv_grad = jnp.swapaxes(jnp.concatenate([land(q_held), land(k_held), v_lat[:1]]), 0, 1)
    fc2_grad, fc1_grad = land(fc2_held)[0].T, land(fc1_held)[0]
    cproj_grad, pair_grad = land(cproj_held), land(pair_held)
    cross_kv_grad = jnp.swapaxes(land(text_held), 0, 1)

    out_mine = (down_own[:part] + down_in[1].astype(F32)).astype(BF)
    out_other = (down_oth[part:] + down_in[0].astype(F32)).astype(BF)
    output = by_rank(out_mine, out_other)
    text_grad = by_rank(text_part, text_in.astype(F32))
    grad_latents = by_rank(d_lat[:part], d_in[0].astype(F32))
    grad_skip = by_rank(d_skp[:part], d_in[1].astype(F32))

    flat, at, sums = small.reshape(-1), 0, []
    for shape in small_shapes:
        size = functools.reduce(lambda p, q: p * q, shape)
        sums.append(flat[at : at + size].reshape(shape))
        at += size
    early, middle, late = sums[:13], sums[13:22], sums[22:]
    mod_grad = lax.dot_general(
        silu_rows.astype(F32),
        middle[8],
        ROWS_CONTRACT,
        precision=lax.Precision.HIGHEST,
        preferred_element_type=F32,
    )

    def narrow(a):
        return mine(a.reshape(a.shape[:-1] + (2, -1)), a.ndim - 1)

    return (
        output,
        grad_latents,
        grad_skip,
        text_grad,
        late[0],
        late[1],
        skip_grad,
        middle[2],
        mod_grad,
        middle[1],
        middle[0],
        middle[1],
        qkv_grad,
        narrow(middle[3]),
        middle[4],
        middle[5],
        middle[6],
        middle[7],
        pair_grad[0].T,
        early[12],
        early[5],
        early[6],
        pair_grad[1],
        narrow(early[7]),
        cross_kv_grad,
        narrow(early[8]),
        early[9],
        early[10],
        early[11],
        cproj_grad[0].T,
        early[4],
        early[2],
        early[3],
        fc1_grad,
        narrow(early[0]),
        fc2_grad,
        early[1],
    )


def is_spec(spec):
    return isinstance(spec, P)


def split_dp(spec):
    parts = []
    for entry in spec:
        names = entry if isinstance(entry, tuple) else (entry,)
        names = sum((("z", "y") if n == DP else (n,) for n in names), ())
        parts.append(names if len(names) > 1 else names[0])
    return P(*parts)


def solution(mesh):
    in_specs = (
        P(DP, (CORE, RANK), None),
        P(DP, (CORE, RANK), None),
        P(DP, None, None),
        P(DP, None),
        P(DP, CORE, None),
        P(DP, (CORE, RANK), None),
        P(),
        P(),
        P(None, (DP, CORE), RANK),
        P(),
        P((DP, CORE), None),
        P(),
        P(),
        P(),
        P((DP, CORE), None, RANK),
        P(None, RANK),
        P(),
        P(),
        P(),
        P(),
        P(RANK, (DP, CORE)),
        P(),
        P(),
        P(),
        P((DP, CORE), RANK),
        P(RANK),
        P((DP, CORE), None, RANK),
        P(None, RANK),
        P(),
        P(),
        P(),
        P(RANK, (DP, CORE)),
        P(),
        P(),
        P(),
        P((DP, CORE), RANK),
        P(RANK),
        P(RANK, (DP, CORE)),
        P(),
    )
    out_specs = (
        P(DP, (CORE, RANK), None),
        P(DP, (CORE, RANK), None),
        P(DP, (CORE, RANK), None),
        P(DP, None, None),
        P(),
        P(),
        P(None, (DP, CORE), RANK),
        P(),
        P((DP, CORE), None),
        P(),
        P(),
        P(),
        P((DP, CORE), None, RANK),
        P(None, RANK),
        P(),
        P(),
        P(),
        P(),
        P(RANK, (DP, CORE)),
        P(),
        P(),
        P(),
        P((DP, CORE), RANK),
        P(RANK),
        P((DP, CORE), None, RANK),
        P(None, RANK),
        P(),
        P(),
        P(),
        P(RANK, (DP, CORE)),
        P(),
        P(),
        P(),
        P((DP, CORE), RANK),
        P(RANK),
        P(RANK, (DP, CORE)),
        P(),
    )
    program = on_device
    sizes = dict(mesh.shape)
    if (sizes[DP], sizes[CORE], sizes[RANK]) == (8, 2, 2):
        program = one_image_per_chip
        mesh = Mesh(mesh.devices.reshape(4, 2, 2, 2), GRID_AXES)
        in_specs = jax.tree.map(split_dp, in_specs, is_leaf=is_spec)
        out_specs = jax.tree.map(split_dp, out_specs, is_leaf=is_spec)
    return jax.shard_map(
        program, mesh=mesh, in_specs=in_specs, out_specs=out_specs, check_vma=False
    )
```

```python
import functools

import jax
import jax.numpy as jnp
from jax import lax
from jax.experimental import pallas as pl
from jax.experimental.pallas import tpu as pltpu
from jax.sharding import Mesh
from jax.sharding import PartitionSpec as P

DP, CORE, RANK = "dp", "context", "tensor"

D = 1408
HD = 88
FF = 6144
DT = 1024


EPS = 1e-06
ROWS_CONTRACT = (((0,), (0,)), ((), ()))
COLS_CONTRACT = (((1,), (1,)), ((), ()))


def spread(values):
    return lax.all_gather(values, RANK, axis=1, tiled=True)


def collect(values):
    return lax.psum_scatter(values, RANK, scatter_dimension=1, tiled=True)


def weight_grad(activations, gradients):
    return lax.dot_general(
        activations, gradients, ROWS_CONTRACT, preferred_element_type=jnp.float32
    )


def input_grad(gradients, weight_mat):
    return lax.dot_general(gradients, weight_mat, COLS_CONTRACT, preferred_element_type=jnp.float32)


def norm_forward(values, norm_gain, norm_beta):
    centered = values - jnp.mean(values, axis=-1, keepdims=True)
    inv_std = lax.rsqrt(jnp.mean(centered * centered, axis=-1, keepdims=True) + EPS)
    normed = centered * inv_std
    return (normed * norm_gain + norm_beta, normed, inv_std)


def norm_backward(upstream, normed, inv_std, norm_gain):
    scaled = upstream * norm_gain
    inner_term = (
        scaled
        - jnp.mean(scaled, axis=-1, keepdims=True)
        - normed * jnp.mean(scaled * normed, axis=-1, keepdims=True)
    )
    lead_axes = tuple(range(upstream.ndim - 1))
    return (
        inv_std * inner_term,
        jnp.sum(upstream * normed, axis=lead_axes),
        jnp.sum(upstream, axis=lead_axes),
    )


def rope_angles(positions):
    quarter = HD // 4
    frequency = 10000.0 ** (-2.0 * jnp.arange(quarter, dtype=jnp.float32) / (HD // 2))
    places = positions.astype(jnp.float32)
    return jnp.concatenate([places[..., 0:1] * frequency, places[..., 1:2] * frequency], axis=-1)


def rotate(values, angles, direction):
    full_shape = values.shape
    paired = values.reshape(full_shape[:-1] + (HD // 2, 2))
    cos_part = jnp.cos(angles)[..., None, :]
    sin_part = jnp.sin(angles)[..., None, :] * direction
    former = paired[..., 0]
    latter = paired[..., 1]
    turned = jnp.stack(
        [former * cos_part - latter * sin_part, former * sin_part + latter * cos_part], axis=-1
    )
    return turned.reshape(full_shape)


def attend_forward(query_img, key_img, value_img):
    scores = jnp.einsum(
        "qhd,khd->hqk", query_img, key_img, preferred_element_type=jnp.float32
    ) * HD ** (-0.5)
    row_peak = jnp.max(scores, axis=-1, keepdims=True)
    exponent = jnp.exp(scores - row_peak)
    row_total = jnp.sum(exponent, axis=-1, keepdims=True)
    weights_low = (exponent / row_total).astype(jnp.bfloat16)
    result = jnp.einsum("hqk,khd->qhd", weights_low, value_img, preferred_element_type=jnp.float32)
    return (result, row_peak[..., 0] + jnp.log(row_total[..., 0]))


def attend_backward(query_img, key_img, value_img, logsum, grad_img):
    scores = jnp.einsum(
        "qhd,khd->hqk", query_img, key_img, preferred_element_type=jnp.float32
    ) * HD ** (-0.5)
    probs_full = jnp.exp(scores - logsum[..., None])
    grad_probs = jnp.einsum("qhd,khd->hqk", grad_img, value_img, preferred_element_type=jnp.float32)
    delta_row = jnp.sum(probs_full * grad_probs, axis=-1, keepdims=True)
    grad_scores = (probs_full * (grad_probs - delta_row)).astype(jnp.bfloat16)
    grad_query = jnp.einsum(
        "hqk,khd->qhd", grad_scores, key_img, preferred_element_type=jnp.float32
    ) * HD ** (-0.5)
    grad_key = jnp.einsum(
        "hqk,qhd->khd", grad_scores, query_img, preferred_element_type=jnp.float32
    ) * HD ** (-0.5)
    grad_value = jnp.einsum(
        "hqk,qhd->khd",
        probs_full.astype(jnp.bfloat16),
        grad_img,
        preferred_element_type=jnp.float32,
    )
    return (grad_query, grad_key, grad_value)


def bias_total(gradients):
    return jnp.sum(gradients.astype(jnp.float32).reshape(-1, gradients.shape[-1]), axis=0)


def on_device(
    latents,
    skip_states,
    text_states,
    time_vector,
    grid_pos,
    out_grad,
    norm0_gain,
    norm0_beta,
    skip_weight,
    skip_bias,
    mod_weight,
    mod_bias,
    norm1_gain,
    norm1_beta,
    qkv_weight,
    qkv_bias,
    qnorm_gain,
    qnorm_beta,
    knorm_gain,
    knorm_beta,
    proj_weight,
    proj_bias,
    norm3_gain,
    norm3_beta,
    cross_q_weight,
    cross_q_bias,
    cross_kv_weight,
    cross_kv_bias,
    cqnorm_gain,
    cqnorm_beta,
    cknorm_gain,
    cross_proj_weight,
    cross_proj_bias,
    norm2_gain,
    norm2_beta,
    fc1_weight,
    fc1_bias,
    fc2_weight,
    fc2_bias,
):
    context_count = lax.axis_size(CORE)
    tensor_rank = lax.axis_index(RANK)
    gathered = (
        lax.all_gather(skip_weight, (DP, CORE), axis=1, tiled=True),
        lax.all_gather(mod_weight, (DP, CORE), axis=0, tiled=True),
        lax.all_gather(qkv_weight, (DP, CORE), axis=0, tiled=True),
        lax.all_gather(proj_weight, (DP, CORE), axis=1, tiled=True),
        lax.all_gather(cross_q_weight, (DP, CORE), axis=0, tiled=True),
        lax.all_gather(cross_kv_weight, (DP, CORE), axis=0, tiled=True),
        lax.all_gather(cross_proj_weight, (DP, CORE), axis=1, tiled=True),
        lax.all_gather(fc1_weight, (DP, CORE), axis=0, tiled=True),
        lax.all_gather(fc2_weight, (DP, CORE), axis=1, tiled=True),
    )
    (
        skip_full,
        mod_full,
        qkv_full,
        proj_full,
        crossq_full,
        crosskv_full,
        crossproj_full,
        fc1_full,
        fc2_full,
    ) = gathered
    local_width = qkv_full.shape[2]
    heads_local = local_width // HD
    images = latents.shape[0]
    group_rows = grid_pos.shape[1]
    text_rows = text_states.shape[1]
    flat_rows = images * group_rows
    angles = rope_angles(grid_pos)
    joined = jnp.concatenate(
        [latents.astype(jnp.float32), skip_states.astype(jnp.float32)], axis=-1
    )
    skip_normed, skip_unit, skip_inv = norm_forward(
        joined, norm0_gain.reshape(-1), norm0_beta.reshape(-1)
    )
    skip_act = spread(skip_normed.astype(jnp.bfloat16)).reshape(flat_rows, 2 * D)
    skip_cols = jnp.dot(
        skip_act, skip_full.reshape(2 * D, local_width), preferred_element_type=jnp.float32
    )
    hidden1 = (
        lax.all_to_all(
            skip_cols.reshape(images, group_rows, local_width),
            RANK,
            split_axis=1,
            concat_axis=2,
            tiled=True,
        )
        + skip_bias
    )
    silu_low = jax.nn.silu(time_vector).astype(jnp.bfloat16)
    shift = jnp.dot(silu_low, mod_full, preferred_element_type=jnp.float32) + mod_bias
    norm1_out, unit_one, inv_one = norm_forward(hidden1, norm1_gain, norm1_beta)
    attn_act = spread((norm1_out + shift[:, None, :]).astype(jnp.bfloat16)).reshape(flat_rows, D)
    merged = jnp.dot(
        attn_act, qkv_full.reshape(D, 3 * local_width), preferred_element_type=jnp.float32
    ) + qkv_bias.reshape(-1)
    merged = merged.reshape(images, group_rows, 3, heads_local, HD)
    query_norm, query_unit, query_inv = norm_forward(merged[:, :, 0], qnorm_gain, qnorm_beta)
    key_norm, key_unit, key_inv = norm_forward(merged[:, :, 1], knorm_gain, knorm_beta)
    queries = rotate(query_norm, angles, 1.0).astype(jnp.bfloat16)
    keys_low = rotate(key_norm, angles, 1.0).astype(jnp.bfloat16)
    values_low = merged[:, :, 2].astype(jnp.bfloat16)
    keys_all, values_all = (
        lax.all_gather(
            keys_low.reshape(images, group_rows, local_width), CORE, axis=1, tiled=True
        ),
        lax.all_gather(
            values_low.reshape(images, group_rows, local_width), CORE, axis=1, tiled=True
        ),
    )
    keys_all = keys_all.reshape(images, -1, heads_local, HD)
    values_all = values_all.reshape(images, -1, heads_local, HD)
    attn_out, attn_lse = lax.map(
        lambda packed: attend_forward(*packed), (queries, keys_all, values_all)
    )
    attn_low = attn_out.reshape(flat_rows, local_width).astype(jnp.bfloat16)
    hidden2 = (
        hidden1
        + collect(
            jnp.dot(attn_low, proj_full, preferred_element_type=jnp.float32).reshape(
                images, group_rows, D
            )
        )
        + proj_bias
    )
    norm3_out, unit_three, inv_three = norm_forward(hidden2, norm3_gain, norm3_beta)
    cross_act = spread(norm3_out.astype(jnp.bfloat16)).reshape(flat_rows, D)
    cross_raw = (
        jnp.dot(cross_act, crossq_full, preferred_element_type=jnp.float32) + cross_q_bias
    ).reshape(images, group_rows, heads_local, HD)
    cquery_norm, cquery_unit, cquery_inv = norm_forward(cross_raw, cqnorm_gain, cqnorm_beta)
    cross_queries = rotate(cquery_norm, angles, 1.0).astype(jnp.bfloat16)
    text_low = text_states.reshape(images * text_rows, DT)
    text_kv = jnp.dot(
        text_low, crosskv_full.reshape(DT, 2 * local_width), preferred_element_type=jnp.float32
    ) + cross_kv_bias.reshape(-1)
    text_kv = text_kv.reshape(images, text_rows, 2, heads_local, HD)
    ckey_norm, ckey_unit, ckey_inv = norm_forward(text_kv[:, :, 0], cknorm_gain, 0.0)
    cross_keys = ckey_norm.astype(jnp.bfloat16)
    cross_values = text_kv[:, :, 1].astype(jnp.bfloat16)
    cross_out, cross_lse = lax.map(
        lambda packed: attend_forward(*packed), (cross_queries, cross_keys, cross_values)
    )
    cross_low = cross_out.reshape(flat_rows, local_width).astype(jnp.bfloat16)
    hidden3 = (
        hidden2
        + collect(
            jnp.dot(cross_low, crossproj_full, preferred_element_type=jnp.float32).reshape(
                images, group_rows, D
            )
        )
        + cross_proj_bias
    )
    norm2_out, unit_two, inv_two = norm_forward(hidden3, norm2_gain, norm2_beta)
    mlp_act = spread(norm2_out.astype(jnp.bfloat16)).reshape(flat_rows, D)
    pre_act = jnp.dot(mlp_act, fc1_full, preferred_element_type=jnp.float32) + fc1_bias
    post_low = jax.nn.gelu(pre_act, approximate=True).astype(jnp.bfloat16)
    output = (
        hidden3
        + collect(
            jnp.dot(post_low, fc2_full, preferred_element_type=jnp.float32).reshape(
                images, group_rows, D
            )
        )
        + fc2_bias
    )
    out_low = out_grad.astype(jnp.bfloat16)
    fc2_bias_grad = bias_total(out_low)
    out_all = spread(out_low).reshape(flat_rows, D)
    fc2_grad = weight_grad(post_low, out_all)
    post_grad = input_grad(out_all, fc2_full)
    gelu_pull = jax.vjp(lambda inputs: jax.nn.gelu(inputs, approximate=True), pre_act)[1]
    pre_low = gelu_pull(post_grad)[0].astype(jnp.bfloat16)
    fc1_grad = weight_grad(mlp_act, pre_low)
    fc1_bias_grad = bias_total(pre_low)
    mlp_up = collect(input_grad(pre_low, fc1_full).reshape(images, group_rows, D))
    norm2_in, norm2_gain_grad, norm2_beta_grad = norm_backward(
        mlp_up, unit_two, inv_two, norm2_gain
    )
    grad_three = out_grad + norm2_in
    cross_grad_low = grad_three.astype(jnp.bfloat16)
    cross_proj_bias_grad = bias_total(cross_grad_low)
    cross_grad_all = spread(cross_grad_low).reshape(flat_rows, D)
    cross_proj_grad = weight_grad(cross_low, cross_grad_all)
    cross_o_grad = (
        input_grad(cross_grad_all, crossproj_full)
        .astype(jnp.bfloat16)
        .reshape(images, group_rows, heads_local, HD)
    )
    cq_grad, ck_grad, cv_grad = lax.map(
        lambda packed: attend_backward(*packed),
        (cross_queries, cross_keys, cross_values, cross_lse, cross_o_grad),
    )
    ck_grad, cv_grad = (
        lax.psum(ck_grad.astype(jnp.bfloat16), CORE).astype(jnp.float32),
        lax.psum(cv_grad.astype(jnp.bfloat16), CORE).astype(jnp.float32),
    )
    share = 1.0 / context_count
    ck_in, cknorm_gain_grad, cknorm_unused = norm_backward(
        ck_grad, ckey_unit, ckey_inv, cknorm_gain
    )
    text_grad_low = (
        jnp.stack([ck_in, cv_grad], axis=2)
        .reshape(images * text_rows, 2 * local_width)
        .astype(jnp.bfloat16)
    )
    cross_kv_grad = weight_grad(text_low, text_grad_low).reshape(DT, 2, local_width) * share
    cross_kv_bias_grad = bias_total(text_grad_low).reshape(2, local_width) * share
    text_part = input_grad(text_grad_low, crosskv_full.reshape(DT, 2 * local_width)).reshape(
        images, text_rows, DT
    )
    cq_raw, cqnorm_gain_grad, cqnorm_beta_grad = norm_backward(
        rotate(cq_grad, angles, -1.0), cquery_unit, cquery_inv, cqnorm_gain
    )
    cq_low = cq_raw.reshape(flat_rows, local_width).astype(jnp.bfloat16)
    cross_q_grad = weight_grad(cross_act, cq_low)
    cross_q_bias_grad = bias_total(cq_low)
    norm3_up = collect(input_grad(cq_low, crossq_full).reshape(images, group_rows, D))
    norm3_in, norm3_gain_grad, norm3_beta_grad = norm_backward(
        norm3_up, unit_three, inv_three, norm3_gain
    )
    grad_two = grad_three + norm3_in
    attn_grad_low = grad_two.astype(jnp.bfloat16)
    proj_bias_grad = bias_total(attn_grad_low)
    attn_grad_all = spread(attn_grad_low).reshape(flat_rows, D)
    proj_grad = weight_grad(attn_low, attn_grad_all)
    attn_o_grad = (
        input_grad(attn_grad_all, proj_full)
        .astype(jnp.bfloat16)
        .reshape(images, group_rows, heads_local, HD)
    )
    q_grad, k_all_grad, v_all_grad = lax.map(
        lambda packed: attend_backward(*packed),
        (queries, keys_all, values_all, attn_lse, attn_o_grad),
    )
    k_grad, v_grad = (
        lax.psum_scatter(
            k_all_grad.reshape(images, -1, local_width).astype(jnp.bfloat16),
            CORE,
            scatter_dimension=1,
            tiled=True,
        ).astype(jnp.float32),
        lax.psum_scatter(
            v_all_grad.reshape(images, -1, local_width).astype(jnp.bfloat16),
            CORE,
            scatter_dimension=1,
            tiled=True,
        ).astype(jnp.float32),
    )
    q_raw, qnorm_gain_grad, qnorm_beta_grad = norm_backward(
        rotate(q_grad, angles, -1.0), query_unit, query_inv, qnorm_gain
    )
    k_raw, knorm_gain_grad, knorm_beta_grad = norm_backward(
        rotate(k_grad.reshape(images, group_rows, heads_local, HD), angles, -1.0),
        key_unit,
        key_inv,
        knorm_gain,
    )
    merged_low = jnp.stack(
        [q_raw, k_raw, v_grad.reshape(images, group_rows, heads_local, HD)], axis=2
    )
    merged_low = merged_low.reshape(flat_rows, 3 * local_width).astype(jnp.bfloat16)
    qkv_grad = weight_grad(attn_act, merged_low).reshape(D, 3, local_width)
    qkv_bias_grad = bias_total(merged_low).reshape(3, local_width)
    norm1_up = collect(
        input_grad(merged_low, qkv_full.reshape(D, 3 * local_width)).reshape(images, group_rows, D)
    )
    shift_part = jnp.sum(norm1_up, axis=1)
    mod_bias_grad = jnp.sum(shift_part, axis=0)
    text_grad, shift_grad = (
        lax.psum(text_part.astype(jnp.bfloat16), RANK).astype(jnp.float32),
        lax.psum(shift_part.astype(jnp.bfloat16), RANK).astype(jnp.float32),
    )
    mod_grad = lax.dot_general(
        silu_low.astype(jnp.float32),
        shift_grad,
        ROWS_CONTRACT,
        precision=lax.Precision.HIGHEST,
        preferred_element_type=jnp.float32,
    )
    norm1_in, norm1_gain_grad, norm1_beta_grad = norm_backward(
        norm1_up, unit_one, inv_one, norm1_gain
    )
    grad_one = grad_two + norm1_in
    skip_grad_low = grad_one.astype(jnp.bfloat16)
    skip_bias_grad = bias_total(skip_grad_low)
    skip_cols_grad = lax.all_to_all(
        skip_grad_low, RANK, split_axis=2, concat_axis=1, tiled=True
    ).reshape(flat_rows, local_width)
    skip_grad = weight_grad(skip_act, skip_cols_grad).reshape(2, D, local_width)
    cat_up = collect(
        input_grad(skip_cols_grad, skip_full.reshape(2 * D, local_width)).reshape(
            images, group_rows, 2 * D
        )
    )
    cat_in, norm0_gain_grad, norm0_beta_grad = norm_backward(
        cat_up, skip_unit, skip_inv, norm0_gain.reshape(-1)
    )
    grad_latents = cat_in[..., :D]
    grad_skip = cat_in[..., D:]

    def widen(piece, total_width):
        blank = jnp.zeros(piece.shape[:-1] + (total_width,), jnp.float32)
        return lax.dynamic_update_slice_in_dim(
            blank, piece, tensor_rank * piece.shape[-1], piece.ndim - 1
        )

    summed = lax.psum(
        (
            norm0_gain_grad,
            norm0_beta_grad,
            skip_bias_grad,
            mod_bias_grad,
            norm1_gain_grad,
            norm1_beta_grad,
            widen(qkv_bias_grad, D),
            qnorm_gain_grad,
            qnorm_beta_grad,
            knorm_gain_grad,
            knorm_beta_grad,
            proj_bias_grad,
            norm3_gain_grad,
            norm3_beta_grad,
            widen(cross_q_bias_grad, D),
            widen(cross_kv_bias_grad, D),
            cqnorm_gain_grad,
            cqnorm_beta_grad,
            cknorm_gain_grad * share,
            cross_proj_bias_grad,
            norm2_gain_grad,
            norm2_beta_grad,
            widen(fc1_bias_grad, FF),
            fc2_bias_grad,
        ),
        (DP, CORE, RANK),
    )

    def narrow(whole, piece_width):
        return lax.dynamic_slice_in_dim(
            whole, tensor_rank * piece_width, piece_width, whole.ndim - 1
        )

    weight_sums = (
        lax.psum_scatter(
            skip_grad.astype(jnp.bfloat16), (DP, CORE), scatter_dimension=1, tiled=True
        ).astype(jnp.float32),
        lax.psum_scatter(
            mod_grad.astype(jnp.bfloat16), (DP, CORE), scatter_dimension=0, tiled=True
        ).astype(jnp.float32),
        lax.psum_scatter(
            qkv_grad.astype(jnp.bfloat16), (DP, CORE), scatter_dimension=0, tiled=True
        ).astype(jnp.float32),
        lax.psum_scatter(
            proj_grad.astype(jnp.bfloat16), (DP, CORE), scatter_dimension=1, tiled=True
        ).astype(jnp.float32),
        lax.psum_scatter(
            cross_q_grad.astype(jnp.bfloat16), (DP, CORE), scatter_dimension=0, tiled=True
        ).astype(jnp.float32),
        lax.psum_scatter(
            cross_kv_grad.astype(jnp.bfloat16), (DP, CORE), scatter_dimension=0, tiled=True
        ).astype(jnp.float32),
        lax.psum_scatter(
            cross_proj_grad.astype(jnp.bfloat16), (DP, CORE), scatter_dimension=1, tiled=True
        ).astype(jnp.float32),
        lax.psum_scatter(
            fc1_grad.astype(jnp.bfloat16), (DP, CORE), scatter_dimension=0, tiled=True
        ).astype(jnp.float32),
        lax.psum_scatter(
            fc2_grad.astype(jnp.bfloat16), (DP, CORE), scatter_dimension=1, tiled=True
        ).astype(jnp.float32),
    )
    return (
        output.astype(jnp.bfloat16),
        grad_latents,
        grad_skip,
        text_grad,
        summed[0].reshape(2, D),
        summed[1].reshape(2, D),
        weight_sums[0],
        summed[2],
        weight_sums[1],
        summed[3],
        summed[4],
        summed[5],
        weight_sums[2],
        narrow(summed[6], local_width),
        summed[7],
        summed[8],
        summed[9],
        summed[10],
        weight_sums[3],
        summed[11],
        summed[12],
        summed[13],
        weight_sums[4],
        narrow(summed[14], local_width),
        weight_sums[5],
        narrow(summed[15], local_width),
        summed[16],
        summed[17],
        summed[18],
        weight_sums[6],
        summed[19],
        summed[20],
        summed[21],
        weight_sums[7],
        narrow(summed[22], fc1_bias.shape[0]),
        weight_sums[8],
        summed[23],
    )


F32 = jnp.float32
BF = jnp.bfloat16
VMEM_BYTES = 60 << 20
NN = (((1,), (0,)), ((), ()))
NT = (((1,), (1,)), ((), ()))
TN = (((0,), (0,)), ((), ()))
GRID_AXES = ("z", "y", CORE, RANK)
SWAP = [(0, 1), (1, 0)]
GELU_C = (2.0 / 3.141592653589793) ** 0.5
LANES = 128
ROPE, NORM, CAST = 2, 1, 0


def dotf(a, b, dims):
    return lax.dot_general(a, b, dims, preferred_element_type=F32)


def call(body, **kw):
    inner = body.func if isinstance(body, functools.partial) else body
    return pl.pallas_call(
        body,
        name=inner.__name__,
        compiler_params=pltpu.CompilerParams(vmem_limit_bytes=VMEM_BYTES),
        cost_estimate=pl.CostEstimate(flops=1000, bytes_accessed=1000, transcendentals=0),
        **kw,
    )


def shaped(shape, dtype):
    return jax.ShapeDtypeStruct(shape, dtype)


def fixed(*shape):
    return pl.BlockSpec(shape, lambda *_: (0,) * len(shape))


def scalars():
    return pl.BlockSpec(memory_space=pltpu.SMEM)


def over_x(v):
    return lax.ppermute(v, RANK, SWAP)


def over_core(v):
    return lax.ppermute(v, CORE, SWAP)


def over_y(v):
    return lax.ppermute(v, "y", SWAP)


def swap_z(v):
    return lax.all_to_all(v, "z", split_axis=0, concat_axis=0, tiled=True)


def swap_zy(v):
    return lax.all_to_all(v, ("z", "y"), split_axis=0, concat_axis=0, tiled=True)


def copies(v, n):
    return jnp.broadcast_to(v[None], (n,) + v.shape)


def all_z(v):
    return swap_z(copies(v, 4))


def over_z(v, k):
    return lax.ppermute(v, "z", [(i, i ^ k) for i in range(4)])


def after(value, *deps):
    return lax.optimization_barrier((value, deps))[0]


class Order:
    def __init__(self):
        self.last = None

    def gate(self, value):
        return value if self.last is None else after(value, self.last)

    def mark(self, value):
        self.last = value
        return value

    def pin(self, value):
        return self.mark(self.gate(value))


def assemble_body(halves, ids, *refs):
    o = refs[-1]
    for half in range(halves):
        for k in range(4):
            slot = (ids[1] ^ (k >> 1)) * 2 + (ids[2] ^ (k & 1))
            piece = refs[4 * half + k][0]
            if halves == 1:
                o[:, 0, slot] = piece
            else:
                w = piece.shape[-1]
                o[:, 0, slot, :, half * w : (half + 1) * w] = piece


def assemble(ids, groups):
    _, n, r, w = groups[0][0].shape
    halves = len(groups)
    spec = pl.BlockSpec((1, n, r, w), lambda s, i: (s, 0, 0, 0))
    wide = halves * w
    out = call(
        functools.partial(assemble_body, halves),
        out_shape=shaped((n, 4, 4, r, wide), groups[0][0].dtype),
        grid_spec=pltpu.PrefetchScalarGridSpec(
            num_scalar_prefetch=1,
            grid=(4,),
            in_specs=[spec] * (4 * halves),
            out_specs=pl.BlockSpec((n, 1, 4, r, wide), lambda s, i: (0, s, 0, 0, 0)),
        ),
    )(ids, *[p for g in groups for p in g])
    return out.reshape(n, 16 * r, wide)


def row_unit(v):
    centered = v - jnp.mean(v, axis=-1, keepdims=True)
    inv = lax.rsqrt(jnp.mean(centered * centered, axis=-1, keepdims=True) + EPS)
    return centered * inv, inv


def norm0_body(lat, skp, gain, beta, o):
    a, b = lat[...].astype(F32), skp[...].astype(F32)
    n = 2.0 * a.shape[1]
    mean = (jnp.sum(a, -1, keepdims=True) + jnp.sum(b, -1, keepdims=True)) / n
    a, b = a - mean, b - mean
    var = (jnp.sum(a * a, -1, keepdims=True) + jnp.sum(b * b, -1, keepdims=True)) / n
    inv = lax.rsqrt(var + EPS)
    o[0] = (a * inv * gain[0:1, :] + beta[0:1, :]).astype(BF)
    o[1] = (b * inv * gain[1:2, :] + beta[1:2, :]).astype(BF)


def norm0(lat, skp, gain, beta, rows):
    t, w = lat.shape
    row = pl.BlockSpec((rows, w), lambda i: (i, 0))
    return call(
        norm0_body,
        grid=(t // rows,),
        in_specs=[row, row, fixed(2, w), fixed(2, w)],
        out_specs=pl.BlockSpec((2, rows, w), lambda i: (0, i, 0)),
        out_shape=shaped((2, t, w), BF),
    )(lat, skp, gain, beta)


def mm_norm_body(dims, turn, has_res, *refs):
    ids, act, w, bias, gain, beta = refs[:6]
    res = refs[6] if has_res else None
    hidden, low, acc = refs[-3:]
    s = pl.program_id(0)
    part = dotf(act[0], w[0], dims)

    @pl.when(s == 0)
    def _():
        acc[...] = part

    @pl.when(s > 0)
    def _():
        acc[...] += part

    @pl.when(s == pl.num_programs(0) - 1)
    def _():
        v = acc[...]
        if turn:
            v = pltpu.roll(v, ids[3] * (v.shape[1] // 2), 1)
        v = v + bias[...]
        if has_res:
            v = v + res[...]
        hidden[...] = v
        unit, _ = row_unit(v)
        low[...] = (unit * gain[...] + beta[...]).astype(BF)


def mm_norm(ids, act, w, first, dims, turn, bias, gain, beta, res):
    n, t, k = act.shape
    _, a, b = w.shape
    out = b if dims == NN else a
    vec = fixed(1, out)
    big = fixed(t, out)
    extra = [] if res is None else [res]
    return call(
        functools.partial(mm_norm_body, dims, turn, res is not None),
        grid=(n,),
        in_specs=[
            scalars(),
            pl.BlockSpec((1, t, k), lambda s: (s, 0, 0)),
            pl.BlockSpec((1, a, b), lambda s: (first + s, 0, 0)),
            vec,
            vec,
            vec,
        ]
        + [big] * len(extra),
        out_specs=[big, big],
        out_shape=[shaped((t, out), F32), shaped((t, out), BF)],
        scratch_shapes=[pltpu.VMEM((t, out), F32)],
    )(ids, act, w, bias[None], gain[None], beta[None], *extra)


def norm_grad_tail(up, hidden, res, gain, total, low, sums):
    unit, inv = row_unit(hidden)
    scaled = up * gain
    inner = (
        scaled
        - jnp.mean(scaled, axis=-1, keepdims=True)
        - unit * jnp.mean(scaled * unit, axis=-1, keepdims=True)
    )
    g = res + inv * inner
    total[...] = g
    rounded = g.astype(BF)
    low[...] = rounded
    sums[0:1, :] = jnp.sum(up * unit, axis=0, keepdims=True)
    sums[1:2, :] = jnp.sum(up, axis=0, keepdims=True)
    sums[2:3, :] = jnp.sum(rounded.astype(F32), axis=0, keepdims=True)
    return rounded


def norm_grad_body(up, up_in, hidden, res, gain, total, low, sums):
    norm_grad_tail(
        up[...] + up_in[...].astype(F32), hidden[...], res[...], gain[...], total, low, sums
    )


def norm_grad(up, up_in, hidden, res, gain):
    t, w = up.shape
    return call(
        norm_grad_body,
        out_shape=[shaped((t, w), F32), shaped((t, w), BF), shaped((3, w), F32)],
    )(up, up_in, hidden, res, gain[None])


def mm_norm_grad_body(turn, ids, g, w, hidden, res, gain, *refs):
    total, low, sums = refs[:3]
    acc = refs[-1]
    s = pl.program_id(0)
    part = dotf(g[0], w[0], NT)

    @pl.when(s == 0)
    def _():
        acc[...] = part

    @pl.when(s > 0)
    def _():
        acc[...] += part

    @pl.when(s == pl.num_programs(0) - 1)
    def _():
        rounded = norm_grad_tail(
            acc[...], hidden[...], res[...], gain[...], total, low, sums
        )
        if turn:
            shift = ids[3] * (rounded.shape[1] // 2)
            refs[3][...] = pltpu.roll(rounded.astype(F32), shift, 1).astype(BF)


def mm_norm_grad(ids, g, w, first, hidden, res, gain, turn):
    n, t, k = g.shape
    out = w.shape[1]
    big = fixed(t, out)
    return call(
        functools.partial(mm_norm_grad_body, turn),
        grid=(n,),
        in_specs=[
            scalars(),
            pl.BlockSpec((1, t, k), lambda s: (s, 0, 0)),
            pl.BlockSpec((1, out, k), lambda s: (first + s, 0, 0)),
            big,
            big,
            fixed(1, out),
        ],
        out_specs=[big, big, fixed(3, out)] + [big] * turn,
        out_shape=[shaped((t, out), F32), shaped((t, out), BF), shaped((3, out), F32)]
        + [shaped((t, out), BF)] * turn,
        scratch_shapes=[pltpu.VMEM((t, out), F32)],
    )(ids, g, w, hidden, res, gain[None])


def norm0_grad_body(g, w, lat, skp, gain, d_lat, d_skp, sums, ups):
    s = pl.program_id(0)
    ups[s] = dotf(g[...], w[0], NT)

    @pl.when(s == 1)
    def _():
        a, b = lat[...].astype(F32), skp[...].astype(F32)
        n = 2.0 * a.shape[1]
        mean = (jnp.sum(a, -1, keepdims=True) + jnp.sum(b, -1, keepdims=True)) / n
        a, b = a - mean, b - mean
        var = (jnp.sum(a * a, -1, keepdims=True) + jnp.sum(b * b, -1, keepdims=True)) / n
        inv = lax.rsqrt(var + EPS)
        a, b = a * inv, b * inv
        ua, ub = ups[0], ups[1]
        sums[0:1, :] = jnp.sum(ua * a, axis=0, keepdims=True)
        sums[1:2, :] = jnp.sum(ub * b, axis=0, keepdims=True)
        sums[2:3, :] = jnp.sum(ua, axis=0, keepdims=True)
        sums[3:4, :] = jnp.sum(ub, axis=0, keepdims=True)
        ua, ub = ua * gain[0:1, :], ub * gain[1:2, :]
        m1 = (jnp.sum(ua, -1, keepdims=True) + jnp.sum(ub, -1, keepdims=True)) / n
        m2 = (jnp.sum(ua * a, -1, keepdims=True) + jnp.sum(ub * b, -1, keepdims=True)) / n
        d_lat[...] = inv * (ua - m1 - a * m2)
        d_skp[...] = inv * (ub - m1 - b * m2)


def norm0_grad(g, w, lat, skp, gain):
    t, d = lat.shape
    big = fixed(t, d)
    return call(
        norm0_grad_body,
        grid=(2,),
        in_specs=[big, pl.BlockSpec((1,) + w.shape[1:], lambda s: (s, 0, 0)), big, big, fixed(2, d)],
        out_specs=[big, big, fixed(4, d)],
        out_shape=[shaped((t, d), F32), shaped((t, d), F32), shaped((4, d), F32)],
        scratch_shapes=[pltpu.VMEM((2, t, d), F32)],
    )(g, w, lat, skp, gain)


def mm_body(dims, act, w, o):
    o[...] = dotf(act[...], w[0], dims).astype(o.dtype)


def mm_nn(act, w, first):
    t, k = act.shape
    out = w.shape[2]
    return call(
        functools.partial(mm_body, NN),
        grid=(1,),
        in_specs=[fixed(t, k), pl.BlockSpec((1, k, out), lambda s: (first, 0, 0))],
        out_specs=fixed(t, out),
        out_shape=shaped((t, out), BF),
    )(act, w)


def mm_nt_body(g, w, o):
    part = dotf(g[0], w[0], NT)

    @pl.when(pl.program_id(0) == 0)
    def _():
        o[...] = part

    @pl.when(pl.program_id(0) > 0)
    def _():
        o[...] += part


def mm_nt(g, w):
    n, t, k = g.shape
    out = w.shape[1]
    return call(
        mm_nt_body,
        grid=(n,),
        in_specs=[
            pl.BlockSpec((1, t, k), lambda s: (s, 0, 0)),
            pl.BlockSpec((1, out, k), lambda s: (s, 0, 0)),
        ],
        out_specs=fixed(t, out),
        out_shape=shaped((t, out), F32),
    )(g, w)


def ff_up_body(act, w, b, post, slope):
    v = dotf(act[...], w[0], NN) + b[...]
    inner = jnp.tanh(GELU_C * (v + 0.044715 * v * v * v))
    half = 0.5 * (1.0 + inner)
    post[...] = (v * half).astype(BF)
    slope[...] = (
        half + 0.5 * v * (1.0 - inner * inner) * (GELU_C * (1.0 + 0.134145 * v * v))
    ).astype(BF)


def ff_tile(width):
    return 768 if width % 768 == 0 else width


def ff_up(act, w, bias):
    t, k = act.shape
    width = w.shape[2]
    tile = ff_tile(width)
    col = pl.BlockSpec((t, tile), lambda j: (0, j))
    return call(
        ff_up_body,
        grid=(width // tile,),
        in_specs=[
            fixed(t, k),
            pl.BlockSpec((1, k, tile), lambda j: (0, 0, j)),
            pl.BlockSpec((1, tile), lambda j: (0, j)),
        ],
        out_specs=[col, col],
        out_shape=[shaped((t, width), BF)] * 2,
    )(act, w, bias)


def ff_up_grad_body(gm, w, slope, g, total):
    low = (dotf(gm[...], w[0], NN) * slope[...].astype(F32)).astype(BF)
    g[...] = low
    total[...] = jnp.sum(low.astype(F32), axis=0, keepdims=True)


def ff_up_grad(gm, w, slope):
    t, k = gm.shape
    width = w.shape[2]
    tile = ff_tile(width)
    col = pl.BlockSpec((t, tile), lambda j: (0, j))
    return call(
        ff_up_grad_body,
        grid=(width // tile,),
        in_specs=[fixed(t, k), pl.BlockSpec((1, k, tile), lambda j: (0, 0, j)), col],
        out_specs=[col, pl.BlockSpec((1, tile), lambda j: (0, j))],
        out_shape=[shaped((t, width), BF), shaped((1, width), F32)],
    )(gm, w, slope)


def ff_down_body(h, w, o, acc):
    part = dotf(h[...], w[0], NT)
    step = pl.program_id(0)

    @pl.when(step == 0)
    def _():
        acc[...] = part

    @pl.when(step > 0)
    def _():
        acc[...] += part

    @pl.when(step == pl.num_programs(0) - 1)
    def _():
        o[...] = acc[...].astype(o.dtype)


def ff_down(h, w, dtype):
    t, width = h.shape
    k = w.shape[1]
    tile = ff_tile(width)
    return call(
        ff_down_body,
        grid=(width // tile,),
        in_specs=[
            pl.BlockSpec((t, tile), lambda j: (0, j)),
            pl.BlockSpec((1, k, tile), lambda j: (0, 0, j)),
        ],
        out_specs=fixed(t, k),
        out_shape=shaped((t, k), dtype),
        scratch_shapes=[pltpu.VMEM((t, k), F32)],
    )(h, w)


def core_half(ids, a):
    half = a.shape[1] // 2
    return jnp.where(ids[2] == 0, a[:, :half].astype(F32), a[:, half:].astype(F32)).astype(BF)


def split_rows(ids, acc, far):
    quarter = acc.shape[0] // 4
    at = pl.multiple_of((ids[1] ^ far) * quarter, 8)
    return jnp.concatenate(
        [acc[pl.ds(at, quarter), :], acc[pl.ds(2 * quarter + at, quarter), :]], axis=0
    )


def wgrad_body(jobs, n_in, ids, *refs):
    ins = refs[:n_in]
    outs = refs[n_in:-1]
    acc = refs[-1]
    cache = {}
    for pairs, places in jobs:
        total = None
        for a, (g, slab) in pairs:
            if a not in cache:
                cache[a] = core_half(ids, ins[a][...])
            grad = ins[g][...] if slab is None else ins[g][slab]
            part = dotf(cache[a], grad, TN)
            total = part if total is None else total + part
        acc[...] = total
        half = total.shape[1] // 2
        for far in (0, 1):
            rows = split_rows(ids, acc, far)
            for oth in (0, 1):
                out, at = places[2 * oth + far]
                outs[out][at] = rows[:, oth * half : (oth + 1) * half].astype(BF)


def wgrad(ids, arrays, jobs, out_shapes):
    a0 = arrays[0]
    g = arrays[jobs[0][0][0][1][0]]
    return call(
        functools.partial(wgrad_body, jobs, len(arrays)),
        in_specs=[scalars()] + [pl.BlockSpec(memory_space=pltpu.VMEM)] * len(arrays),
        out_shape=[shaped(s, BF) for s in out_shapes],
        scratch_shapes=[pltpu.VMEM((a0.shape[1] // 2, g.shape[-1]), F32)],
    )(ids, *arrays)


def ff_wgrad_body(n, ids, *refs):
    acts, gs = refs[:n], refs[n : 2 * n]
    near, far, turned, acc = refs[2 * n :]

    @pl.when(pl.program_id(0) == 0)
    def _():
        for k in range(n):
            t = acts[k].shape[0]
            turned[:, k * t : (k + 1) * t] = core_half(ids, acts[k][...]).T

    total = None
    for k in range(n):
        t = acts[k].shape[0]
        part = dotf(turned[:, k * t : (k + 1) * t], gs[k][...], NN)
        total = part if total is None else total + part
    acc[...] = total
    near[...] = split_rows(ids, acc, 0).astype(BF)
    far[...] = split_rows(ids, acc, 1).astype(BF)


def ff_wgrad(ids, acts, gs):
    n = len(acts)
    t, k = acts[0].shape
    width = gs[0].shape[1]
    tile = ff_tile(width)
    col = pl.BlockSpec((k // 4, tile), lambda j: (0, j))
    return call(
        functools.partial(ff_wgrad_body, n),
        grid=(width // tile,),
        in_specs=[scalars()]
        + [fixed(t, k)] * n
        + [pl.BlockSpec((t, tile), lambda j: (0, j))] * n,
        out_specs=[col, col],
        out_shape=[shaped((k // 4, width), BF)] * 2,
        scratch_shapes=[pltpu.VMEM((k // 2, n * t), BF), pltpu.VMEM((k // 2, tile), F32)],
    )(ids, *acts, *gs)


def two_dots(v, onehot):
    high = v.astype(BF)
    low = (v - high.astype(F32)).astype(BF)
    return dotf(high, onehot, NN) + dotf(low, onehot, NN)


def head_unit(v, s_in, s_out):
    centered = v - two_dots(two_dots(v, s_in) * (1.0 / HD), s_out)
    inv = lax.rsqrt(two_dots(centered * centered, s_in) * (1.0 / HD) + EPS)
    return centered * two_dots(inv, s_out), inv


def swap_pairs(v):
    even = lax.broadcasted_iota(jnp.int32, v.shape, 1) % 2 == 0
    return jnp.where(even, pltpu.roll(v, v.shape[1] - 1, 1), pltpu.roll(v, 1, 1))


def head_spreads(width):
    lanes = jnp.arange(width) // HD
    into = (lanes[:, None] == jnp.arange(LANES)[None, :]).astype(BF)
    return into, into.T


def mm_heads_body(kinds, act, w, bias, gain, beta, cos, sin, s_in, s_out, *refs):
    units, invs = refs[:2]
    for k, kind in enumerate(kinds):

        @pl.when(pl.program_id(0) == k)
        def _(k=k, kind=kind):
            v = dotf(act[...], w[0], NN) + bias[0]
            if kind != CAST:
                unit, inv = head_unit(v, s_in[...], s_out[...])
                units[0] = unit
                invs[0] = inv
                v = unit * gain[k : k + 1, :] + beta[k : k + 1, :]
                if kind == ROPE:
                    v = v * cos[...] + swap_pairs(v) * sin[...]
            if k == 0:
                refs[2][...] = v.astype(BF)
            else:
                refs[3][0] = v.astype(BF)


def mm_heads(act, w, first, kinds, bias, gains, betas, tabs, spreads):
    n = len(kinds)
    t, k = act.shape
    out = w.shape[2]
    normed = sum(kind != CAST for kind in kinds)
    slab = pl.BlockSpec((1, t, out), lambda s: (jnp.minimum(s, normed - 1), 0, 0))
    few = pl.BlockSpec((1, t, LANES), lambda s: (jnp.minimum(s, normed - 1), 0, 0))
    rest = pl.BlockSpec((1, t, out), lambda s: (jnp.maximum(s - 1, 0), 0, 0))
    return call(
        functools.partial(mm_heads_body, kinds),
        grid=(n,),
        in_specs=[
            fixed(t, k),
            pl.BlockSpec((1, k, out), lambda s: (first + s, 0, 0)),
            pl.BlockSpec((1, 1, out), lambda s: (s, 0, 0)),
            fixed(n, out),
            fixed(n, out),
        ]
        + [fixed(*a.shape) for a in tabs + spreads],
        out_specs=[slab, few, fixed(t, out)] + [rest] * (n > 1),
        out_shape=[
            shaped((normed, t, out), F32),
            shaped((normed, t, LANES), F32),
            shaped((t, out), BF),
        ]
        + [shaped((n - 1, t, out), BF)] * (n > 1),
    )(act, w, bias[:, None], gains, betas, *tabs, *spreads)


def heads_grad_body(kinds, plan, n_up, units, invs, *refs):
    ups = refs[:n_up]
    gain, cos, sin, s_in, s_out, out, sums = refs[n_up:]

    @pl.when(pl.program_id(0) == 0)
    def _():
        sums[...] = jnp.zeros_like(sums)

    for k, kind in enumerate(kinds):
        up = None
        for ref, slab in plan[k]:
            piece = (ups[ref][...] if slab is None else ups[ref][slab]).astype(F32)
            up = piece if up is None else up + piece
        if kind != CAST:
            if kind == ROPE:
                up = up * cos[...] - swap_pairs(up) * sin[...]
            unit = units[k]
            inv = two_dots(invs[k], s_out[...])
            scaled = up * gain[k : k + 1, :]
            m1 = two_dots(two_dots(scaled, s_in[...]) * (1.0 / HD), s_out[...])
            m2 = two_dots(two_dots(scaled * unit, s_in[...]) * (1.0 / HD), s_out[...])
            sums[0, k : k + 1, :] += jnp.sum(up * unit, axis=0, keepdims=True)
            sums[1, k : k + 1, :] += jnp.sum(up, axis=0, keepdims=True)
            up = inv * (scaled - m1 - unit * m2)
        low = up.astype(BF)
        out[k] = low
        sums[2, k : k + 1, :] += jnp.sum(low.astype(F32), axis=0, keepdims=True)


def heads_grad(norms, kinds, plan, ups, gains, tabs, spreads, rows):
    n = len(kinds)
    _, t, w = norms[0].shape

    def block(a):
        if a.ndim == 2:
            return pl.BlockSpec((rows, a.shape[1]), lambda i: (i, 0))
        return pl.BlockSpec((a.shape[0], rows, a.shape[2]), lambda i: (0, i, 0))

    tab_specs = [block(a) if a.shape[0] == t else fixed(*a.shape) for a in tabs]
    return call(
        functools.partial(heads_grad_body, kinds, plan, len(ups)),
        grid=(t // rows,),
        in_specs=[block(a) for a in norms]
        + [block(u) for u in ups]
        + [fixed(n, w)]
        + tab_specs
        + [fixed(*a.shape) for a in spreads],
        out_specs=[pl.BlockSpec((n, rows, w), lambda i: (0, i, 0)), fixed(3, n, w)],
        out_shape=[shaped((n, t, w), BF), shaped((3, n, w), F32)],
    )(*norms, *ups, gains, *tabs, *spreads)


def att_forward_body(nb, used, *refs):
    q_ref = refs[0]
    kvs = refs[1 : 1 + nb]
    o_ref, lse_ref = refs[1 + nb :]
    scale = HD**-0.5
    for h in range(q_ref.shape[1] // HD):
        s = slice(h * HD, (h + 1) * HD)
        q = q_ref[:, s]
        scores = [dotf(kv[0, :used, s], q, NT) for kv in kvs]
        peak = functools.reduce(
            jnp.maximum, [jnp.max(x, axis=0, keepdims=True) for x in scores]
        )
        expo = [jnp.exp((x - peak) * scale) for x in scores]
        total = sum(jnp.sum(e, axis=0, keepdims=True) for e in expo)
        recip = 1.0 / total
        out = sum(dotf(kv[1, :used, s], (e * recip).astype(BF), TN) for kv, e in zip(kvs, expo))
        o_ref[0, :, s] = out.T.astype(BF)
        lse_ref[h : h + 1, :] = peak * scale + jnp.log(total)


def att_forward(q, kvs, used):
    t, w = q.shape
    return call(
        functools.partial(att_forward_body, len(kvs), used),
        out_shape=[shaped((1, t, w), BF), shaped((w // HD, t), F32)],
    )(q, *kvs)


def att_backward_body(nb, used, *refs):
    q_ref, do_ref, lse_ref = refs[:3]
    kvs = refs[3 : 3 + nb]
    dq_ref = refs[3 + nb]
    dkvs = refs[4 + nb :]
    scale = HD**-0.5
    for kv, dkv in zip(kvs, dkvs):
        if used < kv.shape[1]:
            dkv[...] = jnp.zeros_like(dkv)
    for h in range(q_ref.shape[1] // HD):
        s = slice(h * HD, (h + 1) * HD)
        q = q_ref[:, s]
        do = do_ref[:, s]
        lse = lse_ref[h : h + 1, :]
        probs = [jnp.exp(dotf(kv[0, :used, s], q, NT) * scale - lse) for kv in kvs]
        dps = [dotf(kv[1, :used, s], do, NT) for kv in kvs]
        delta = sum(jnp.sum(p * d, axis=0, keepdims=True) for p, d in zip(probs, dps))
        dq = None
        for i in range(nb):
            ds = (probs[i] * (dps[i] - delta)).astype(BF)
            part = dotf(kvs[i][0, :used, s], ds, TN)
            dq = part if dq is None else dq + part
            dkvs[i][0, :used, s] = (dotf(ds, q, NN) * scale).astype(dkvs[i].dtype)
            dkvs[i][1, :used, s] = dotf(probs[i].astype(BF), do, NN).astype(dkvs[i].dtype)
        dq_ref[:, s] = (dq * scale).T


def att_backward(q, do, lse, kvs, kinds, used):
    t, w = q.shape
    nb = len(kvs)
    return call(
        functools.partial(att_backward_body, nb, used),
        out_shape=[shaped((t, w), F32)] + [shaped(kv.shape, d) for kv, d in zip(kvs, kinds)],
    )(q, do, lse, *kvs)


def one_image_per_chip(
    latents,
    skip_states,
    text_states,
    time_vector,
    grid_pos,
    out_grad,
    norm0_gain,
    norm0_beta,
    skip_weight,
    skip_bias,
    mod_weight,
    mod_bias,
    norm1_gain,
    norm1_beta,
    qkv_weight,
    qkv_bias,
    qnorm_gain,
    qnorm_beta,
    knorm_gain,
    knorm_beta,
    proj_weight,
    proj_bias,
    norm3_gain,
    norm3_beta,
    cross_q_weight,
    cross_q_bias,
    cross_kv_weight,
    cross_kv_bias,
    cqnorm_gain,
    cqnorm_beta,
    cknorm_gain,
    cross_proj_weight,
    cross_proj_bias,
    norm2_gain,
    norm2_beta,
    fc1_weight,
    fc1_bias,
    fc2_weight,
    fc2_bias,
):
    z, y = lax.axis_index("z"), lax.axis_index("y")
    core, rank = lax.axis_index(CORE), lax.axis_index(RANK)
    ids = jnp.stack([z, y, core, rank]).astype(jnp.int32)
    part = latents.shape[1]
    width = qkv_weight.shape[2]
    heads = 2 * width // HD
    block, text_block = D // 16, DT // 16
    order = Order()
    gate, mark, pin = order.gate, order.mark, order.pin

    def mine(a, axis=0):
        return lax.dynamic_index_in_dim(a, rank, axis, keepdims=False)

    def other(a, axis=0):
        return lax.dynamic_index_in_dim(a, 1 - rank, axis, keepdims=False)

    def by_rank(own, oth, axis=0):
        first = rank == 0
        return jnp.stack([jnp.where(first, own, oth), jnp.where(first, oth, own)], axis=axis)

    def natural(a):
        half = a.shape[-1] // 2
        return jnp.where(rank == 0, a, jnp.concatenate([a[..., half:], a[..., :half]], axis=-1))

    def stage(value):
        return mark(gate(value))

    def to_x(value):
        return over_x(stage(value))

    def to_y(value):
        return over_y(stage(value))

    def to_core(value):
        return over_core(stage(value))

    def to_z(value, k):
        return over_z(stage(value), k)

    def from_z(value):
        return swap_z(stage(copies(value, 4)))

    def trade_zy(value):
        return swap_zy(stage(value))

    time_all = trade_zy(copies(time_vector, 8))
    bias_pack = jnp.concatenate([qkv_bias, cross_q_bias[None], cross_kv_bias])
    bias_in = to_x(bias_pack)
    states_in = to_x(jnp.stack([other(latents), other(skip_states)]))
    time_all = pin(time_all)
    skip_z = from_z(gate(skip_weight))
    silu_all = jax.nn.silu(time_all.reshape(-1, D)).astype(BF)
    mod_rows = mod_weight.shape[0]
    image = (z * 2 + y) * 2 + rank
    silu_rows = lax.dynamic_slice_in_dim(
        silu_all, ((z * 2 + y) * 2 + core) * mod_rows, mod_rows, 1
    )
    mod_part = mark(dotf(silu_rows, mod_weight, NN))

    pos_own = mine(grid_pos)
    pos = jnp.concatenate(
        [
            lax.dynamic_slice_in_dim(pos_own, rank * part, part, 0),
            lax.dynamic_slice_in_dim(pos_own, (1 - rank) * part, part, 0),
        ]
    )
    angles = rope_angles(pos)
    cos_row = jnp.repeat(jnp.cos(angles), 2, axis=-1)
    sin_half = jnp.sin(angles)
    sin_row = jnp.stack([-sin_half, sin_half], axis=-1).reshape(cos_row.shape)
    tabs = [jnp.tile(cos_row, (1, heads)), jnp.tile(sin_row, (1, heads))]
    no_tabs = [jnp.zeros((8, LANES), F32)] * 2
    spreads = list(head_spreads(2 * width))

    def per_head(*rows):
        return jnp.stack([jnp.tile(r, heads) for r in rows])

    qk_gain = per_head(qnorm_gain, knorm_gain, knorm_gain)
    qk_beta = per_head(qnorm_beta, knorm_beta, knorm_beta)
    cq_gain, cq_beta = per_head(cqnorm_gain), per_head(cqnorm_beta)
    ck_gain = per_head(cknorm_gain, cknorm_gain)
    biases = jnp.concatenate([bias_pack, bias_in], axis=-1)
    text_used = text_states.shape[1]
    text_fill = -text_used % 16
    text = jnp.pad(mine(text_states), ((0, text_fill), (0, 0)))

    tabs, qk_gain, qk_beta, cq_gain, cq_beta, ck_gain, biases, text = pin(
        (tabs, qk_gain, qk_beta, cq_gain, cq_beta, ck_gain, biases, text)
    )
    pieces = pin(
        (
            jnp.swapaxes(qkv_weight, 0, 1),
            jnp.stack([proj_weight.T, cross_q_weight, cross_proj_weight.T]),
            jnp.swapaxes(cross_kv_weight, 0, 1),
            fc2_weight.T[None],
            out_grad.astype(BF),
        )
    )
    qkv_piece, mix_piece, text_piece, fc2_piece, out_low = pieces
    skip_z, states_in = pin((skip_z, states_in))
    skip_x, skip_zc = to_x(skip_z), to_core(skip_z)
    mod_z = pin(trade_zy(gate(mod_part).reshape(8, 2, D)))
    skip_y, qkv_z = to_y(gate(skip_z)), from_z(gate(qkv_piece))
    mod_sum = jnp.sum(mod_z, axis=0)
    mod_c = to_core(mod_sum)
    lat = jnp.concatenate([mine(latents), states_in[0]])
    skp = jnp.concatenate([mine(skip_states), states_in[1]])
    act0 = mark(norm0(lat, skp, norm0_gain, norm0_beta, 128))
    skip_y, skip_x, skip_zc, mod_c = pin((skip_y, skip_x, skip_zc, mod_c))
    skip_xy, skip_yc, skip_xc = to_x(skip_y), to_core(skip_y), to_core(skip_x)
    skip_yc, skip_xc, qkv_z = pin((skip_yc, skip_xc, qkv_z))
    qkv_y, qkv_x, mix_z = to_y(qkv_z), to_x(qkv_z), from_z(gate(mix_piece))
    skip_xy = pin(skip_xy)
    skip_xyc = pin(to_core(skip_xy))
    shift = mine(mod_sum + mod_c) + mod_bias
    skip_full = mark(
        assemble(ids, [[skip_z, skip_zc, skip_y, skip_yc], [skip_x, skip_xc, skip_xy, skip_xyc]])
    )
    hidden1, act1 = mark(
        mm_norm(
            ids, act0, skip_full, 0, NN, True, skip_bias, norm1_gain, norm1_beta + shift, None
        )
    )
    qkv_y, qkv_x = pin((qkv_y, qkv_x))
    qkv_zc, qkv_yc, qkv_xc = to_core(gate(qkv_z)), to_core(qkv_y), to_core(qkv_x)
    qkv_xy = to_y(qkv_x)
    mix_z, qkv_zc, qkv_yc, qkv_xc = pin((mix_z, qkv_zc, qkv_yc, qkv_xc))
    mix_x, text_z = to_x(mix_z), from_z(gate(text_piece))
    qkv_xy = pin(qkv_xy)
    text_z = pin(text_z)
    fc1_z = from_z(gate(fc1_weight[None]))
    qkv_xyc, mix_y = to_core(gate(qkv_xy)), to_y(gate(mix_z))
    qkv_xyc = pin(qkv_xyc)
    mix_zc = to_core(gate(mix_z))
    qkv_full = mark(
        assemble(ids, [[qkv_z, qkv_zc, qkv_y, qkv_yc], [qkv_x, qkv_xc, qkv_xy, qkv_xyc]])
    )

    qkv_kinds = (ROPE, ROPE, CAST)
    *qkv_norms, q_low, kv_low = mark(
        mm_heads(gate(act1), qkv_full, 0, qkv_kinds, biases[:3], qk_gain, qk_beta, tabs, spreads)
    )
    mix_x, mix_y, mix_zc, fc1_z = pin((mix_x, mix_y, mix_zc, fc1_z))
    kv_in, mix_xy, text_y = to_core(gate(kv_low)), to_x(mix_y), to_y(gate(text_z))
    fc2_z = from_z(gate(fc2_piece))
    kv_in = pin(kv_in)
    mix_xc, mix_yc = to_core(gate(mix_x)), to_core(gate(mix_y))
    att, lse = mark(att_forward(gate(q_low), [kv_low, kv_in], kv_low.shape[1]))
    text_y, mix_xc, mix_yc, mix_xy = pin((text_y, mix_xc, mix_yc, mix_xy))
    fc1_y, text_x = to_y(gate(fc1_z)), to_x(gate(text_z))
    mix_xyc, text_zc, text_yc = to_core(mix_xy), to_core(gate(text_z)), to_core(text_y)
    mix_xyc, text_zc, text_yc = pin((mix_xyc, text_zc, text_yc))
    mix_full = mark(
        assemble(ids, [[mix_z, mix_zc, mix_y, mix_yc], [mix_x, mix_xc, mix_xy, mix_xyc]])
    )
    hidden2, act3 = mark(
        mm_norm(
            ids, gate(att), mix_full, 0, NT, False, proj_bias, norm3_gain, norm3_beta, hidden1
        )
    )
    text_x = pin(text_x)
    text_xy, text_xc = to_x(gate(text_y)), to_core(text_x)
    fc1_zc = to_core(gate(fc1_z))

    t_kinds = (NORM, CAST)
    *cq_norms, cq = mark(
        mm_heads(
            gate(act3), mix_full, 1, (ROPE,), biases[3:4], cq_gain, cq_beta, tabs, spreads
        )
    )
    text_xy, text_xc, fc1_zc, fc2_z, fc1_y = pin((text_xy, text_xc, fc1_zc, fc2_z, fc1_y))
    fc2_y, out_in, text_xyc = to_y(fc2_z), to_x(gate(out_low)), to_core(text_xy)
    fc1_yc, fc2_zc = to_core(fc1_y), to_core(fc2_z)
    text_xyc, fc1_yc, fc2_zc = pin((text_xyc, fc1_yc, fc2_zc))
    text_full = mark(
        assemble(
            ids, [[gate(text_z), text_zc, text_y, text_yc], [text_x, text_xc, text_xy, text_xyc]]
        )
    )
    *t_norms, tk, tv = mark(
        mm_heads(
            text, text_full, 0, t_kinds, biases[4:], ck_gain, jnp.zeros_like(ck_gain), no_tabs, spreads
        )
    )
    act1_cp, act0_cp, att_cp = to_core(gate(act1)), to_core(gate(act0)), to_core(gate(att[0]))
    tkv = jnp.concatenate([tk[None], tv])
    fc1_full = mark(assemble(ids, [[gate(fc1_z), fc1_zc, fc1_y, fc1_yc]]))
    catt, clse = mark(att_forward(gate(cq), [tkv], text_used))
    hidden3, act2 = mark(
        mm_norm(
            ids, gate(catt), mix_full, 2, NT, False, cross_proj_bias, norm2_gain, norm2_beta, hidden2
        )
    )

    act1_cp, act0_cp, att_cp, out_in, fc2_y = pin((act1_cp, act0_cp, att_cp, out_in, fc2_y))
    act2_in, act2_cp, fc2_yc = to_x(act2), to_core(gate(act2)), to_core(fc2_y)
    act3_cp = to_core(gate(act3))
    gm_own = jnp.concatenate([mine(out_low), mine(out_in)])
    gm_oth = jnp.concatenate([other(out_in), other(out_low)])
    fc2_bias_grad = bias_total(gm_own)
    post_own, slope_own = mark(ff_up(gate(act2), fc1_full, fc1_bias[None]))
    act2_cp, act3_cp, fc2_yc = pin((act2_cp, act3_cp, fc2_yc))
    post_own_cp, gm_own_cp, gm_oth_cp, catt_cp = (
        to_core(gate(v)) for v in (post_own, gm_own, gm_oth, catt[0])
    )
    fc2_full = mark(assemble(ids, [[gate(fc2_z), fc2_zc, fc2_y, fc2_yc]]))
    down_own = mark(ff_down(gate(post_own), fc2_full, F32))
    post_own_cp, gm_own_cp, gm_oth_cp, catt_cp, act2_in = pin(
        (post_own_cp, gm_own_cp, gm_oth_cp, catt_cp, act2_in)
    )
    act2_in_cp = to_core(act2_in)
    post_oth, slope_oth = mark(ff_up(act2_in, fc1_full, fc1_bias[None]))
    post_oth_cp = to_core(gate(post_oth))

    both = ("z", CORE)
    far_pair = [
        (2 * zz + cc, 2 * (zz ^ 2) + cc) for zz in range(4) for cc in range(2) if zz // 2 != cc
    ]
    in_pair = [
        (2 * zz + cc, 2 * (zz ^ 1) + cc) for zz in range(4) for cc in range(2) if zz // 2 == cc
    ]
    hand = [(2 * zz + zz // 2, 2 * zz + 1 - zz // 2) for zz in range(4)]

    def z_first(total):
        total = total.astype(BF)
        return total, lax.ppermute(stage(total), both, far_pair)

    def z_second(held, r):
        total, got = held
        n, _, w = total.shape
        blocks = (total.astype(F32) + got.astype(F32)).astype(BF).reshape(n, 2, 2 * r, w)
        same = lax.dynamic_index_in_dim(blocks, z & 1, 1, False)
        flip = lax.dynamic_index_in_dim(blocks, 1 - (z & 1), 1, False)
        return same, lax.ppermute(stage(flip), both, in_pair)

    def z_third(held, r):
        same, got = held
        n, _, w = same.shape
        done = (same.astype(F32) + got.astype(F32)).reshape(n, 2, r, w)
        keep = lax.dynamic_index_in_dim(done, core, 1, False)
        give = lax.dynamic_index_in_dim(done, 1 - core, 1, False).astype(BF)
        return keep, lax.ppermute(stage(give), both, hand)

    def land(held):
        return jnp.where(z // 2 == core, held[0], held[1].astype(F32))

    g_pre_oth, fc1_sum_oth = mark(ff_up_grad(gate(gm_oth), fc2_full, slope_oth))
    g_oth_cp = to_core(g_pre_oth)
    up_oth = mark(ff_down(gate(g_pre_oth), fc1_full, BF))
    post_oth_cp, g_oth_cp, act2_in_cp = pin((post_oth_cp, g_oth_cp, act2_in_cp))
    up_in = to_x(up_oth)
    g_pre_own, fc1_sum_own = mark(ff_up_grad(gate(gm_own), fc2_full, slope_own))
    g_own_cp = to_core(g_pre_own)
    fc2_near, fc2_far = mark(
        ff_wgrad(
            ids,
            [gm_own, gm_own_cp, gm_oth, gm_oth_cp],
            [gate(post_own), post_own_cp, post_oth, post_oth_cp],
        )
    )
    fc2_in = to_y(fc2_far)
    up_own = mark(ff_down(gate(g_pre_own), fc1_full, F32))
    fc1_bias_grad = (fc1_sum_own + fc1_sum_oth)[0]
    g_own_cp = pin(g_own_cp)
    fc1_near, fc1_far = mark(
        ff_wgrad(
            ids,
            [gate(act2), act2_cp, act2_in, act2_in_cp],
            [g_pre_own, g_own_cp, g_pre_oth, g_oth_cp],
        )
    )
    fc1_in = to_y(fc1_far)
    up_in = pin(up_in)
    out_full = jnp.concatenate([mine(out_grad), mine(out_in).astype(F32)])
    grad3, gc, sums2 = mark(norm_grad(gate(up_own), up_in, hidden3, out_full, norm2_gain))
    gc_cp = to_core(gc)
    dc = mark(mm_nn(gate(gc), mix_full, 2))

    gc_cp, fc2_in = pin((gc_cp, fc2_in))
    fc2_held = z_first((fc2_near.astype(F32) + fc2_in.astype(F32))[None])
    mark(fc2_held[0])
    dcq, dtkv = mark(att_backward(cq, gate(dc), clse, [tkv], [BF], text_used))
    dtkv_in = to_core(dtkv)
    cproj_keep, cproj_send = mark(
        wgrad(
            ids,
            [gate(gc), gc_cp, catt, catt_cp],
            ((((0, (2, 0)), (1, (3, None))), ((0, 0), (0, 1), (1, 0), (1, 1))),),
            [(2, D // 4, width)] * 2,
        )
    )
    cproj_in = to_x(cproj_send)
    g_cq, cq_sums = mark(
        heads_grad(
            cq_norms, (ROPE,), (((0, None),),), [gate(dcq)], cq_gain, tabs, spreads, 128
        )
    )
    g_cq_cp = to_core(g_cq)
    grad2, ga, sums3 = mark(
        mm_norm_grad(ids, gate(g_cq), mix_full, 1, hidden2, grad3, norm3_gain, False)
    )
    ga_cp = to_core(gate(ga))
    dtkv_in, g_cq_cp, fc2_held, fc1_in = pin((dtkv_in, g_cq_cp, fc2_held, fc1_in))
    fc2_held = z_second(fc2_held, block)
    mark(fc2_held[0])
    fc1_held = z_first((fc1_near.astype(F32) + fc1_in.astype(F32))[None])
    mark(fc1_held[0])
    g_text, text_sums = mark(
        heads_grad(
            t_norms,
            t_kinds,
            (((0, 0), (1, 0)), ((0, 1), (1, 1))),
            [gate(dtkv), dtkv_in],
            ck_gain,
            no_tabs,
            spreads,
            text.shape[0],
        )
    )
    text_near, text_far = mark(
        wgrad(
            ids,
            [text, gate(g_text)],
            (
                (((0, (1, 0)),), ((0, 0), (1, 0), (0, 2), (1, 2))),
                (((0, (1, 1)),), ((0, 1), (1, 1), (0, 3), (1, 3))),
            ),
            [(4, DT // 4, width)] * 2,
        )
    )
    text_in_y = to_y(text_far.reshape(16, text_block, width))
    text_part = mark(mm_nt(gate(g_text), text_full))[:text_used]
    fc2_held, cproj_in, ga_cp = pin((fc2_held, cproj_in, ga_cp))
    fc2_held = z_third(fc2_held, block)
    text_in = to_x(text_part.astype(BF))
    cproj_sum = cproj_keep.astype(F32) + cproj_in.astype(F32)
    cproj_in_y = to_y(cproj_sum[1:].astype(BF))

    pair_keep, pair_send = mark(
        wgrad(
            ids,
            [gate(ga), ga_cp, act3, act3_cp, att, att_cp, g_cq, g_cq_cp],
            (
                (((0, (4, 0)), (1, (5, None))), ((0, 0), (0, 2), (1, 0), (1, 2))),
                (((2, (6, 0)), (3, (7, 0))), ((0, 1), (0, 3), (1, 1), (1, 3))),
            ),
            [(4, D // 4, width)] * 2,
        )
    )
    pair_in = to_x(pair_send)
    da = mark(mm_nn(gate(ga), mix_full, 0))
    fc2_held, text_in, text_in_y, fc1_held = pin((fc2_held, text_in, text_in_y, fc1_held))
    fc1_held = z_second(fc1_held, block)
    text_total = text_near.astype(F32) + text_in_y.reshape(text_near.shape).astype(F32)
    text_in_x = to_x(text_total[2:].astype(BF).reshape(8, text_block, width))
    dq, dkv, dkv_give = mark(
        att_backward(q_low, gate(da), lse, [kv_low, kv_in], [F32, BF], kv_low.shape[1])
    )
    pair_in, fc1_held = pin((pair_in, fc1_held))
    dkv_in = to_core(gate(dkv_give))
    fc1_held = z_third(fc1_held, block)

    down_oth = mark(ff_down(gate(post_oth), fc2_full, F32))
    down_own = down_own + hidden3 + fc2_bias
    down_send = mark(jnp.stack([down_own[part:], down_oth[:part]]).astype(BF))
    dkv_in, cproj_in_y = pin((dkv_in, cproj_in_y))
    pair_total = pair_keep.astype(F32) + pair_in.astype(F32)
    pair_in_y, down_in = to_y(pair_total[2:].astype(BF)), to_x(down_send)
    cproj_held = z_first(cproj_sum[:1] + cproj_in_y.astype(F32))
    g_qkv, qkv_sums = mark(
        heads_grad(
            qkv_norms,
            qkv_kinds,
            (((0, None),), ((1, 0), (2, 0)), ((1, 1), (2, 1))),
            [gate(dq), dkv, dkv_in],
            qk_gain,
            tabs,
            spreads,
            128,
        )
    )
    text_in_x, cproj_held, fc1_held = pin((text_in_x, cproj_held, fc1_held))
    g_qkv_cp = to_core(gate(g_qkv))
    text_held = z_first(text_total[:2] + text_in_x.reshape(2, DT // 4, width).astype(F32))
    cproj_held = z_second(cproj_held, block)
    grad1, gs, sums1, gs_turned = mark(
        mm_norm_grad(ids, gate(g_qkv), qkv_full, 0, hidden1, grad2, norm1_gain, True)
    )
    g_qkv_cp, pair_in_y, text_held, cproj_held = pin(
        (g_qkv_cp, pair_in_y, text_held, cproj_held)
    )
    gs_cp = to_core(gate(gs_turned))

    def one(k, places):
        return (((0, (2, k)), (1, (3, k))), places)

    q_near, q_far, k_near, k_far = mark(
        wgrad(
            ids,
            [gate(act1), act1_cp, g_qkv, g_qkv_cp],
            (
                one(0, ((0, 0), (1, 0), (0, 1), (1, 1))),
                one(1, ((2, 0), (3, 0), (2, 1), (3, 1))),
            ),
            [(2, D // 4, width)] * 4,
        )
    )
    q_in = to_y(q_far)
    text_held, cproj_held = z_second(gate(text_held), text_block), z_third(gate(cproj_held), block)
    v_keep, v_send = mark(
        wgrad(
            ids,
            [gate(act1), act1_cp, g_qkv, g_qkv_cp],
            (one(2, ((0, 0), (0, 1), (1, 0), (1, 1))),),
            [(2, D // 4, width)] * 2,
        )
    )
    v_in = to_x(v_send)
    gs_cp, text_held, cproj_held = pin((gs_cp, text_held, cproj_held))
    pair_held = z_first(gate(pair_total[:2]) + pair_in_y.astype(F32))

    def first_half(keep, got):
        total = keep.astype(F32) + got.astype(F32)
        return total[:1], total[1:].astype(BF)

    def second_half(total, got):
        return total + got.astype(F32)

    lat_keep, lat_send, skp_near, skp_far = mark(
        wgrad(
            ids,
            [gate(act0[0]), act0_cp[0], act0[1], act0_cp[1], gs_turned, gs_cp],
            (
                (((0, (4, None)), (1, (5, None))), ((0, 0), (0, 1), (1, 0), (1, 1))),
                (((2, (4, None)), (3, (5, None))), ((2, 0), (3, 0), (2, 1), (3, 1))),
            ),
            [(2, D // 4, width)] * 4,
        )
    )
    q_in, v_in, pair_held = pin((q_in, v_in, pair_held))
    k_in, lat_in = to_y(gate(k_far)), to_x(gate(lat_send))
    pair_held, text_held = z_second(pair_held, block), z_third(text_held, text_block)
    q_sum, q_give = first_half(q_near, q_in)
    v_sum, v_give = first_half(v_keep, v_in)
    d_lat, d_skp, sums0 = mark(norm0_grad(gate(gs_turned), skip_full, lat, skp, norm0_gain))
    d_send = mark(jnp.stack([d_lat[part:], d_skp[part:]]).astype(BF))

    def fold(v):
        return jnp.sum(v.reshape(-1, heads, HD), axis=(0, 1))

    share = 0.5
    small_shapes = []

    def small_sums():
        wide = jnp.concatenate([fc1_bias_grad, jnp.zeros_like(fc1_bias_grad)])
        rows = (jnp.arange(16) == image).astype(F32)
        parts = [
            natural(wide),
            fc2_bias_grad,
            sums2[0],
            sums2[1],
            sums2[2],
            sums3[0],
            sums3[1],
            natural(cq_sums[2, 0]),
            natural(text_sums[2]) * share,
            fold(cq_sums[0]),
            fold(cq_sums[1]),
            fold(text_sums[0, 0]) * share,
            sums3[2],
            sums1[0],
            sums1[1],
            sums1[2],
            natural(qkv_sums[2]),
            fold(qkv_sums[0, 0]),
            fold(qkv_sums[1, 0]),
            fold(qkv_sums[0, 1]),
            fold(qkv_sums[1, 1]),
            rows[:, None] * sums1[1][None],
            sums0[:2],
            sums0[2:],
        ]
        small_shapes.extend(p.shape for p in parts)
        flat = jnp.concatenate([p.reshape(-1) for p in parts])
        pad = -flat.shape[0] % 1024
        return jnp.concatenate([flat, jnp.zeros((pad,), F32)]).reshape(-1, LANES)

    small = mark(small_sums())
    k_in, lat_in, pair_held, text_held = pin((k_in, lat_in, pair_held, text_held))
    small_in = to_z(small, 1)
    k_sum, k_give = first_half(k_near, k_in)
    lat_sum, lat_give = first_half(lat_keep, lat_in)
    skp_in, qk_in = to_y(skp_far), to_x(jnp.concatenate([q_give, k_give]))
    small_in = pin(small_in)
    small = small + small_in
    small_in, pair_held = to_z(small, 2), z_third(pair_held, block)
    small_in, pair_held = pin((small_in, pair_held))
    small = small + small_in
    small_in = to_core(small)
    skp_in, qk_in, small_in, down_in = pin((skp_in, qk_in, small_in, down_in))
    small = small + small_in
    small_in = to_x(small)
    skp_sum, skp_give = first_half(skp_near, skp_in)
    v_in = to_y(jnp.concatenate([v_give, lat_give]))
    skp_in = to_x(skp_give)
    d_in = to_x(d_send)
    qk_held = z_first(second_half(jnp.concatenate([q_sum, k_sum]), qk_in))
    small_in, skp_in, qk_held = pin((small_in, skp_in, qk_held))
    small = small + small_in
    skp_held, qk_held = z_first(second_half(skp_sum, skp_in)), z_second(qk_held, block)
    v_in = pin(v_in)
    v_held = z_first(second_half(jnp.concatenate([v_sum, lat_sum]), v_in))
    small_in = to_y(small)
    qk_held, skp_held = pin((qk_held, skp_held))
    qk_held, skp_held = z_third(qk_held, block), z_second(skp_held, block)
    v_held, qk_held, skp_held, small_in = pin((v_held, qk_held, skp_held, small_in))
    small = small + small_in
    v_held, skp_held = z_second(v_held, block), z_third(skp_held, block)
    v_held, skp_held, d_in = pin((v_held, skp_held, d_in))
    v_held = z_third(v_held, block)
    v_lat, skip_b = land(v_held), land(skp_held)
    skip_grad = jnp.concatenate([v_lat[1:], skip_b])
    qkv_grad = jnp.swapaxes(jnp.concatenate([land(qk_held), v_lat[:1]]), 0, 1)
    fc2_grad, fc1_grad = land(fc2_held)[0].T, land(fc1_held)[0]
    cproj_grad, pair_grad = land(cproj_held), land(pair_held)
    cross_kv_grad = jnp.swapaxes(land(text_held), 0, 1)

    out_mine = (down_own[:part] + down_in[1].astype(F32)).astype(BF)
    out_other = (down_oth[part:] + down_in[0].astype(F32)).astype(BF)
    output = by_rank(out_mine, out_other)
    text_grad = by_rank(text_part, text_in.astype(F32))
    grad_latents = by_rank(d_lat[:part], d_in[0].astype(F32))
    grad_skip = by_rank(d_skp[:part], d_in[1].astype(F32))

    flat, at, sums = small.reshape(-1), 0, []
    for shape in small_shapes:
        size = functools.reduce(lambda p, q: p * q, shape)
        sums.append(flat[at : at + size].reshape(shape))
        at += size
    early, middle, late = sums[:13], sums[13:22], sums[22:]
    mod_grad = lax.dot_general(
        silu_rows.astype(F32),
        middle[8],
        ROWS_CONTRACT,
        precision=lax.Precision.HIGHEST,
        preferred_element_type=F32,
    )

    def narrow(a):
        return mine(a.reshape(a.shape[:-1] + (2, -1)), a.ndim - 1)

    return (
        output,
        grad_latents,
        grad_skip,
        text_grad,
        late[0],
        late[1],
        skip_grad,
        middle[2],
        mod_grad,
        middle[1],
        middle[0],
        middle[1],
        qkv_grad,
        narrow(middle[3]),
        middle[4],
        middle[5],
        middle[6],
        middle[7],
        pair_grad[0].T,
        early[12],
        early[5],
        early[6],
        pair_grad[1],
        narrow(early[7]),
        cross_kv_grad,
        narrow(early[8]),
        early[9],
        early[10],
        early[11],
        cproj_grad[0].T,
        early[4],
        early[2],
        early[3],
        fc1_grad,
        narrow(early[0]),
        fc2_grad,
        early[1],
    )


def is_spec(spec):
    return isinstance(spec, P)


def split_dp(spec):
    parts = []
    for entry in spec:
        names = entry if isinstance(entry, tuple) else (entry,)
        names = sum((("z", "y") if n == DP else (n,) for n in names), ())
        parts.append(names if len(names) > 1 else names[0])
    return P(*parts)


def solution(mesh):
    in_specs = (
        P(DP, (CORE, RANK), None),
        P(DP, (CORE, RANK), None),
        P(DP, None, None),
        P(DP, None),
        P(DP, CORE, None),
        P(DP, (CORE, RANK), None),
        P(),
        P(),
        P(None, (DP, CORE), RANK),
        P(),
        P((DP, CORE), None),
        P(),
        P(),
        P(),
        P((DP, CORE), None, RANK),
        P(None, RANK),
        P(),
        P(),
        P(),
        P(),
        P(RANK, (DP, CORE)),
        P(),
        P(),
        P(),
        P((DP, CORE), RANK),
        P(RANK),
        P((DP, CORE), None, RANK),
        P(None, RANK),
        P(),
        P(),
        P(),
        P(RANK, (DP, CORE)),
        P(),
        P(),
        P(),
        P((DP, CORE), RANK),
        P(RANK),
        P(RANK, (DP, CORE)),
        P(),
    )
    out_specs = (
        P(DP, (CORE, RANK), None),
        P(DP, (CORE, RANK), None),
        P(DP, (CORE, RANK), None),
        P(DP, None, None),
        P(),
        P(),
        P(None, (DP, CORE), RANK),
        P(),
        P((DP, CORE), None),
        P(),
        P(),
        P(),
        P((DP, CORE), None, RANK),
        P(None, RANK),
        P(),
        P(),
        P(),
        P(),
        P(RANK, (DP, CORE)),
        P(),
        P(),
        P(),
        P((DP, CORE), RANK),
        P(RANK),
        P((DP, CORE), None, RANK),
        P(None, RANK),
        P(),
        P(),
        P(),
        P(RANK, (DP, CORE)),
        P(),
        P(),
        P(),
        P((DP, CORE), RANK),
        P(RANK),
        P(RANK, (DP, CORE)),
        P(),
    )
    program = on_device
    sizes = dict(mesh.shape)
    if (sizes[DP], sizes[CORE], sizes[RANK]) == (8, 2, 2):
        program = one_image_per_chip
        mesh = Mesh(mesh.devices.reshape(4, 2, 2, 2), GRID_AXES)
        in_specs = jax.tree.map(split_dp, in_specs, is_leaf=is_spec)
        out_specs = jax.tree.map(split_dp, out_specs, is_leaf=is_spec)
    return jax.shard_map(
        program, mesh=mesh, in_specs=in_specs, out_specs=out_specs, check_vma=False
    )
```
